512 devices in a mesh: particle: 16 (over y_lo, z), space: 32 (over x, y_hi, core).
Axes of the slice: x: 4, y: 8 (y_hi: 4, y_lo: 2; y = y_hi * 2 + y_lo), z: 8, core: 2. Of those that a mesh axis runs over, the one named last changes fastest.
Arguments:
- stream: float32 [16, 2048, 2048], P('particle', 'space'), may hold values from -6 to 6
- depth_field: float32 [2048, 2048], P('space'), may hold values from 0.5 to 4
- obs_col: int32 [2048, 16], P('space'), may hold values from 0 to 2047
- obs_val: float32 [2048, 16], P('space'), may hold values from -6 to 6
- obs_weight: float32 [2048, 16], P('space'), may hold values from 0.1 to 1
- log_weight: float32 [16], P('particle'), may hold values from -24576 to 24576
- target: float32 [1], replicated, may hold values from 0 to 8192
- spectrum: float32 [512, 512], P('space'), may hold values from 1 to 10
- noise_coef: bfloat16 [16, 512, 512], P('particle', 'space'), may hold values from -6 to 6
- selection: int32 [2, 16], replicated, may hold values from 0 to 1
Outputs:
- analysis: float32 [16, 2048, 2048], P('particle', 'space')
- misfit_out: float32 [16], P('particle')
The draws below stay inside these ranges and needn't reach their ends.
All inputs are finite; a program needn't handle non-finite values.
Results may differ from the reference program's by a relative error of at most 0.0003.
The reference program's roundings to bfloat16 on the way (of `gradient`, `row_modes`, `shaped` and `inverted`) count: a program that leaves them out, or rounds other values in their place, can miss the bound.
Values may be sent and summed in bfloat16 or wider, within the bound.
No kernel may reach another device: no remote copies, remote signals or barrier semaphores. Data moves between devices by JAX's collectives and lax.ppermute only.
A program may use at most 64 MiB of HBM per device.

```python
import math
import jax
import jax.numpy as jnp
from jax import lax

NX = 2048
P_DEV = 1
KM = 256
OBS_ROW = 16
ITERS = 2
SECTIONS = 2
NY = 2048
PARTICLES = 16
MODES = 512


def plant(values, rng, low, high):
    spot = [jax.random.randint(jax.random.fold_in(rng, axis), (), 0, length) for axis, length in enumerate(values.shape)]
    longest = values.shape.index(max(values.shape))
    next_to = spot[:longest] + [(spot[longest] + 1) % values.shape[longest]] + spot[longest + 1:]
    return values.at[tuple(spot)].set(low).at[tuple(next_to)].set(high)


def steps_of(rng, shape, cuts, least, high):
    level, own = 1.0, jax.random.fold_in(rng, 6)
    for axis_at, blocks in cuts:
        heights = jnp.exp(jax.random.uniform(jax.random.fold_in(own, axis_at), (blocks,), jnp.float32, least / len(cuts), high / len(cuts)))
        level = level * jnp.repeat(heights, shape[axis_at] // blocks).reshape([-1 if axis == axis_at else 1 for axis in range(len(shape))])
    return level


def normal_values(key, dims, spread, bound, cuts=(), held_as=jnp.bfloat16):
    array = jax.random.normal(key, dims, jnp.float32) * spread
    if len(cuts) > 0:
        array = steps_of(key, dims, cuts, -0.22, 0.18) * array
    return jnp.clip(array, min=-bound, max=bound).astype(held_as)


def setup_inputs(seed: int = 0) -> dict:
    key_of = jax.random.split(jax.random.key(seed), 11)
    return {
        "stream": normal_values(key_of[0], (PARTICLES, NY, NX), 1.0, 6.0, ((0, 16), (1, 32)), jnp.float32),
        "depth_field": jnp.clip(jnp.exp(math.log(4.0) - 2.0794415 * jax.random.uniform(key_of[1], (NY, NX), jnp.float32) ** steps_of(key_of[1], (NY, NX), ((0, 32),), -0.2, 0.2)), 0.5, 4.0),
        "obs_col": plant(jax.random.randint(key_of[2], (NY, OBS_ROW), 0, NX), jax.random.fold_in(key_of[2], 1), 0, NX - 1).astype(jnp.int32),
        "obs_val": normal_values(key_of[3], (NY, OBS_ROW), 1.0, 6.0, ((0, 32),), jnp.float32),
        "obs_weight": jnp.clip(jnp.exp(math.log(1.0) - 2.3025851 * jax.random.uniform(key_of[4], (NY, OBS_ROW), jnp.float32) ** steps_of(key_of[4], (NY, OBS_ROW), ((0, 32),), -0.2, 0.2)), 0.1, 1.0),
        "log_weight": normal_values(key_of[5], (PARTICLES,), (OBS_ROW * NY // 8), 24576.0, ((0, 16),), jnp.float32),
        "target": jnp.clip(jax.random.uniform(key_of[6], (1,), jnp.float32, 0.0, 8192.0), 0.0, 8192.0),
        "spectrum": jnp.clip(jnp.exp(math.log(10.0) - 2.3025851 * jax.random.uniform(key_of[7], (MODES, MODES), jnp.float32) ** steps_of(key_of[7], (MODES, MODES), ((0, 32),), -0.2, 0.2)), 1.0, 10.0),
        "noise_coef": normal_values(key_of[8], (PARTICLES, MODES, MODES), 1.0, 6.0, ((0, 16), (1, 32))),
        "selection": plant(jax.random.randint(key_of[9], (SECTIONS, PARTICLES), 0, 2 * P_DEV), jax.random.fold_in(key_of[9], 1), 0, (2 * P_DEV) - 1).astype(jnp.int32),
    }


STRETCH = 0.05
RELAX_RATE = 0.8
NOISE_AMP = 0.3

def tables(extent, half_modes):
    cell_index = jnp.arange(extent, dtype=jnp.int32)[:, None]
    frequency = jnp.arange(half_modes + 1, dtype=jnp.int32)[None, :]
    angles = (cell_index * frequency % extent).astype(jnp.float32) * (2.0 * math.pi / extent)
    cosines = jnp.cos(angles).astype(jnp.bfloat16)
    sines = jnp.sin(angles[:, 1:half_modes]).astype(jnp.bfloat16)
    return jnp.concatenate([cosines, sines], axis=1)

def compare_obs(grid_field, obs_col, obs_val, obs_weight):
    index_grid = jnp.broadcast_to(obs_col, grid_field.shape[:-1] + obs_col.shape[-1:])
    seen_vals = jnp.take_along_axis(grid_field, index_grid, axis=-1)
    mismatch_vals = obs_val - seen_vals
    return (mismatch_vals, 0.5 * lax.optimization_barrier(jnp.sum(obs_weight * mismatch_vals * mismatch_vals, axis=(-2, -1))))

def spread_obs(weighted_miss, obs_col, columns):
    row_index = jnp.broadcast_to(jnp.arange(obs_col.shape[0], dtype=jnp.int32)[:, None], obs_col.shape)
    return jnp.zeros((obs_col.shape[0], columns), jnp.float32).at[row_index, obs_col].add(weighted_miss)

def operate(grid_field, screening):
    padded = jnp.pad(grid_field, ((1, 1), (0, 0)))
    return padded[2:] + padded[:-2] + jnp.roll(grid_field, 1, axis=1) + jnp.roll(grid_field, -1, axis=1) - (4.0 + screening) * grid_field

def reference(stream, depth_field, obs_col, obs_val, obs_weight, log_weight, target, spectrum, noise_coef, selection):
    x_table = tables(NX, KM)
    y_table = tables(NY, KM)
    norm_factor = 4.0 / (NX * NY)
    screening = STRETCH / depth_field

    def one_member(packed):
        grid_field, member_weight, member_noise = packed
        mismatch_vals, misfit = compare_obs(grid_field, obs_col, obs_val, obs_weight)
        gradient = spread_obs(obs_weight * mismatch_vals, obs_col, NX).astype(jnp.bfloat16)
        row_modes = jnp.dot(gradient, x_table, preferred_element_type=jnp.float32).astype(jnp.bfloat16)
        coefficients = jnp.dot(row_modes.T, y_table, preferred_element_type=jnp.float32)
        weighted = coefficients * (norm_factor * spectrum)
        energy = jnp.sum(coefficients * weighted)
        shaped = (jnp.sqrt(norm_factor * spectrum) * member_noise.astype(jnp.float32)).astype(jnp.bfloat16)
        stacked = jnp.stack([weighted.astype(jnp.bfloat16), shaped]).astype(jnp.float32)
        inverted = jnp.einsum('qkm,ym->qky', stacked, y_table.astype(jnp.float32), precision=lax.Precision.HIGHEST).astype(jnp.bfloat16)
        pulled = jnp.einsum('qky,xk->qyx', inverted.astype(jnp.float32), x_table.astype(jnp.float32), precision=lax.Precision.HIGHEST)
        step_size = (misfit + member_weight - target[0]) / (energy + 1.0)
        increment = step_size * pulled[0] + NOISE_AMP * pulled[1]
        relaxed = grid_field + increment
        pv_target = operate(grid_field, screening) + increment
        for sweep_index in range(ITERS):
            relaxed = relaxed + RELAX_RATE * (operate(relaxed, screening) - pv_target) / (4.0 + screening)
        return relaxed
    fields = lax.map(one_member, (stream, log_weight, noise_coef))
    slot_index = jnp.arange(fields.shape[0], dtype=jnp.int32)
    island = slot_index // P_DEV
    for section_bit in range(SECTIONS):
        chosen = selection[section_bit]
        partner = jnp.bitwise_xor(island, 1 << section_bit)
        source = jnp.where(chosen < P_DEV, island * P_DEV + chosen, partner * P_DEV + chosen - P_DEV)
        fields = fields[source]
    final_miss, misfit_out = compare_obs(fields, obs_col, obs_val, obs_weight)
    return (fields, misfit_out)
```

```python
import math

import jax
import jax.numpy as jnp
import ml_dtypes
import numpy as np
from jax import lax
from jax.experimental import pallas as pl
from jax.experimental.pallas import tpu as pltpu
from jax.sharding import PartitionSpec as P

STRETCH = 0.05
RELAX_RATE = 0.8
NOISE_AMP = 0.3
LANES = 128
GROUP = 4
VMEM_LIMIT = 48 * 1024 * 1024


def table(extent, half_modes):
    cell = np.arange(extent, dtype=np.int64)[:, None]
    freq = np.arange(half_modes + 1, dtype=np.int64)[None, :]
    angles = (cell * freq % extent).astype(np.float64) * (2.0 * math.pi / extent)
    return np.concatenate([np.cos(angles), np.sin(angles[:, 1:half_modes])], axis=1).astype(
        ml_dtypes.bfloat16
    )


def halo_table(y_table, bands):
    rows = y_table.shape[0]
    width = rows // bands
    out = np.zeros((bands, 2, 4, y_table.shape[1]), dtype=y_table.dtype)
    for band in range(bands):
        for at, row in enumerate((-2, -1, width, width + 1)):
            source = band * width + row
            if 0 <= source < rows:
                out[band, :, at] = y_table[source]
    return out.reshape(bands * 8, y_table.shape[1])


def pack(values):
    rows, per_row = values.shape
    return values.reshape(rows // 8, 8, per_row).transpose(1, 0, 2).reshape(8, rows // 8 * per_row)


def lane_iota():
    return lax.broadcasted_iota(jnp.int32, (8, LANES), 1)


def split3(value):
    high = value.astype(jnp.bfloat16).astype(jnp.float32)
    rest = value - high
    mid = rest.astype(jnp.bfloat16).astype(jnp.float32)
    return high, mid, rest - mid


def source_slot(sel_ref, meta_ref):
    slot = meta_ref[0]
    one = jnp.where(sel_ref[1, slot] < 1, slot, slot ^ 2)
    return jnp.where(sel_ref[0, one] < 1, one, one ^ 1)


def fill_cols(col_ref, col_scr):
    per_row, rows = col_ref.shape
    col_scr[:, 0:per_row] = col_ref[...].T


def gather_rows(field_ref, col_scr, seen_scr, per_row):
    rows, columns = field_ref.shape
    lane = lane_iota()

    def one_group(group, carry):
        at = pl.multiple_of(group * 8, 8)
        cols = col_scr[pl.ds(at, 8), :]
        high, low = cols >> 7, cols & 127
        seen = jnp.zeros((8, LANES), jnp.float32)
        for j in range(per_row):
            high_j = jnp.broadcast_to(high[:, j : j + 1], (8, LANES))
            low_j = jnp.broadcast_to(low[:, j : j + 1], (8, LANES))
            picked = field_ref[pl.ds(at, 8), 0:LANES]
            for chunk in range(1, columns // LANES):
                picked = jnp.where(
                    high_j == chunk,
                    field_ref[pl.ds(at, 8), chunk * LANES : (chunk + 1) * LANES],
                    picked,
                )
            value = jnp.sum(jnp.where(lane == low_j, picked, 0.0), axis=1, keepdims=True)
            seen = jnp.where(lane == j, value, seen)
        seen_scr[pl.ds(at, 8), :] = seen
        return carry

    lax.fori_loop(0, rows // 8, one_group, 0)


def packed(scr, per_row):
    groups = scr.shape[0] // 8
    lane = lane_iota()
    out = scr[0:8, :]
    for group in range(1, groups):
        rolled = pltpu.roll(scr[group * 8 : group * 8 + 8, :], group * per_row, axis=1)
        out = jnp.where(lane // per_row == group, rolled, out)
    return out


def observe_kernel(lw_ref, col_ref, stream_ref, out_ref, col_scr, seen_scr):
    per_row = col_ref.shape[0]
    fill_cols(col_ref, col_scr)
    gather_rows(stream_ref, col_scr, seen_scr, per_row)
    seen = packed(seen_scr, per_row)
    weight = jnp.full((8, LANES), lw_ref[0], jnp.float32)
    for peer in range(GROUP):
        out_ref[peer, 0:8, :] = seen
        out_ref[peer, 8:16, :] = weight


def gradient_kernel(
    meta_ref, sel_ref, col_ref, val_ref, wgt_ref, seen_ref, tt_ref, send_ref, miss_ref, part_ref,
    col_scr, wm_scr, grad_scr,
):
    per_row, rows = col_ref.shape
    columns = tt_ref.shape[1]
    position = source_slot(sel_ref, meta_ref) % GROUP
    fill_cols(col_ref, col_scr)
    both = seen_ref[position]
    mismatch = val_ref[...] - both[0:8]
    weighted = wgt_ref[...] * mismatch
    miss_ref[0:8, :] = mismatch
    miss_ref[8:16, :] = both[8:16]
    part_ref[...] = jnp.full((8, LANES), 0.5 * jnp.sum(weighted * mismatch), jnp.float32)
    for group in range(rows // 8):
        shift = (LANES - group * per_row) % LANES
        wm_scr[group * 8 : group * 8 + 8, :] = (
            pltpu.roll(weighted, shift, axis=1) if shift else weighted
        )
    lane = lane_iota()

    def one_group(group, carry):
        at = pl.multiple_of(group * 8, 8)
        cols = col_scr[pl.ds(at, 8), :]
        wms = wm_scr[pl.ds(at, 8), :]
        col_j = [jnp.broadcast_to(cols[:, j : j + 1], (8, LANES)) for j in range(per_row)]
        wm_j = [jnp.broadcast_to(wms[:, j : j + 1], (8, LANES)) for j in range(per_row)]
        for chunk in range(columns // LANES):
            here = lane + chunk * LANES
            total = jnp.where(col_j[0] == here, wm_j[0], 0.0)
            for j in range(1, per_row):
                total = total + jnp.where(col_j[j] == here, wm_j[j], 0.0)
            grad_scr[pl.ds(at, 8), chunk * LANES : (chunk + 1) * LANES] = total
        return carry

    lax.fori_loop(0, rows // 8, one_group, 0)
    gradient = grad_scr[...].astype(jnp.bfloat16)
    modes = lax.dot_general(
        tt_ref[...], gradient, (((1,), (1,)), ((), ())), preferred_element_type=jnp.float32
    )
    bands = send_ref.shape[0]
    split = modes.reshape(bands, 2, 8, rows)
    send_ref[...] = jnp.concatenate([split[:, 0], split[:, 1]], axis=2).astype(jnp.bfloat16)


def spectral_kernel(
    meta_ref, sel_ref, modes_ref, noise_ref, spec_ref, part_ref, tt_ref, ht_ref, send_ref,
):
    bands = modes_ref.shape[0]
    half = LANES // 2
    modes_here, n_modes = spec_ref.shape
    rows = tt_ref.shape[1]
    norm_factor = 4.0 / (rows * rows)
    position = source_slot(sel_ref, meta_ref) % GROUP
    me = meta_ref[1] % 8
    lane = lane_iota()
    low = lane < half
    tops, bottoms = [], []
    for pair in range(bands // 2):
        even = modes_ref[2 * pair].astype(jnp.float32)
        odd = modes_ref[2 * pair + 1].astype(jnp.float32)
        tops.append(jnp.where(low, even, pltpu.roll(odd, half, axis=1)))
        bottoms.append(jnp.where(low, pltpu.roll(even, half, axis=1), odd))
    columns = jnp.concatenate(
        [jnp.concatenate(tops, axis=1), jnp.concatenate(bottoms, axis=1)], axis=0
    ).astype(jnp.bfloat16)
    coefficients = lax.dot_general(
        columns, tt_ref[...], (((1,), (1,)), ((), ())), preferred_element_type=jnp.float32
    )
    scaled = norm_factor * spec_ref[...]
    weighted = coefficients * scaled
    energy = jnp.sum(coefficients * weighted)
    shaped = (jnp.sqrt(scaled) * noise_ref[position].astype(jnp.float32)).astype(jnp.bfloat16)
    weighted = weighted.astype(jnp.bfloat16)
    stacked = jnp.concatenate([weighted, shaped], axis=0)
    inverted = jnp.dot(stacked, tt_ref[...], preferred_element_type=jnp.float32)
    low16 = lax.broadcasted_iota(jnp.int32, (modes_here, LANES), 1) < half
    for pair in range(bands // 2):
        first = inverted[0:modes_here, pair * LANES : (pair + 1) * LANES]
        second = inverted[modes_here:, pair * LANES : (pair + 1) * LANES]
        send_ref[2 * pair, 0:modes_here, :] = jnp.where(
            low16, first, pltpu.roll(second, half, axis=1)
        ).astype(jnp.bfloat16)
        send_ref[2 * pair + 1, 0:modes_here, :] = jnp.where(
            low16, pltpu.roll(first, half, axis=1), second
        ).astype(jnp.bfloat16)
    halo = lax.dot_general(
        ht_ref[...], stacked, (((1,), (1,)), ((), ())), preferred_element_type=jnp.float32
    )
    halo = halo.reshape(bands, 8, 2 * modes_here)
    row8 = lax.broadcasted_iota(jnp.int32, (bands, 8, LANES), 1)
    lane8 = lax.broadcasted_iota(jnp.int32, (bands, 8, LANES), 2)
    wide = jnp.concatenate([halo, jnp.zeros((bands, 8, LANES - 2 * modes_here), jnp.float32)], axis=2)
    wide = wide.reshape(bands * 8, LANES)
    at = me * modes_here
    as_first = pltpu.roll(wide, at, axis=1).reshape(bands, 8, LANES)
    as_second = pltpu.roll(wide, (at + LANES - modes_here) % LANES, axis=1).reshape(bands, 8, LANES)
    placed = jnp.where(row8 < 4, as_first, as_second)
    pieces = jnp.zeros((8, LANES), jnp.float32)
    row = lax.broadcasted_iota(jnp.int32, (8, LANES), 0)
    energy = jnp.full((8, LANES), energy, jnp.float32)
    for at_row, piece in enumerate(split3(part_ref[...]) + split3(energy)):
        pieces = jnp.where(row == at_row, piece, pieces)
    pieces = jnp.broadcast_to(pieces[None], (bands, 8, LANES))
    mine = lane8 // modes_here == me
    scalar_at = lane8 == ((me + 1) % 8) * modes_here
    tail = jnp.where(mine, placed, jnp.where(scalar_at, pieces, 0.0))
    send_ref[:, modes_here:, :] = tail.astype(jnp.bfloat16)


def relax_kernel(
    target_ref, col_ref, wgt_ref, miss_ref, rate_ref, modes_ref, tt_ref, field_ref, part_ref,
    col_scr, seen_scr, inc_scr, one_scr,
):
    per_row, rows = col_ref.shape
    bands, _, _ = modes_ref.shape
    n_modes, columns = tt_ref.shape
    modes_here = n_modes // bands
    fill_cols(col_ref, col_scr)
    lane = lane_iota()
    quads, scalars = [], jnp.zeros((8, LANES), jnp.float32)
    for quad in range(bands // 8):
        total = jnp.zeros((8, LANES), jnp.float32)
        for at in range(8):
            tail = modes_ref[quad * 8 + at, modes_here:, :].astype(jnp.float32)
            window = lane // modes_here
            total = jnp.where(window == at, tail, total)
            scalars = scalars + jnp.where(window == (at + 1) % 8, tail, 0.0)
        quads.append(total)
    halo = jnp.concatenate(quads, axis=1)
    row = lax.broadcasted_iota(jnp.int32, (8, LANES), 0)
    misfit = jnp.sum(jnp.where(row < 3, scalars, 0.0))
    energy = jnp.sum(jnp.where((row >= 3) & (row < 6), scalars, 0.0))
    weight = jnp.max(miss_ref[8:16, :])
    misfit_v = jnp.full((8, LANES), misfit + weight - target_ref[0], jnp.float32)
    step = (misfit_v / jnp.full((8, LANES), energy + 1.0, jnp.float32))[0:1, 0:1]
    main = modes_ref[:, 0:modes_here, :].reshape(n_modes, LANES)
    left = jnp.concatenate([main.astype(jnp.float32).T, halo], axis=0).astype(jnp.bfloat16)
    pulled = jnp.dot(left, tt_ref[...], preferred_element_type=jnp.float32)
    inc_scr[8 : 8 + rows, :] = step * pulled[0:rows] + NOISE_AMP * pulled[rows : 2 * rows]
    edge = step * pulled[2 * rows : 2 * rows + 4] + NOISE_AMP * pulled[2 * rows + 4 : 2 * rows + 8]
    inc_scr[6:8, :] = edge[0:2]
    inc_scr[8 + rows : 10 + rows, :] = edge[2:4]

    def beside(values):
        return pltpu.roll(values, 1, axis=1) + pltpu.roll(values, columns - 1, axis=1)

    here = inc_scr[7 : 9 + rows, :]
    around = inc_scr[6 : 8 + rows, :] + inc_scr[8 : 10 + rows, :] + beside(here)
    one_scr[7 : 9 + rows, :] = (1.0 - RELAX_RATE) * here + rate_ref[7 : 9 + rows, :] * (around - here)
    here = one_scr[8 : 8 + rows, :]
    around = one_scr[7 : 7 + rows, :] + one_scr[9 : 9 + rows, :] + beside(here)
    field_ref[...] = (1.0 - RELAX_RATE) * here + rate_ref[8 : 8 + rows, :] * (
        around - inc_scr[8 : 8 + rows, :]
    )
    gather_rows(field_ref, col_scr, seen_scr, per_row)
    left_over = miss_ref[0:8, :] - packed(seen_scr, per_row)
    part = 0.5 * jnp.sum(wgt_ref[...] * left_over * left_over)
    part_ref[...] = jnp.full(part_ref.shape, part, jnp.float32)


SMEM = pl.BlockSpec(memory_space=pltpu.SMEM)
VMEM = pl.BlockSpec(memory_space=pltpu.VMEM)


def call(kernel, in_specs, out_shape, scratch, name):
    return pl.pallas_call(
        kernel,
        in_specs=in_specs,
        out_specs=jax.tree.map(lambda _: VMEM, out_shape),
        out_shape=out_shape,
        scratch_shapes=scratch,
        name=name,
        compiler_params=pltpu.CompilerParams(vmem_limit_bytes=VMEM_LIMIT),
    )


def swapped(value, axis, bit):
    mask = 2**bit
    pairs = [(source, source ^ mask) for source in range(lax.axis_size(axis))]
    return lax.ppermute(value, axis, pairs)


def per_device(
    stream, depth_field, obs_col, obs_val, obs_weight, log_weight, target, spectrum, noise_coef,
    selection,
):
    _, rows, columns = stream.shape
    per_row = obs_col.shape[1]
    modes_here, n_modes = spectrum.shape
    bands = lax.axis_size("space")
    particles = lax.axis_size("particle")
    y_table = table(rows * bands, n_modes // 2)
    tt_all = jnp.asarray(np.ascontiguousarray(y_table.T))
    ht_all = jnp.asarray(halo_table(y_table, bands))
    f32, bf16 = jnp.float32, jnp.bfloat16
    shape = jax.ShapeDtypeStruct
    groups = [[g * GROUP + i for i in range(GROUP)] for g in range(particles // GROUP)]
    slot = lax.axis_index("particle")
    meta = jnp.stack([slot, lax.axis_index("space")]).astype(jnp.int32)
    own = stream[0]
    col_t = obs_col.T
    tile = pltpu.VMEM((rows, LANES), f32)
    col_tile = pltpu.VMEM((rows, LANES), jnp.int32)

    seen = call(
        observe_kernel, [SMEM, VMEM, VMEM], shape((GROUP, 16, LANES), f32), [col_tile, tile], "observe"
    )(log_weight, col_t, own)
    seen = lax.all_to_all(seen, "particle", 0, 0, axis_index_groups=groups, tiled=True)
    noise = jnp.broadcast_to(noise_coef, (GROUP,) + noise_coef.shape[1:])
    noise = lax.all_to_all(noise, "particle", 0, 0, axis_index_groups=groups, tiled=True)

    weight_p = pack(obs_weight)
    send, miss, part = call(
        gradient_kernel,
        [SMEM, SMEM, VMEM, VMEM, VMEM, VMEM, VMEM],
        (shape((bands, 8, LANES), bf16), shape((16, LANES), f32), shape((8, LANES), f32)),
        [col_tile, tile, pltpu.VMEM((rows, columns), f32)],
        "gradient",
    )(meta, selection, col_t, pack(obs_val), weight_p, seen, tt_all)
    col_modes = lax.all_to_all(send, "space", 0, 0, tiled=True)

    send = call(
        spectral_kernel,
        [SMEM, SMEM, VMEM, VMEM, VMEM, VMEM, VMEM, VMEM],
        shape((bands, modes_here + 8, LANES), bf16),
        [],
        "spectral",
    )(meta, selection, col_modes, noise, spectrum, part, tt_all, ht_all)
    band_modes = lax.all_to_all(send, "space", 0, 0, tiled=True)

    above = lax.ppermute(depth_field[-1:], "space", [(i, i + 1) for i in range(bands - 1)])
    below = lax.ppermute(depth_field[:1], "space", [(i + 1, i) for i in range(bands - 1)])
    blank = jnp.zeros((7, columns), f32)
    depth = jnp.concatenate([blank, above, depth_field, below, blank], axis=0)
    rate = RELAX_RATE * depth / (4.0 * depth + STRETCH)

    fields = own
    for section in range(2):
        chosen = selection[section, slot]
        fields = jnp.where(chosen < 1, fields, swapped(fields, "particle", section))

    field, part = call(
        relax_kernel,
        [SMEM, VMEM, VMEM, VMEM, VMEM, VMEM, VMEM],
        (shape((rows, columns), f32), shape((bands, 1, LANES), f32)),
        [col_tile, tile, pltpu.VMEM((rows + 16, columns), f32), pltpu.VMEM((rows + 16, columns), f32)],
        "relax",
    )(target, col_t, weight_p, miss, rate, band_modes, tt_all)
    parts = lax.all_to_all(part, "space", 0, 0, tiled=True)
    misfit_out = jnp.sum(parts[:, 0, 0:1], axis=0)
    return (fields + field)[None], misfit_out


def solution(mesh):
    return jax.shard_map(
        per_device,
        mesh=mesh,
        in_specs=(
            P("particle", "space", None),
            P("space", None),
            P("space", None),
            P("space", None),
            P("space", None),
            P("particle"),
            P(),
            P("space", None),
            P("particle", "space", None),
            P(),
        ),
        out_specs=(P("particle", "space", None), P("particle")),
        check_vma=False,
    )
```

```python
import math

import jax
import jax.numpy as jnp
import ml_dtypes
import numpy as np
from jax import lax
from jax.experimental import pallas as pl
from jax.experimental.pallas import tpu as pltpu
from jax.sharding import PartitionSpec as P

STRETCH = 0.05
RELAX_RATE = 0.8
NOISE_AMP = 0.3
LANES = 128
GROUP = 4
VMEM_LIMIT = 48 * 1024 * 1024


def table(extent, half_modes):
    cell = np.arange(extent, dtype=np.int64)[:, None]
    freq = np.arange(half_modes + 1, dtype=np.int64)[None, :]
    angles = (cell * freq % extent).astype(np.float64) * (2.0 * math.pi / extent)
    return np.concatenate([np.cos(angles), np.sin(angles[:, 1:half_modes])], axis=1).astype(
        ml_dtypes.bfloat16
    )


def halo_table(y_table, bands):
    rows = y_table.shape[0]
    width = rows // bands
    out = np.zeros((bands, 2, 4, y_table.shape[1]), dtype=y_table.dtype)
    for band in range(bands):
        for at, row in enumerate((-2, -1, width, width + 1)):
            source = band * width + row
            if 0 <= source < rows:
                out[band, :, at] = y_table[source]
    return out.reshape(bands * 8, y_table.shape[1])


def lane_iota():
    return lax.broadcasted_iota(jnp.int32, (8, LANES), 1)


def split3(value):
    high = value.astype(jnp.bfloat16).astype(jnp.float32)
    rest = value - high
    mid = rest.astype(jnp.bfloat16).astype(jnp.float32)
    return high, mid, rest - mid


def source_slot(sel_ref, meta_ref):
    slot = meta_ref[0]
    one = jnp.where(sel_ref[1, slot] < 1, slot, slot ^ 2)
    return jnp.where(sel_ref[0, one] < 1, one, one ^ 1)


def fill_tile(source_ref, scr):
    per_row = source_ref.shape[0]
    scr[...] = jnp.zeros(scr.shape, scr.dtype)
    scr[:, 0:per_row] = source_ref[...].T


def gather_rows(field_ref, col_scr, seen_scr):
    rows, columns = field_ref.shape
    for at in range(0, rows, 8):
        cols = col_scr[at : at + 8, :]
        high, low = cols >> 7, cols & 127
        seen = jnp.zeros((8, LANES), jnp.float32)
        for chunk in range(columns // LANES):
            here = field_ref[at : at + 8, chunk * LANES : (chunk + 1) * LANES]
            got = jnp.take_along_axis(here, low, axis=1, mode="promise_in_bounds")
            seen = jnp.where(high == chunk, got, seen)
        seen_scr[at : at + 8, :] = seen


def packed(tile, per_row):
    lane = lane_iota()
    out = tile[0:8, :]
    for group in range(1, tile.shape[0] // 8):
        rolled = pltpu.roll(tile[group * 8 : group * 8 + 8, :], group * per_row, axis=1)
        out = jnp.where(lane // per_row == group, rolled, out)
    return out


def observe_kernel(
    lw_ref, col_hbm, val_hbm, wgt_hbm, noise_hbm, stream_hbm, out_ref, col_scr, wgt_scr,
    col_ref, val_ref, wgt_ref, noise_ref, stream_ref, val_scr, seen_scr, sems,
):
    copies = [
        pltpu.make_async_copy(source, to, sems.at[at])
        for at, (source, to) in enumerate(
            (
                (col_hbm, col_ref),
                (val_hbm, val_ref),
                (stream_hbm, stream_ref),
                (noise_hbm, noise_ref),
                (wgt_hbm, wgt_ref),
            )
        )
    ]
    for copy in copies:
        copy.start()
    per_row = col_ref.shape[0]
    modes_here, n_modes = noise_ref.shape
    copies[0].wait()
    copies[1].wait()
    fill_tile(col_ref, col_scr)
    fill_tile(val_ref, val_scr)
    copies[2].wait()
    gather_rows(stream_ref, col_scr, seen_scr)
    mismatch = packed(val_scr[...] - seen_scr[...], per_row)
    weight = jnp.full((8, LANES), lw_ref[0], jnp.float32)
    row = lax.broadcasted_iota(jnp.int32, (8, LANES), 0)
    high, mid, low = split3(weight)
    weight = jnp.where(row == 0, high, jnp.where(row == 1, mid, jnp.where(row == 2, low, 0.0)))
    values = jnp.concatenate(list(split3(mismatch)) + [weight], axis=0).astype(jnp.bfloat16)
    copies[4].wait()
    fill_tile(wgt_ref, wgt_scr)
    copies[3].wait()
    noise = noise_ref[...]
    chunks = n_modes // LANES
    for peer in range(GROUP):
        for chunk in range(chunks):
            out_ref[peer, chunk * modes_here : (chunk + 1) * modes_here, :] = noise[
                :, chunk * LANES : (chunk + 1) * LANES
            ]
        out_ref[peer, chunks * modes_here :, :] = values


def gradient_kernel(
    meta_ref, sel_ref, col_scr, wgt_scr, seen_ref, tt_hbm, send_ref, miss_ref, part_ref,
    tt_ref, grad_scr, sem,
):
    load = pltpu.make_async_copy(tt_hbm, tt_ref, sem)
    load.start()
    rows = grad_scr.shape[0]
    per_row = LANES * 8 // rows
    columns = tt_ref.shape[1]
    position = source_slot(sel_ref, meta_ref) & (GROUP - 1)
    first = seen_ref.shape[1] - 32
    sent = seen_ref[position][first:, :].astype(jnp.float32)
    mismatch = sent[0:8] + sent[8:16] + sent[16:24]
    weight = sent[24:25] + sent[25:26] + sent[26:27]
    miss_ref[rows:, :] = jnp.broadcast_to(weight, (8, LANES))
    tiles = [mismatch] + [
        pltpu.roll(mismatch, LANES - group * per_row, axis=1) for group in range(1, rows // 8)
    ]
    mismatch = jnp.concatenate(tiles, axis=0)
    miss_ref[0:rows, :] = mismatch
    weighted = wgt_scr[...] * mismatch
    part_ref[...] = jnp.full((8, LANES), 0.5 * jnp.sum(weighted * mismatch), jnp.float32)

    def repeated(tile):
        step = per_row
        while step < LANES:
            tile = tile + pltpu.roll(tile, step, axis=1)
            step *= 2
        return tile

    diagonal = lane_iota() // per_row == lax.broadcasted_iota(jnp.int32, (8, LANES), 0)
    row_f = lax.broadcasted_iota(jnp.int32, (LANES, LANES), 0).astype(jnp.float32)
    for group in range(rows // 8):
        at = group * 8
        cols = repeated(col_scr[at : at + 8, :])
        high = jnp.where(diagonal, cols >> 7, -1)
        low = jnp.sum(
            jnp.where(diagonal, (cols & 127).astype(jnp.float32), 0.0), axis=0, keepdims=True
        )
        one_hot = jnp.where(row_f == low, 1.0, 0.0).astype(jnp.bfloat16)
        left = []
        for piece in split3(repeated(weighted[at : at + 8, :])):
            left.append(
                jnp.concatenate(
                    [jnp.where(high == chunk, piece, 0.0) for chunk in range(columns // LANES)], axis=0
                ).astype(jnp.bfloat16)
            )
        spread = lax.dot_general(
            jnp.concatenate(left, axis=1),
            jnp.concatenate([one_hot] * 3, axis=1),
            (((1,), (1,)), ((), ())),
            preferred_element_type=jnp.float32,
        )
        for chunk in range(columns // LANES):
            grad_scr[at : at + 8, chunk * LANES : (chunk + 1) * LANES] = spread[
                chunk * 8 : chunk * 8 + 8, :
            ]
    gradient = grad_scr[...].astype(jnp.bfloat16)
    load.wait()
    modes = lax.dot_general(
        tt_ref[...], gradient, (((1,), (1,)), ((), ())), preferred_element_type=jnp.float32
    )
    bands = send_ref.shape[0]
    split = modes.reshape(bands, 2, 8, rows)
    send_ref[...] = jnp.concatenate([split[:, 0], split[:, 1]], axis=2).astype(jnp.bfloat16)


def spectral_kernel(
    meta_ref, sel_ref, modes_ref, noise_ref, spec_ref, part_ref, tt_ref, ht_ref, send_ref,
):
    bands = modes_ref.shape[0]
    half = LANES // 2
    modes_here, n_modes = spec_ref.shape
    rows = tt_ref.shape[1]
    norm_factor = 4.0 / (rows * rows)
    position = source_slot(sel_ref, meta_ref) & (GROUP - 1)
    me = meta_ref[1] & 7
    lane = lane_iota()
    low = lane < half
    tops, bottoms = [], []
    for pair in range(bands // 2):
        even = modes_ref[2 * pair].astype(jnp.float32)
        odd = modes_ref[2 * pair + 1].astype(jnp.float32)
        tops.append(jnp.where(low, even, pltpu.roll(odd, half, axis=1)))
        bottoms.append(jnp.where(low, pltpu.roll(even, half, axis=1), odd))
    columns = jnp.concatenate(
        [jnp.concatenate(tops, axis=1), jnp.concatenate(bottoms, axis=1)], axis=0
    ).astype(jnp.bfloat16)
    coefficients = lax.dot_general(
        columns, tt_ref[...], (((1,), (1,)), ((), ())), preferred_element_type=jnp.float32
    )
    scaled = norm_factor * spec_ref[...]
    weighted = coefficients * scaled
    energy = jnp.sum(coefficients * weighted)
    noise = noise_ref[position][0 : noise_ref.shape[1] - 32, :]
    noise = jnp.concatenate(
        [noise[at : at + modes_here] for at in range(0, noise.shape[0], modes_here)], axis=1
    )
    shaped = (jnp.sqrt(scaled) * noise.astype(jnp.float32)).astype(jnp.bfloat16)
    weighted = weighted.astype(jnp.bfloat16)
    stacked = jnp.concatenate([weighted, shaped], axis=0)
    inverted = jnp.dot(stacked, tt_ref[...], preferred_element_type=jnp.float32)
    low16 = lax.broadcasted_iota(jnp.int32, (modes_here, LANES), 1) < half
    for pair in range(bands // 2):
        first = inverted[0:modes_here, pair * LANES : (pair + 1) * LANES]
        second = inverted[modes_here:, pair * LANES : (pair + 1) * LANES]
        send_ref[2 * pair, 0:modes_here, :] = jnp.where(
            low16, first, pltpu.roll(second, half, axis=1)
        ).astype(jnp.bfloat16)
        send_ref[2 * pair + 1, 0:modes_here, :] = jnp.where(
            low16, pltpu.roll(first, half, axis=1), second
        ).astype(jnp.bfloat16)
    halo = lax.dot_general(
        ht_ref[...], stacked, (((1,), (1,)), ((), ())), preferred_element_type=jnp.float32
    )
    halo = halo.reshape(bands, 8, 2 * modes_here)
    row8 = lax.broadcasted_iota(jnp.int32, (bands, 8, LANES), 1)
    lane8 = lax.broadcasted_iota(jnp.int32, (bands, 8, LANES), 2)
    wide = jnp.concatenate([halo, jnp.zeros((bands, 8, LANES - 2 * modes_here), jnp.float32)], axis=2)
    wide = wide.reshape(bands * 8, LANES)
    at = me * modes_here
    as_first = pltpu.roll(wide, at, axis=1).reshape(bands, 8, LANES)
    as_second = pltpu.roll(wide, (at + LANES - modes_here) % LANES, axis=1).reshape(bands, 8, LANES)
    placed = jnp.where(row8 < 4, as_first, as_second)
    pieces = jnp.zeros((8, LANES), jnp.float32)
    row = lax.broadcasted_iota(jnp.int32, (8, LANES), 0)
    energy = jnp.full((8, LANES), energy, jnp.float32)
    for at_row, piece in enumerate(split3(part_ref[...]) + split3(energy)):
        pieces = jnp.where(row == at_row, piece, pieces)
    pieces = jnp.broadcast_to(pieces[None], (bands, 8, LANES))
    mine = lane8 // modes_here == me
    scalar_at = lane8 == ((me + 1) % 8) * modes_here
    tail = jnp.where(mine, placed, jnp.where(scalar_at, pieces, 0.0))
    send_ref[:, modes_here:, :] = tail.astype(jnp.bfloat16)


def relax_kernel(
    target_ref, col_scr, wgt_scr, miss_ref, depth_hbm, above_ref, below_ref, modes_ref, tt_ref,
    field_ref, part_ref, seen_scr, inc_scr, one_scr, rate_ref, depth_ref, sem,
):
    depth = pltpu.make_async_copy(depth_hbm, depth_ref, sem)
    depth.start()
    rows = depth_ref.shape[0]

    def rate(depth):
        return RELAX_RATE * depth / (4.0 * depth + STRETCH)

    bands, _, _ = modes_ref.shape
    n_modes, columns = tt_ref.shape
    modes_here = n_modes // bands
    lane = lane_iota()
    quads, scalars = [], jnp.zeros((8, LANES), jnp.float32)
    for quad in range(bands // 8):
        total = jnp.zeros((8, LANES), jnp.float32)
        for at in range(8):
            tail = modes_ref[quad * 8 + at, modes_here:, :].astype(jnp.float32)
            window = lane // modes_here
            total = jnp.where(window == at, tail, total)
            scalars = scalars + jnp.where(window == (at + 1) % 8, tail, 0.0)
        quads.append(total)
    halo = jnp.concatenate(quads, axis=1)
    row = lax.broadcasted_iota(jnp.int32, (8, LANES), 0)
    misfit = jnp.sum(jnp.where(row < 3, scalars, 0.0))
    energy = jnp.sum(jnp.where((row >= 3) & (row < 6), scalars, 0.0))
    weight = jnp.max(miss_ref[rows:, :])
    misfit_v = jnp.full((8, LANES), misfit + weight - target_ref[0], jnp.float32)
    step = (misfit_v / jnp.full((8, LANES), energy + 1.0, jnp.float32))[0:1, 0:1]
    main = modes_ref[:, 0:modes_here, :].reshape(n_modes, LANES)
    left = jnp.concatenate([main.astype(jnp.float32).T, halo], axis=0).astype(jnp.bfloat16)
    pulled = jnp.dot(left, tt_ref[...], preferred_element_type=jnp.float32)
    inc_scr[8 : 8 + rows, :] = step * pulled[0:rows] + NOISE_AMP * pulled[rows : 2 * rows]
    edge = step * pulled[2 * rows : 2 * rows + 4] + NOISE_AMP * pulled[2 * rows + 4 : 2 * rows + 8]
    inc_scr[6:8, :] = edge[0:2]
    inc_scr[8 + rows : 10 + rows, :] = edge[2:4]

    depth.wait()
    rate_ref[7:8, :] = rate(above_ref[...])
    rate_ref[8 : 8 + rows, :] = rate(depth_ref[...])
    rate_ref[8 + rows : 9 + rows, :] = rate(below_ref[...])

    def beside(values):
        return pltpu.roll(values, 1, axis=1) + pltpu.roll(values, columns - 1, axis=1)

    here = inc_scr[7 : 9 + rows, :]
    around = inc_scr[6 : 8 + rows, :] + inc_scr[8 : 10 + rows, :] + beside(here)
    one_scr[7 : 9 + rows, :] = (1.0 - RELAX_RATE) * here + rate_ref[7 : 9 + rows, :] * (around - here)
    here = one_scr[8 : 8 + rows, :]
    around = one_scr[7 : 7 + rows, :] + one_scr[9 : 9 + rows, :] + beside(here)
    field_ref[...] = (1.0 - RELAX_RATE) * here + rate_ref[8 : 8 + rows, :] * (
        around - inc_scr[8 : 8 + rows, :]
    )
    gather_rows(field_ref, col_scr, seen_scr)
    left_over = miss_ref[0:rows, :] - seen_scr[...]
    part = 0.5 * jnp.sum(wgt_scr[...] * left_over * left_over)
    part_ref[...] = jnp.full(part_ref.shape, part, jnp.float32)


SMEM = pl.BlockSpec(memory_space=pltpu.SMEM)
VMEM = pl.BlockSpec(memory_space=pltpu.VMEM)
HBM = pl.BlockSpec(memory_space=pltpu.HBM)


COST = {"observe": 40, "gradient": 40, "spectral": 1, "relax": 1}


def call(kernel, in_specs, out_shape, scratch, name):
    return pl.pallas_call(
        kernel,
        in_specs=in_specs,
        out_specs=jax.tree.map(lambda _: VMEM, out_shape),
        out_shape=out_shape,
        scratch_shapes=scratch,
        name=name,
        cost_estimate=pl.CostEstimate(
            flops=COST[name] * 10**9, transcendentals=0, bytes_accessed=4 * 10**6
        ),
        compiler_params=pltpu.CompilerParams(vmem_limit_bytes=VMEM_LIMIT),
    )


def in_hbm(value):
    return pltpu.with_memory_space_constraint(value, pltpu.HBM)


def swapped(value, axis, bit):
    mask = 2**bit
    pairs = [(source, source ^ mask) for source in range(lax.axis_size(axis))]
    return lax.ppermute(value, axis, pairs)


def per_device(
    stream, depth_field, obs_col, obs_val, obs_weight, log_weight, target, spectrum, noise_coef,
    selection,
):
    _, rows, columns = stream.shape
    per_row = obs_col.shape[1]
    modes_here, n_modes = spectrum.shape
    bands = lax.axis_size("space")
    particles = lax.axis_size("particle")
    y_table = table(rows * bands, n_modes // 2)
    tt_all = jnp.asarray(np.ascontiguousarray(y_table.T))
    ht_all = jnp.asarray(halo_table(y_table, bands))
    f32, bf16 = jnp.float32, jnp.bfloat16
    shape = jax.ShapeDtypeStruct
    groups = [[g * GROUP + i for i in range(GROUP)] for g in range(particles // GROUP)]
    slot = lax.axis_index("particle")
    meta = jnp.stack([slot, lax.axis_index("space")]).astype(jnp.int32)
    own = stream[0]
    col_t, val_t, wgt_t = obs_col.T, obs_val.T, obs_weight.T
    vmem = pltpu.VMEM
    tile = vmem((rows, LANES), f32)
    whole = vmem((rows, columns), f32)
    padded = vmem((rows + 16, columns), f32)
    small = (per_row, rows)
    dma = pltpu.SemaphoreType.DMA

    sent, col_tile, wgt_tile = call(
        observe_kernel,
        [SMEM, HBM, HBM, HBM, HBM, HBM],
        (
            shape((GROUP, modes_here * n_modes // LANES + 32, LANES), bf16),
            shape((rows, LANES), jnp.int32),
            shape((rows, LANES), f32),
        ),
        [vmem(small, jnp.int32), vmem(small, f32), vmem(small, f32), vmem((modes_here, n_modes), bf16),
         whole, tile, tile, dma((5,))],
        "observe",
    )(log_weight, *map(in_hbm, (col_t, val_t, wgt_t, noise_coef[0], own)))
    sent, held = lax.optimization_barrier((sent, own))
    sent = lax.all_to_all(sent, "particle", 0, 0, axis_index_groups=groups, tiled=True)
    swap = swapped(held, "particle", 0)

    send, miss, part = call(
        gradient_kernel,
        [SMEM, SMEM, VMEM, VMEM, VMEM, HBM],
        (shape((bands, 8, LANES), bf16), shape((rows + 8, LANES), f32), shape((8, LANES), f32)),
        [vmem((n_modes, columns), bf16), whole, dma(())],
        "gradient",
    )(meta, selection, col_tile, wgt_tile, sent, in_hbm(tt_all))
    col_modes = lax.all_to_all(send, "space", 0, 0, tiled=True)

    near = jnp.where(selection[0, slot] < 1, own, swap)
    far = swapped(near, "particle", 1)
    col_modes, near = lax.optimization_barrier((col_modes, near))

    send = call(
        spectral_kernel,
        [SMEM, SMEM, VMEM, VMEM, VMEM, VMEM, VMEM, VMEM],
        shape((bands, modes_here + 8, LANES), bf16),
        [],
        "spectral",
    )(meta, selection, col_modes, sent, spectrum, part, tt_all, ht_all)
    send, depth = lax.optimization_barrier((send, depth_field))
    band_modes = lax.all_to_all(send, "space", 0, 0, tiled=True)
    above = lax.ppermute(depth[-1:], "space", [(i, i + 1) for i in range(bands - 1)])
    below = lax.ppermute(depth[:1], "space", [(i + 1, i) for i in range(bands - 1)])

    field, part = call(
        relax_kernel,
        [SMEM, VMEM, VMEM, VMEM, HBM, VMEM, VMEM, VMEM, VMEM],
        (shape((rows, columns), f32), shape((bands, 1, LANES), f32)),
        [tile, padded, padded, padded, whole, dma(())],
        "relax",
    )(target, col_tile, wgt_tile, miss, in_hbm(depth_field), above, below, band_modes, tt_all)
    parts = lax.all_to_all(part, "space", 0, 0, tiled=True)
    analysis = field + jnp.where(selection[1, slot] < 1, near, far)
    parts, analysis = lax.optimization_barrier((parts, analysis))
    misfit_out = jnp.sum(parts[:, 0, 0:1], axis=0)
    return analysis[None], misfit_out


def solution(mesh):
    return jax.shard_map(
        per_device,
        mesh=mesh,
        in_specs=(
            P("particle", "space", None),
            P("space", None),
            P("space", None),
            P("space", None),
            P("space", None),
            P("particle"),
            P(),
            P("space", None),
            P("particle", "space", None),
            P(),
        ),
        out_specs=(P("particle", "space", None), P("particle")),
        check_vma=False,
    )
```

```python
import math

import jax
import jax.numpy as jnp
import ml_dtypes
import numpy as np
from jax import lax
from jax.experimental import pallas as pl
from jax.experimental.pallas import tpu as pltpu
from jax.sharding import PartitionSpec as P

STRETCH = 0.05
RELAX_RATE = 0.8
NOISE_AMP = 0.3
LANES = 128
GROUP = 4
VMEM_LIMIT = 48 * 1024 * 1024


def table(extent, half_modes):
    cell = np.arange(extent, dtype=np.int64)[:, None]
    freq = np.arange(half_modes + 1, dtype=np.int64)[None, :]
    angles = (cell * freq % extent).astype(np.float64) * (2.0 * math.pi / extent)
    return np.concatenate([np.cos(angles), np.sin(angles[:, 1:half_modes])], axis=1).astype(
        ml_dtypes.bfloat16
    )


def halo_table(y_table, bands):
    rows = y_table.shape[0]
    width = rows // bands
    out = np.zeros((bands, 2, 4, y_table.shape[1]), dtype=y_table.dtype)
    for band in range(bands):
        for at, row in enumerate((-2, -1, width, width + 1)):
            source = band * width + row
            if 0 <= source < rows:
                out[band, :, at] = y_table[source]
    return out.reshape(bands * 8, y_table.shape[1])


def lane_iota():
    return lax.broadcasted_iota(jnp.int32, (8, LANES), 1)


def split3(value):
    high = value.astype(jnp.bfloat16).astype(jnp.float32)
    rest = value - high
    mid = rest.astype(jnp.bfloat16).astype(jnp.float32)
    return high, mid, rest - mid


def source_slot(sel_ref, meta_ref):
    slot = meta_ref[0]
    one = jnp.where(sel_ref[1, slot] < 1, slot, slot ^ 2)
    return jnp.where(sel_ref[0, one] < 1, one, one ^ 1)


def fill_tile(source_ref, scr):
    per_row = source_ref.shape[0]
    scr[...] = jnp.zeros(scr.shape, scr.dtype)
    scr[:, 0:per_row] = source_ref[...].T


def gather_rows(field_ref, col_scr, seen_scr):
    rows, columns = field_ref.shape
    for at in range(0, rows, 8):
        cols = col_scr[at : at + 8, :]
        high, low = cols >> 7, cols & 127
        seen = jnp.zeros((8, LANES), jnp.float32)
        for chunk in range(columns // LANES):
            here = field_ref[at : at + 8, chunk * LANES : (chunk + 1) * LANES]
            got = jnp.take_along_axis(here, low, axis=1, mode="promise_in_bounds")
            seen = jnp.where(high == chunk, got, seen)
        seen_scr[at : at + 8, :] = seen


def packed(tile, per_row):
    lane = lane_iota()
    out = tile[0:8, :]
    for group in range(1, tile.shape[0] // 8):
        rolled = pltpu.roll(tile[group * 8 : group * 8 + 8, :], group * per_row, axis=1)
        out = jnp.where(lane // per_row == group, rolled, out)
    return out


def observe_kernel(
    lw_ref, col_hbm, val_hbm, wgt_hbm, noise_hbm, stream_hbm, depth_hbm, tt_hbm,
    out_ref, col_scr, wgt_scr, tt_ref, first_ref, last_ref,
    col_ref, val_ref, wgt_ref, noise_ref, stream_ref, depth_ref, val_scr, seen_scr, sems,
):
    rows = depth_hbm.shape[0]
    pairs = (
        (col_hbm, col_ref),
        (val_hbm, val_ref),
        (stream_hbm, stream_ref),
        (noise_hbm, noise_ref),
        (wgt_hbm, wgt_ref),
        (depth_hbm.at[0:8, :], depth_ref.at[0:8, :]),
        (depth_hbm.at[rows - 8 : rows, :], depth_ref.at[8:16, :]),
        (tt_hbm, tt_ref),
    )
    loads = [pltpu.make_async_copy(a, b, sems.at[at]) for at, (a, b) in enumerate(pairs)]
    for load in loads:
        load.start()
    per_row = col_ref.shape[0]
    modes_here, n_modes = noise_ref.shape
    loads[0].wait()
    loads[1].wait()
    fill_tile(col_ref, col_scr)
    fill_tile(val_ref, val_scr)
    loads[2].wait()
    gather_rows(stream_ref, col_scr, seen_scr)
    mismatch = packed(val_scr[...] - seen_scr[...], per_row)
    weight = jnp.full((8, LANES), lw_ref[0], jnp.float32)
    row = lax.broadcasted_iota(jnp.int32, (8, LANES), 0)
    high, mid, low = split3(weight)
    weight = jnp.where(row == 0, high, jnp.where(row == 1, mid, jnp.where(row == 2, low, 0.0)))
    values = jnp.concatenate(list(split3(mismatch)) + [weight], axis=0).astype(jnp.bfloat16)
    loads[4].wait()
    fill_tile(wgt_ref, wgt_scr)
    loads[3].wait()
    noise = noise_ref[...]
    chunks = n_modes // LANES
    for peer in range(GROUP):
        for chunk in range(chunks):
            out_ref[peer, chunk * modes_here : (chunk + 1) * modes_here, :] = noise[
                :, chunk * LANES : (chunk + 1) * LANES
            ]
        out_ref[peer, chunks * modes_here :, :] = values
    loads[5].wait()
    loads[6].wait()
    first_ref[...] = depth_ref[0:1, :]
    last_ref[...] = depth_ref[15:16, :]
    loads[7].wait()


def gradient_kernel(
    meta_ref, sel_ref, col_scr, wgt_scr, seen_ref, tt_ref, send_ref, miss_ref, part_ref, grad_scr,
):
    rows = grad_scr.shape[0]
    per_row = LANES * 8 // rows
    columns = tt_ref.shape[1]
    position = source_slot(sel_ref, meta_ref) & (GROUP - 1)
    first = seen_ref.shape[1] - 32
    sent = seen_ref[position][first:, :].astype(jnp.float32)
    mismatch = sent[0:8] + sent[8:16] + sent[16:24]
    weight = sent[24:25] + sent[25:26] + sent[26:27]
    miss_ref[rows:, :] = jnp.broadcast_to(weight, (8, LANES))
    tiles = [mismatch] + [
        pltpu.roll(mismatch, LANES - group * per_row, axis=1) for group in range(1, rows // 8)
    ]
    mismatch = jnp.concatenate(tiles, axis=0)
    miss_ref[0:rows, :] = mismatch
    weighted = wgt_scr[...] * mismatch
    part_ref[...] = jnp.full((8, LANES), 0.5 * jnp.sum(weighted * mismatch), jnp.float32)

    def repeated(tile):
        step = per_row
        while step < LANES:
            tile = tile + pltpu.roll(tile, step, axis=1)
            step *= 2
        return tile

    diagonal = lane_iota() // per_row == lax.broadcasted_iota(jnp.int32, (8, LANES), 0)
    row_f = lax.broadcasted_iota(jnp.int32, (LANES, LANES), 0).astype(jnp.float32)
    for group in range(rows // 8):
        at = group * 8
        cols = repeated(col_scr[at : at + 8, :])
        high = jnp.where(diagonal, cols >> 7, -1)
        low = jnp.sum(
            jnp.where(diagonal, (cols & 127).astype(jnp.float32), 0.0), axis=0, keepdims=True
        )
        one_hot = jnp.where(row_f == low, 1.0, 0.0).astype(jnp.bfloat16)
        left = []
        for piece in split3(repeated(weighted[at : at + 8, :])):
            left.append(
                jnp.concatenate(
                    [jnp.where(high == chunk, piece, 0.0) for chunk in range(columns // LANES)], axis=0
                ).astype(jnp.bfloat16)
            )
        spread = lax.dot_general(
            jnp.concatenate(left, axis=1),
            jnp.concatenate([one_hot] * 3, axis=1),
            (((1,), (1,)), ((), ())),
            preferred_element_type=jnp.float32,
        )
        for chunk in range(columns // LANES):
            grad_scr[at : at + 8, chunk * LANES : (chunk + 1) * LANES] = spread[
                chunk * 8 : chunk * 8 + 8, :
            ]
    gradient = grad_scr[...].astype(jnp.bfloat16)
    modes = lax.dot_general(
        tt_ref[...], gradient, (((1,), (1,)), ((), ())), preferred_element_type=jnp.float32
    )
    bands = send_ref.shape[0]
    split = modes.reshape(bands, 2, 8, rows)
    send_ref[...] = jnp.concatenate([split[:, 0], split[:, 1]], axis=2).astype(jnp.bfloat16)


def spectral_kernel(
    meta_ref, sel_ref, modes_ref, noise_ref, spec_ref, part_ref, tt_ref, ht_ref, send_ref,
):
    bands = modes_ref.shape[0]
    half = LANES // 2
    modes_here, n_modes = spec_ref.shape
    rows = tt_ref.shape[1]
    norm_factor = 4.0 / (rows * rows)
    position = source_slot(sel_ref, meta_ref) & (GROUP - 1)
    me = meta_ref[1] & 7
    lane = lane_iota()
    low = lane < half
    tops, bottoms = [], []
    for pair in range(bands // 2):
        even = modes_ref[2 * pair].astype(jnp.float32)
        odd = modes_ref[2 * pair + 1].astype(jnp.float32)
        tops.append(jnp.where(low, even, pltpu.roll(odd, half, axis=1)))
        bottoms.append(jnp.where(low, pltpu.roll(even, half, axis=1), odd))
    columns = jnp.concatenate(
        [jnp.concatenate(tops, axis=1), jnp.concatenate(bottoms, axis=1)], axis=0
    ).astype(jnp.bfloat16)
    coefficients = lax.dot_general(
        columns, tt_ref[...], (((1,), (1,)), ((), ())), preferred_element_type=jnp.float32
    )
    scaled = norm_factor * spec_ref[...]
    weighted = coefficients * scaled
    energy = jnp.sum(coefficients * weighted)
    noise = noise_ref[position][0 : noise_ref.shape[1] - 32, :]
    noise = jnp.concatenate(
        [noise[at : at + modes_here] for at in range(0, noise.shape[0], modes_here)], axis=1
    )
    shaped = (jnp.sqrt(scaled) * noise.astype(jnp.float32)).astype(jnp.bfloat16)
    weighted = weighted.astype(jnp.bfloat16)
    stacked = jnp.concatenate([weighted, shaped], axis=0)
    inverted = jnp.dot(stacked, tt_ref[...], preferred_element_type=jnp.float32)
    low16 = lax.broadcasted_iota(jnp.int32, (modes_here, LANES), 1) < half
    for pair in range(bands // 2):
        first = inverted[0:modes_here, pair * LANES : (pair + 1) * LANES]
        second = inverted[modes_here:, pair * LANES : (pair + 1) * LANES]
        send_ref[2 * pair, 0:modes_here, :] = jnp.where(
            low16, first, pltpu.roll(second, half, axis=1)
        ).astype(jnp.bfloat16)
        send_ref[2 * pair + 1, 0:modes_here, :] = jnp.where(
            low16, pltpu.roll(first, half, axis=1), second
        ).astype(jnp.bfloat16)
    halo = lax.dot_general(
        ht_ref[...], stacked, (((1,), (1,)), ((), ())), preferred_element_type=jnp.float32
    )
    halo = halo.reshape(bands, 8, 2 * modes_here)
    row8 = lax.broadcasted_iota(jnp.int32, (bands, 8, LANES), 1)
    lane8 = lax.broadcasted_iota(jnp.int32, (bands, 8, LANES), 2)
    wide = jnp.concatenate([halo, jnp.zeros((bands, 8, LANES - 2 * modes_here), jnp.float32)], axis=2)
    wide = wide.reshape(bands * 8, LANES)
    at = me * modes_here
    as_first = pltpu.roll(wide, at, axis=1).reshape(bands, 8, LANES)
    as_second = pltpu.roll(wide, (at + LANES - modes_here) % LANES, axis=1).reshape(bands, 8, LANES)
    placed = jnp.where(row8 < 4, as_first, as_second)
    pieces = jnp.zeros((8, LANES), jnp.float32)
    row = lax.broadcasted_iota(jnp.int32, (8, LANES), 0)
    energy = jnp.full((8, LANES), energy, jnp.float32)
    for at_row, piece in enumerate(split3(part_ref[...]) + split3(energy)):
        pieces = jnp.where(row == at_row, piece, pieces)
    pieces = jnp.broadcast_to(pieces[None], (bands, 8, LANES))
    mine = lane8 // modes_here == me
    scalar_at = lane8 == ((me + 1) % 8) * modes_here
    tail = jnp.where(mine, placed, jnp.where(scalar_at, pieces, 0.0))
    send_ref[:, modes_here:, :] = tail.astype(jnp.bfloat16)


def relax_kernel(
    target_ref, col_scr, wgt_scr, miss_ref, depth_hbm, above_ref, below_ref, modes_ref, tt_ref,
    field_ref, part_ref, seen_scr, inc_scr, one_scr, rate_ref, depth_ref, sem,
):
    depth = pltpu.make_async_copy(depth_hbm, depth_ref, sem)
    depth.start()
    rows = depth_ref.shape[0]

    def rate(depth):
        return RELAX_RATE * depth / (4.0 * depth + STRETCH)

    bands, _, _ = modes_ref.shape
    n_modes, columns = tt_ref.shape
    modes_here = n_modes // bands
    lane = lane_iota()
    quads, scalars = [], jnp.zeros((8, LANES), jnp.float32)
    for quad in range(bands // 8):
        total = jnp.zeros((8, LANES), jnp.float32)
        for at in range(8):
            tail = modes_ref[quad * 8 + at, modes_here:, :].astype(jnp.float32)
            window = lane // modes_here
            total = jnp.where(window == at, tail, total)
            scalars = scalars + jnp.where(window == (at + 1) % 8, tail, 0.0)
        quads.append(total)
    halo = jnp.concatenate(quads, axis=1)
    row = lax.broadcasted_iota(jnp.int32, (8, LANES), 0)
    misfit = jnp.sum(jnp.where(row < 3, scalars, 0.0))
    energy = jnp.sum(jnp.where((row >= 3) & (row < 6), scalars, 0.0))
    weight = jnp.max(miss_ref[rows:, :])
    misfit_v = jnp.full((8, LANES), misfit + weight - target_ref[0], jnp.float32)
    step = (misfit_v / jnp.full((8, LANES), energy + 1.0, jnp.float32))[0:1, 0:1]
    main = modes_ref[:, 0:modes_here, :].reshape(n_modes, LANES)
    left = jnp.concatenate([main.astype(jnp.float32).T, halo], axis=0).astype(jnp.bfloat16)
    pulled = jnp.dot(left, tt_ref[...], preferred_element_type=jnp.float32)
    inc_scr[8 : 8 + rows, :] = step * pulled[0:rows] + NOISE_AMP * pulled[rows : 2 * rows]
    edge = step * pulled[2 * rows : 2 * rows + 4] + NOISE_AMP * pulled[2 * rows + 4 : 2 * rows + 8]
    inc_scr[6:8, :] = edge[0:2]
    inc_scr[8 + rows : 10 + rows, :] = edge[2:4]

    depth.wait()
    rate_ref[7:8, :] = rate(above_ref[...])
    rate_ref[8 : 8 + rows, :] = rate(depth_ref[...])
    rate_ref[8 + rows : 9 + rows, :] = rate(below_ref[...])

    def beside(values):
        return pltpu.roll(values, 1, axis=1) + pltpu.roll(values, columns - 1, axis=1)

    here = inc_scr[7 : 9 + rows, :]
    around = inc_scr[6 : 8 + rows, :] + inc_scr[8 : 10 + rows, :] + beside(here)
    one_scr[7 : 9 + rows, :] = (1.0 - RELAX_RATE) * here + rate_ref[7 : 9 + rows, :] * (around - here)
    here = one_scr[8 : 8 + rows, :]
    around = one_scr[7 : 7 + rows, :] + one_scr[9 : 9 + rows, :] + beside(here)
    field_ref[...] = (1.0 - RELAX_RATE) * here + rate_ref[8 : 8 + rows, :] * (
        around - inc_scr[8 : 8 + rows, :]
    )
    gather_rows(field_ref, col_scr, seen_scr)
    left_over = miss_ref[0:rows, :] - seen_scr[...]
    part = 0.5 * jnp.sum(wgt_scr[...] * left_over * left_over)
    part_ref[...] = jnp.full(part_ref.shape, part, jnp.float32)


SMEM = pl.BlockSpec(memory_space=pltpu.SMEM)
VMEM = pl.BlockSpec(memory_space=pltpu.VMEM)
HBM = pl.BlockSpec(memory_space=pltpu.HBM)


COST = {"observe": 40, "gradient": 40, "spectral": 1, "relax": 1}


def call(kernel, in_specs, out_shape, scratch, name, out_specs=None):
    return pl.pallas_call(
        kernel,
        in_specs=in_specs,
        out_specs=out_specs or jax.tree.map(lambda _: VMEM, out_shape),
        out_shape=out_shape,
        scratch_shapes=scratch,
        name=name,
        cost_estimate=pl.CostEstimate(
            flops=COST[name] * 10**9, transcendentals=0, bytes_accessed=4 * 10**6
        ),
        compiler_params=pltpu.CompilerParams(vmem_limit_bytes=VMEM_LIMIT),
    )


def in_hbm(value):
    return pltpu.with_memory_space_constraint(value, pltpu.HBM)


def swapped(value, axis, bit):
    mask = 2**bit
    pairs = [(source, source ^ mask) for source in range(lax.axis_size(axis))]
    return lax.ppermute(value, axis, pairs)


def per_device(
    stream, depth_field, obs_col, obs_val, obs_weight, log_weight, target, spectrum, noise_coef,
    selection,
):
    _, rows, columns = stream.shape
    per_row = obs_col.shape[1]
    modes_here, n_modes = spectrum.shape
    bands = lax.axis_size("space")
    particles = lax.axis_size("particle")
    y_table = table(rows * bands, n_modes // 2)
    tt_all = jnp.asarray(np.ascontiguousarray(y_table.T))
    ht_all = jnp.asarray(halo_table(y_table, bands))
    f32, bf16 = jnp.float32, jnp.bfloat16
    shape = jax.ShapeDtypeStruct
    groups = [[g * GROUP + i for i in range(GROUP)] for g in range(particles // GROUP)]
    slot = lax.axis_index("particle")
    meta = jnp.stack([slot, lax.axis_index("space")]).astype(jnp.int32)
    own = stream[0]
    col_t, val_t, wgt_t = obs_col.T, obs_val.T, obs_weight.T
    vmem = pltpu.VMEM
    tile = vmem((rows, LANES), f32)
    whole = vmem((rows, columns), f32)
    padded = vmem((rows + 16, columns), f32)
    small = (per_row, rows)
    dma = pltpu.SemaphoreType.DMA

    sent, col_tile, wgt_tile, tt, first, last = call(
        observe_kernel,
        [SMEM] + [HBM] * 7,
        (
            shape((GROUP, modes_here * n_modes // LANES + 32, LANES), bf16),
            shape((rows, LANES), jnp.int32),
            shape((rows, LANES), f32),
            shape((n_modes, columns), bf16),
            shape((1, columns), f32),
            shape((1, columns), f32),
        ),
        [vmem(small, jnp.int32), vmem(small, f32), vmem(small, f32),
         vmem((modes_here, n_modes), bf16), whole, vmem((16, columns), f32), tile, tile, dma((8,))],
        "observe",
    )(log_weight, *map(in_hbm, (col_t, val_t, wgt_t, noise_coef[0], own, depth_field, tt_all)))
    sent, held = lax.optimization_barrier((sent, own))
    sent = lax.all_to_all(sent, "particle", 0, 0, axis_index_groups=groups, tiled=True)
    swap = swapped(held, "particle", 0)

    send, miss, part = call(
        gradient_kernel,
        [SMEM, SMEM, VMEM, VMEM, VMEM, VMEM],
        (shape((bands, 8, LANES), bf16), shape((rows + 8, LANES), f32), shape((8, LANES), f32)),
        [whole],
        "gradient",
    )(meta, selection, col_tile, wgt_tile, sent, tt)
    col_modes = lax.all_to_all(send, "space", 0, 0, tiled=True)

    near = jnp.where(selection[0, slot] < 1, own, swap)
    far = swapped(near, "particle", 1)
    col_modes, near = lax.optimization_barrier((col_modes, near))

    send = call(
        spectral_kernel,
        [SMEM, SMEM, VMEM, VMEM, VMEM, VMEM, VMEM, VMEM],
        shape((bands, modes_here + 8, LANES), bf16),
        [],
        "spectral",
    )(meta, selection, col_modes, sent, spectrum, part, tt, ht_all)
    send, first, last = lax.optimization_barrier((send, first, last))
    band_modes = lax.all_to_all(send, "space", 0, 0, tiled=True)
    above = lax.ppermute(last, "space", [(i, i + 1) for i in range(bands - 1)])
    below = lax.ppermute(first, "space", [(i + 1, i) for i in range(bands - 1)])

    field, part = call(
        relax_kernel,
        [SMEM, VMEM, VMEM, VMEM, HBM, VMEM, VMEM, VMEM, VMEM],
        (shape((rows, columns), f32), shape((bands, 1, LANES), f32)),
        [tile, padded, padded, padded, whole, dma(())],
        "relax",
    )(target, col_tile, wgt_tile, miss, in_hbm(depth_field), above, below, band_modes, tt)
    parts = lax.all_to_all(part, "space", 0, 0, tiled=True)
    analysis = field + jnp.where(selection[1, slot] < 1, near, far)
    parts, analysis = lax.optimization_barrier((parts, analysis))
    misfit_out = jnp.sum(parts[:, 0, 0:1], axis=0)
    return analysis[None], misfit_out


def solution(mesh):
    return jax.shard_map(
        per_device,
        mesh=mesh,
        in_specs=(
            P("particle", "space", None),
            P("space", None),
            P("space", None),
            P("space", None),
            P("space", None),
            P("particle"),
            P(),
            P("space", None),
            P("particle", "space", None),
            P(),
        ),
        out_specs=(P("particle", "space", None), P("particle")),
        check_vma=False,
    )
```

```python
import math

import jax
import jax.numpy as jnp
import ml_dtypes
import numpy as np
from jax import lax
from jax.experimental import pallas as pl
from jax.experimental.pallas import tpu as pltpu
from jax.sharding import PartitionSpec as P

STRETCH = 0.05
RELAX_RATE = 0.8
NOISE_AMP = 0.3
LANES = 128
GROUP = 4
VMEM_LIMIT = 48 * 1024 * 1024


def table(extent, half_modes):
    cell = np.arange(extent, dtype=np.int64)[:, None]
    freq = np.arange(half_modes + 1, dtype=np.int64)[None, :]
    angles = (cell * freq % extent).astype(np.float64) * (2.0 * math.pi / extent)
    return np.concatenate([np.cos(angles), np.sin(angles[:, 1:half_modes])], axis=1).astype(
        ml_dtypes.bfloat16
    )


def halo_table(y_table, bands):
    rows = y_table.shape[0]
    width = rows // bands
    out = np.zeros((bands, 2, 4, y_table.shape[1]), dtype=y_table.dtype)
    for band in range(bands):
        for at, row in enumerate((width, width + 1, -2, -1)):
            source = band * width + row
            if 0 <= source < rows:
                out[band, :, at] = y_table[source]
    return out.reshape(bands * 8, y_table.shape[1])


def lane_iota():
    return lax.broadcasted_iota(jnp.int32, (8, LANES), 1)


def summed(values):
    return jnp.sum(jnp.sum(values, axis=0, keepdims=True), axis=1, keepdims=True)


def split3(value):
    high = value.astype(jnp.bfloat16).astype(jnp.float32)
    rest = value - high
    mid = rest.astype(jnp.bfloat16).astype(jnp.float32)
    return high, mid, rest - mid


def source_slot(sel_ref, meta_ref):
    slot = meta_ref[0]
    one = jnp.where(sel_ref[1, slot] < 1, slot, slot ^ 2)
    return jnp.where(sel_ref[0, one] < 1, one, one ^ 1)


def fill_tile(source_ref, scr):
    per_row = source_ref.shape[0]
    scr[...] = jnp.zeros(scr.shape, scr.dtype)
    scr[:, 0:per_row] = source_ref[...].T


def gather_rows(field_ref, col_scr, seen_scr):
    rows, columns = field_ref.shape
    for at in range(0, rows, 8):
        cols = col_scr[at : at + 8, :]
        high, low = cols >> 7, cols & 127
        seen = jnp.zeros((8, LANES), jnp.float32)
        for chunk in range(columns // LANES):
            here = field_ref[at : at + 8, chunk * LANES : (chunk + 1) * LANES]
            got = jnp.take_along_axis(here, low, axis=1, mode="promise_in_bounds")
            seen = jnp.where(high == chunk, got, seen)
        seen_scr[at : at + 8, :] = seen


def packed(tile, per_row):
    lane = lane_iota()
    out = tile[0:8, :]
    for group in range(1, tile.shape[0] // 8):
        rolled = pltpu.roll(tile[group * 8 : group * 8 + 8, :], group * per_row, axis=1)
        out = jnp.where(lane // per_row == group, rolled, out)
    return out


def observe_kernel(
    lw_ref, col_hbm, val_hbm, wgt_hbm, noise_hbm, stream_hbm, depth_hbm, tt_hbm,
    out_ref, col_scr, wgt_scr, tt_ref, first_ref, last_ref,
    col_ref, val_ref, wgt_ref, noise_ref, stream_ref, depth_ref, val_scr, seen_scr, sems,
):
    rows = depth_hbm.shape[0]
    pairs = (
        (col_hbm, col_ref),
        (val_hbm, val_ref),
        (stream_hbm, stream_ref),
        (noise_hbm, noise_ref),
        (wgt_hbm, wgt_ref),
        (depth_hbm.at[0:8, :], depth_ref.at[0:8, :]),
        (depth_hbm.at[rows - 8 : rows, :], depth_ref.at[8:16, :]),
        (tt_hbm, tt_ref),
    )
    loads = [pltpu.make_async_copy(a, b, sems.at[at]) for at, (a, b) in enumerate(pairs)]
    for load in loads:
        load.start()
    per_row = col_ref.shape[0]
    modes_here, n_modes = noise_ref.shape
    loads[0].wait()
    loads[1].wait()
    fill_tile(col_ref, col_scr)
    fill_tile(val_ref, val_scr)
    loads[2].wait()
    gather_rows(stream_ref, col_scr, seen_scr)
    mismatch = packed(val_scr[...] - seen_scr[...], per_row)
    weight = jnp.full((8, LANES), lw_ref[0], jnp.float32)
    row = lax.broadcasted_iota(jnp.int32, (8, LANES), 0)
    high, mid, low = split3(weight)
    weight = jnp.where(row == 0, high, jnp.where(row == 1, mid, jnp.where(row == 2, low, 0.0)))
    values = jnp.concatenate(list(split3(mismatch)) + [weight], axis=0).astype(jnp.bfloat16)
    loads[4].wait()
    fill_tile(wgt_ref, wgt_scr)
    loads[3].wait()
    noise = noise_ref[...]
    chunks = n_modes // LANES
    for peer in range(GROUP):
        for chunk in range(chunks):
            out_ref[peer, chunk * modes_here : (chunk + 1) * modes_here, :] = noise[
                :, chunk * LANES : (chunk + 1) * LANES
            ]
        out_ref[peer, chunks * modes_here :, :] = values
    loads[5].wait()
    loads[6].wait()
    first_ref[...] = depth_ref[0:1, :]
    last_ref[...] = depth_ref[15:16, :]
    loads[7].wait()


def gradient_kernel(
    meta_ref, sel_ref, col_scr, wgt_scr, seen_ref, tt_ref, send_ref, miss_ref, part_ref, grad_scr,
):
    rows = grad_scr.shape[0]
    per_row = LANES * 8 // rows
    columns = tt_ref.shape[1]
    position = source_slot(sel_ref, meta_ref) & (GROUP - 1)
    first = seen_ref.shape[1] - 32
    sent = seen_ref[position][first:, :].astype(jnp.float32)
    mismatch = sent[0:8] + sent[8:16] + sent[16:24]
    weight = sent[24:25] + sent[25:26] + sent[26:27]
    miss_ref[rows:, :] = jnp.broadcast_to(weight, (8, LANES))
    tiles = [mismatch] + [
        pltpu.roll(mismatch, LANES - group * per_row, axis=1) for group in range(1, rows // 8)
    ]
    mismatch = jnp.concatenate(tiles, axis=0)
    miss_ref[0:rows, :] = mismatch
    weighted = wgt_scr[...] * mismatch
    part_ref[...] = jnp.broadcast_to(0.5 * summed(weighted * mismatch), (8, LANES))

    def repeated(tile):
        step = per_row
        while step < LANES:
            tile = tile + pltpu.roll(tile, step, axis=1)
            step *= 2
        return tile

    diagonal = lane_iota() // per_row == lax.broadcasted_iota(jnp.int32, (8, LANES), 0)
    row_f = lax.broadcasted_iota(jnp.int32, (LANES, LANES), 0).astype(jnp.float32)
    for group in range(rows // 8):
        at = group * 8
        cols = repeated(col_scr[at : at + 8, :])
        high = jnp.where(diagonal, cols >> 7, -1)
        low = jnp.sum(
            jnp.where(diagonal, (cols & 127).astype(jnp.float32), 0.0), axis=0, keepdims=True
        )
        one_hot = jnp.where(row_f == low, 1.0, 0.0).astype(jnp.bfloat16)
        left = []
        for piece in split3(repeated(weighted[at : at + 8, :])):
            left.append(
                jnp.concatenate(
                    [jnp.where(high == chunk, piece, 0.0) for chunk in range(columns // LANES)], axis=0
                ).astype(jnp.bfloat16)
            )
        spread = lax.dot_general(
            jnp.concatenate(left, axis=1),
            jnp.concatenate([one_hot] * 3, axis=1),
            (((1,), (1,)), ((), ())),
            preferred_element_type=jnp.float32,
        )
        for chunk in range(columns // LANES):
            grad_scr[at : at + 8, chunk * LANES : (chunk + 1) * LANES] = spread[
                chunk * 8 : chunk * 8 + 8, :
            ]
    gradient = grad_scr[...].astype(jnp.bfloat16)
    modes = lax.dot_general(
        tt_ref[...], gradient, (((1,), (1,)), ((), ())), preferred_element_type=jnp.float32
    )
    bands = send_ref.shape[0]
    split = modes.reshape(bands, 2, 8, rows)
    send_ref[...] = jnp.concatenate([split[:, 0], split[:, 1]], axis=2).astype(jnp.bfloat16)


def spectral_kernel(
    meta_ref, sel_ref, modes_ref, noise_ref, spec_ref, part_ref, tt_ref, ht_ref, send_ref,
):
    bands = modes_ref.shape[0]
    half = LANES // 2
    modes_here, n_modes = spec_ref.shape
    rows = tt_ref.shape[1]
    norm_factor = 4.0 / (rows * rows)
    position = source_slot(sel_ref, meta_ref) & (GROUP - 1)
    me = meta_ref[1] & 7
    lane = lane_iota()
    low = lane < half
    tops, bottoms = [], []
    for pair in range(bands // 2):
        even = modes_ref[2 * pair].astype(jnp.float32)
        odd = modes_ref[2 * pair + 1].astype(jnp.float32)
        tops.append(jnp.where(low, even, pltpu.roll(odd, half, axis=1)))
        bottoms.append(jnp.where(low, pltpu.roll(even, half, axis=1), odd))
    columns = jnp.concatenate(
        [jnp.concatenate(tops, axis=1), jnp.concatenate(bottoms, axis=1)], axis=0
    ).astype(jnp.bfloat16)
    coefficients = lax.dot_general(
        columns, tt_ref[...], (((1,), (1,)), ((), ())), preferred_element_type=jnp.float32
    )
    scaled = norm_factor * spec_ref[...]
    weighted = coefficients * scaled
    energy = summed(coefficients * weighted)
    noise = noise_ref[position][0 : noise_ref.shape[1] - 32, :]
    noise = jnp.concatenate(
        [noise[at : at + modes_here] for at in range(0, noise.shape[0], modes_here)], axis=1
    )
    shaped = (jnp.sqrt(scaled) * noise.astype(jnp.float32)).astype(jnp.bfloat16)
    weighted = weighted.astype(jnp.bfloat16)
    stacked = jnp.concatenate([weighted, shaped], axis=0)
    inverted = jnp.dot(stacked, tt_ref[...], preferred_element_type=jnp.float32)
    low16 = lax.broadcasted_iota(jnp.int32, (modes_here, LANES), 1) < half
    for pair in range(bands // 2):
        first = inverted[0:modes_here, pair * LANES : (pair + 1) * LANES]
        second = inverted[modes_here:, pair * LANES : (pair + 1) * LANES]
        send_ref[2 * pair, 0:modes_here, :] = jnp.where(
            low16, first, pltpu.roll(second, half, axis=1)
        ).astype(jnp.bfloat16)
        send_ref[2 * pair + 1, 0:modes_here, :] = jnp.where(
            low16, pltpu.roll(first, half, axis=1), second
        ).astype(jnp.bfloat16)
    halo = lax.dot_general(
        ht_ref[...], stacked, (((1,), (1,)), ((), ())), preferred_element_type=jnp.float32
    )
    halo = halo.reshape(bands, 8, 2 * modes_here)
    row8 = lax.broadcasted_iota(jnp.int32, (bands, 8, LANES), 1)
    lane8 = lax.broadcasted_iota(jnp.int32, (bands, 8, LANES), 2)
    wide = jnp.concatenate([halo, jnp.zeros((bands, 8, LANES - 2 * modes_here), jnp.float32)], axis=2)
    wide = wide.reshape(bands * 8, LANES)
    at = me * modes_here
    as_first = pltpu.roll(wide, at, axis=1).reshape(bands, 8, LANES)
    as_second = pltpu.roll(wide, (at + LANES - modes_here) % LANES, axis=1).reshape(bands, 8, LANES)
    placed = jnp.where(row8 < 4, as_first, as_second)
    pieces = jnp.zeros((8, LANES), jnp.float32)
    row = lax.broadcasted_iota(jnp.int32, (8, LANES), 0)
    energy = jnp.broadcast_to(energy, (8, LANES))
    for at_row, piece in enumerate(split3(part_ref[...]) + split3(energy)):
        pieces = jnp.where(row == at_row, piece, pieces)
    pieces = jnp.broadcast_to(pieces[None], (bands, 8, LANES))
    mine = lane8 // modes_here == me
    scalar_at = lane8 == ((me + 1) % 8) * modes_here
    tail = jnp.where(mine, placed, jnp.where(scalar_at, pieces, 0.0))
    send_ref[:, modes_here:, :] = tail.astype(jnp.bfloat16)


def relax_kernel(
    target_ref, col_scr, wgt_scr, miss_ref, depth_hbm, above_ref, below_ref, modes_ref, tt_ref,
    field_ref, part_ref, seen_scr, inc_scr, one_scr, rate_ref, depth_ref, sem,
):
    depth = pltpu.make_async_copy(depth_hbm, depth_ref, sem)
    depth.start()
    rows = depth_ref.shape[0]

    def rate(depth):
        return RELAX_RATE * depth / (4.0 * depth + STRETCH)

    bands, _, _ = modes_ref.shape
    n_modes, columns = tt_ref.shape
    modes_here = n_modes // bands
    lane = lane_iota()
    quads, scalars = [], jnp.zeros((8, LANES), jnp.float32)
    for quad in range(bands // 8):
        total = jnp.zeros((8, LANES), jnp.float32)
        for at in range(8):
            tail = modes_ref[quad * 8 + at, modes_here:, :].astype(jnp.float32)
            window = lane // modes_here
            total = jnp.where(window == at, tail, total)
            scalars = scalars + jnp.where(window == (at + 1) % 8, tail, 0.0)
        quads.append(total)
    halo = jnp.concatenate(quads, axis=1)
    row = lax.broadcasted_iota(jnp.int32, (8, LANES), 0)
    misfit = summed(jnp.where(row < 3, scalars, 0.0))
    energy = summed(jnp.where((row >= 3) & (row < 6), scalars, 0.0))
    weight = miss_ref[rows : rows + 1, 0:1]
    step = (misfit + weight - target_ref[0]) / (energy + 1.0)
    main = modes_ref[:, 0:modes_here, :].reshape(n_modes, LANES)
    pulled = lax.dot_general(main, tt_ref[...], (((0,), (0,)), ((), ())), preferred_element_type=jnp.float32)
    pulled_h = jnp.dot(halo.astype(jnp.bfloat16), tt_ref[...], preferred_element_type=jnp.float32)
    for at in range(0, rows, 8):
        inc_scr[at : at + 8, :] = step * pulled[at : at + 8] + NOISE_AMP * pulled[rows + at : rows + at + 8]
    edge = pulled_h
    edge = step * edge + NOISE_AMP * pltpu.roll(edge, 4, axis=0)
    row8 = lax.broadcasted_iota(jnp.int32, (8, columns), 0)
    inc_scr[rows:, :] = jnp.where(row8 < 2, edge, jnp.where(row8 < 6, 0.0, pltpu.roll(edge, 4, axis=0)))
    depth.wait()

    def rate(depth):
        return RELAX_RATE * depth / (4.0 * depth + STRETCH)

    rate_ref[rows:, :] = jnp.where(
        row8 == 0, rate(below_ref[...]), jnp.where(row8 == 7, rate(above_ref[...]), 0.0)
    )
    for at in range(0, rows, 8):
        rate_ref[at : at + 8, :] = rate(depth_ref[at : at + 8, :])
    length = rows + 8

    def relaxed(source_ref, at):
        here = source_ref[at : at + 8, :]
        before = source_ref[(at - 8) % length : (at - 8) % length + 8, :]
        after = source_ref[(at + 8) % length : (at + 8) % length + 8, :]
        around = (
            pltpu.roll(jnp.where(row8 == 7, before, here), 1, axis=0)
            + pltpu.roll(jnp.where(row8 == 0, after, here), 7, axis=0)
            + pltpu.roll(here, 1, axis=1)
            + pltpu.roll(here, columns - 1, axis=1)
        )
        return (1.0 - RELAX_RATE) * here + rate_ref[at : at + 8, :] * (
            around - inc_scr[at : at + 8, :]
        )

    for at in range(0, length, 8):
        one_scr[at : at + 8, :] = relaxed(inc_scr, at)
    for at in range(0, rows, 8):
        field_ref[at : at + 8, :] = relaxed(one_scr, at)
    gather_rows(field_ref, col_scr, seen_scr)
    left_over = miss_ref[0:rows, :] - seen_scr[...]
    part = 0.5 * summed(wgt_scr[...] * left_over * left_over)
    part_ref[...] = jnp.broadcast_to(part[None], part_ref.shape)


SMEM = pl.BlockSpec(memory_space=pltpu.SMEM)
VMEM = pl.BlockSpec(memory_space=pltpu.VMEM)
HBM = pl.BlockSpec(memory_space=pltpu.HBM)


COST = {"observe": 40, "gradient": 40, "spectral": 1, "relax": 1}


def call(kernel, in_specs, out_shape, scratch, name, out_specs=None):
    return pl.pallas_call(
        kernel,
        in_specs=in_specs,
        out_specs=out_specs or jax.tree.map(lambda _: VMEM, out_shape),
        out_shape=out_shape,
        scratch_shapes=scratch,
        name=name,
        cost_estimate=pl.CostEstimate(
            flops=COST[name] * 10**9, transcendentals=0, bytes_accessed=4 * 10**6
        ),
        compiler_params=pltpu.CompilerParams(vmem_limit_bytes=VMEM_LIMIT),
    )


def in_hbm(value):
    return pltpu.with_memory_space_constraint(value, pltpu.HBM)


def swapped(value, axis, bit):
    mask = 2**bit
    pairs = [(source, source ^ mask) for source in range(lax.axis_size(axis))]
    return lax.ppermute(value, axis, pairs)


def per_device(
    stream, depth_field, obs_col, obs_val, obs_weight, log_weight, target, spectrum, noise_coef,
    selection,
):
    _, rows, columns = stream.shape
    per_row = obs_col.shape[1]
    modes_here, n_modes = spectrum.shape
    bands = lax.axis_size("space")
    particles = lax.axis_size("particle")
    y_table = table(rows * bands, n_modes // 2)
    tt_all = jnp.asarray(np.ascontiguousarray(y_table.T))
    ht_all = jnp.asarray(halo_table(y_table, bands))
    f32, bf16 = jnp.float32, jnp.bfloat16
    shape = jax.ShapeDtypeStruct
    groups = [[g * GROUP + i for i in range(GROUP)] for g in range(particles // GROUP)]
    slot = lax.axis_index("particle")
    meta = jnp.stack([slot, lax.axis_index("space")]).astype(jnp.int32)
    own = stream[0]
    col_t, val_t, wgt_t = obs_col.T, obs_val.T, obs_weight.T
    vmem = pltpu.VMEM
    tile = vmem((rows, LANES), f32)
    whole = vmem((rows, columns), f32)
    padded = vmem((rows + 8, columns), f32)
    small = (per_row, rows)
    dma = pltpu.SemaphoreType.DMA

    sent, col_tile, wgt_tile, tt, first, last = call(
        observe_kernel,
        [SMEM] + [HBM] * 7,
        (
            shape((GROUP, modes_here * n_modes // LANES + 32, LANES), bf16),
            shape((rows, LANES), jnp.int32),
            shape((rows, LANES), f32),
            shape((n_modes, columns), bf16),
            shape((1, columns), f32),
            shape((1, columns), f32),
        ),
        [vmem(small, jnp.int32), vmem(small, f32), vmem(small, f32),
         vmem((modes_here, n_modes), bf16), whole, vmem((16, columns), f32), tile, tile, dma((8,))],
        "observe",
    )(log_weight, *map(in_hbm, (col_t, val_t, wgt_t, noise_coef[0], own, depth_field, tt_all)))
    sent, held = lax.optimization_barrier((sent, own))
    sent = lax.all_to_all(sent, "particle", 0, 0, axis_index_groups=groups, tiled=True)
    swap = swapped(held, "particle", 0)

    send, miss, part = call(
        gradient_kernel,
        [SMEM, SMEM, VMEM, VMEM, VMEM, VMEM],
        (shape((bands, 8, LANES), bf16), shape((rows + 8, LANES), f32), shape((8, LANES), f32)),
        [whole],
        "gradient",
    )(meta, selection, col_tile, wgt_tile, sent, tt)
    col_modes = lax.all_to_all(send, "space", 0, 0, tiled=True)

    near = jnp.where(selection[0, slot] < 1, own, swap)
    far = swapped(near, "particle", 1)
    col_modes, near = lax.optimization_barrier((col_modes, near))

    send = call(
        spectral_kernel,
        [SMEM, SMEM, VMEM, VMEM, VMEM, VMEM, VMEM, VMEM],
        shape((bands, modes_here + 8, LANES), bf16),
        [],
        "spectral",
    )(meta, selection, col_modes, sent, spectrum, part, tt, ht_all)
    send, first, last = lax.optimization_barrier((send, first, last))
    band_modes = lax.all_to_all(send, "space", 0, 0, tiled=True)
    above = lax.ppermute(last, "space", [(i, i + 1) for i in range(bands - 1)])
    below = lax.ppermute(first, "space", [(i + 1, i) for i in range(bands - 1)])

    field, part = call(
        relax_kernel,
        [SMEM, VMEM, VMEM, VMEM, HBM, VMEM, VMEM, VMEM, VMEM],
        (shape((rows, columns), f32), shape((bands, 1, LANES), f32)),
        [tile, padded, padded, padded, whole, dma(())],
        "relax",
    )(target, col_tile, wgt_tile, miss, in_hbm(depth_field), above, below, band_modes, tt)
    parts = lax.all_to_all(part, "space", 0, 0, tiled=True)
    analysis = field + jnp.where(selection[1, slot] < 1, near, far)
    parts, analysis = lax.optimization_barrier((parts, analysis))
    misfit_out = jnp.sum(parts[:, 0, 0:1], axis=0)
    return analysis[None], misfit_out


def solution(mesh):
    return jax.shard_map(
        per_device,
        mesh=mesh,
        in_specs=(
            P("particle", "space", None),
            P("space", None),
            P("space", None),
            P("space", None),
            P("space", None),
            P("particle"),
            P(),
            P("space", None),
            P("particle", "space", None),
            P(),
        ),
        out_specs=(P("particle", "space", None), P("particle")),
        check_vma=False,
    )
```

```python
import math

import jax
import jax.numpy as jnp
import ml_dtypes
import numpy as np
from jax import lax
from jax.experimental import pallas as pl
from jax.experimental.pallas import tpu as pltpu
from jax.sharding import PartitionSpec as P

STRETCH = 0.05
RELAX_RATE = 0.8
NOISE_AMP = 0.3
LANES = 128
GROUP = 4
VMEM_LIMIT = 48 * 1024 * 1024


def table(extent, half_modes):
    cell = np.arange(extent, dtype=np.int64)[:, None]
    freq = np.arange(half_modes + 1, dtype=np.int64)[None, :]
    angles = (cell * freq % extent).astype(np.float64) * (2.0 * math.pi / extent)
    return np.concatenate([np.cos(angles), np.sin(angles[:, 1:half_modes])], axis=1).astype(
        ml_dtypes.bfloat16
    )


def halo_table(y_table, bands):
    rows = y_table.shape[0]
    width = rows // bands
    out = np.zeros((4, bands, y_table.shape[1]), dtype=y_table.dtype)
    for band in range(bands):
        for at, row in enumerate((width, width + 1, -2, -1)):
            source = band * width + row
            if 0 <= source < rows:
                out[at, band] = y_table[source]
    return out.reshape(bands * 4, y_table.shape[1])


def lane_iota():
    return lax.broadcasted_iota(jnp.int32, (8, LANES), 1)


def summed(values):
    return jnp.sum(jnp.sum(values, axis=0, keepdims=True), axis=1, keepdims=True)


def split3(value):
    high = value.astype(jnp.bfloat16).astype(jnp.float32)
    rest = value - high
    mid = rest.astype(jnp.bfloat16).astype(jnp.float32)
    return high, mid, rest - mid


def source_slot(sel_ref, meta_ref):
    slot = meta_ref[0]
    one = jnp.where(sel_ref[1, slot] < 1, slot, slot ^ 2)
    return jnp.where(sel_ref[0, one] < 1, one, one ^ 1)


def fill_tile(source_ref, scr):
    per_row = source_ref.shape[0]
    scr[...] = jnp.zeros(scr.shape, scr.dtype)
    scr[:, 0:per_row] = source_ref[...].T


def gather_rows(field_ref, col_scr, seen_scr):
    rows, columns = field_ref.shape
    for at in range(0, rows, 8):
        cols = col_scr[at : at + 8, :]
        high, low = cols >> 7, cols & 127
        seen = jnp.zeros((8, LANES), jnp.float32)
        for chunk in range(columns // LANES):
            here = field_ref[at : at + 8, chunk * LANES : (chunk + 1) * LANES]
            got = jnp.take_along_axis(here, low, axis=1, mode="promise_in_bounds")
            seen = jnp.where(high == chunk, got, seen)
        seen_scr[at : at + 8, :] = seen


def packed(tile, per_row):
    lane = lane_iota()
    out = tile[0:8, :]
    for group in range(1, tile.shape[0] // 8):
        rolled = pltpu.roll(tile[group * 8 : group * 8 + 8, :], group * per_row, axis=1)
        out = jnp.where(lane // per_row == group, rolled, out)
    return out


def observe_kernel(
    lw_ref, col_hbm, val_hbm, wgt_hbm, noise_hbm, stream_hbm, depth_hbm, tt_hbm,
    out_ref, col_scr, wgt_scr, tt_ref, first_ref, last_ref,
    col_ref, val_ref, wgt_ref, noise_ref, stream_ref, depth_ref, val_scr, seen_scr, sems,
):
    rows = depth_hbm.shape[0]
    pairs = (
        (col_hbm, col_ref),
        (val_hbm, val_ref),
        (stream_hbm, stream_ref),
        (noise_hbm, noise_ref),
        (wgt_hbm, wgt_ref),
        (depth_hbm.at[0:8, :], depth_ref.at[0:8, :]),
        (depth_hbm.at[rows - 8 : rows, :], depth_ref.at[8:16, :]),
        (tt_hbm, tt_ref),
    )
    loads = [pltpu.make_async_copy(a, b, sems.at[at]) for at, (a, b) in enumerate(pairs)]
    for load in loads:
        load.start()
    per_row = col_ref.shape[0]
    modes_here, n_modes = noise_ref.shape
    loads[0].wait()
    loads[1].wait()
    fill_tile(col_ref, col_scr)
    fill_tile(val_ref, val_scr)
    loads[2].wait()
    gather_rows(stream_ref, col_scr, seen_scr)
    mismatch = packed(val_scr[...] - seen_scr[...], per_row)
    weight = jnp.full((8, LANES), lw_ref[0], jnp.float32)
    row = lax.broadcasted_iota(jnp.int32, (8, LANES), 0)
    high, mid, low = split3(weight)
    weight = jnp.where(row == 0, high, jnp.where(row == 1, mid, jnp.where(row == 2, low, 0.0)))
    values = jnp.concatenate(list(split3(mismatch)) + [weight], axis=0).astype(jnp.bfloat16)
    loads[4].wait()
    fill_tile(wgt_ref, wgt_scr)
    loads[3].wait()
    noise = noise_ref[...]
    chunks = n_modes // LANES
    for peer in range(GROUP):
        for chunk in range(chunks):
            out_ref[peer, chunk * modes_here : (chunk + 1) * modes_here, :] = noise[
                :, chunk * LANES : (chunk + 1) * LANES
            ]
        out_ref[peer, chunks * modes_here :, :] = values
    loads[5].wait()
    loads[6].wait()
    first_ref[...] = depth_ref[0:1, :]
    last_ref[...] = depth_ref[15:16, :]
    loads[7].wait()


def gradient_kernel(
    meta_ref, sel_ref, col_scr, wgt_scr, seen_ref, tt_ref, send_ref, miss_ref, part_ref, grad_scr,
):
    rows = grad_scr.shape[0]
    per_row = LANES * 8 // rows
    columns = tt_ref.shape[1]
    position = source_slot(sel_ref, meta_ref) & (GROUP - 1)
    first = seen_ref.shape[1] - 32
    sent = seen_ref[position][first:, :].astype(jnp.float32)
    mismatch = sent[0:8] + sent[8:16] + sent[16:24]
    weight = sent[24:25] + sent[25:26] + sent[26:27]
    miss_ref[rows:, :] = jnp.broadcast_to(weight, (8, LANES))
    tiles = [mismatch] + [
        pltpu.roll(mismatch, LANES - group * per_row, axis=1) for group in range(1, rows // 8)
    ]
    mismatch = jnp.concatenate(tiles, axis=0)
    miss_ref[0:rows, :] = mismatch
    weighted = wgt_scr[...] * mismatch
    part_ref[...] = jnp.broadcast_to(0.5 * summed(weighted * mismatch), (8, LANES))

    def repeated(tile):
        step = per_row
        while step < LANES:
            tile = tile + pltpu.roll(tile, step, axis=1)
            step *= 2
        return tile

    diagonal = lane_iota() // per_row == lax.broadcasted_iota(jnp.int32, (8, LANES), 0)
    row_f = lax.broadcasted_iota(jnp.int32, (LANES, LANES), 0).astype(jnp.float32)
    for group in range(rows // 8):
        at = group * 8
        cols = repeated(col_scr[at : at + 8, :])
        high = jnp.where(diagonal, cols >> 7, -1)
        low = jnp.sum(
            jnp.where(diagonal, (cols & 127).astype(jnp.float32), 0.0), axis=0, keepdims=True
        )
        one_hot = jnp.where(row_f == low, 1.0, 0.0).astype(jnp.bfloat16)
        left = []
        for piece in split3(repeated(weighted[at : at + 8, :])):
            left.append(
                jnp.concatenate(
                    [jnp.where(high == chunk, piece, 0.0) for chunk in range(columns // LANES)], axis=0
                ).astype(jnp.bfloat16)
            )
        spread = lax.dot_general(
            jnp.concatenate(left, axis=1),
            jnp.concatenate([one_hot] * 3, axis=1),
            (((1,), (1,)), ((), ())),
            preferred_element_type=jnp.float32,
        )
        for chunk in range(columns // LANES):
            grad_scr[at : at + 8, chunk * LANES : (chunk + 1) * LANES] = spread[
                chunk * 8 : chunk * 8 + 8, :
            ]
    gradient = grad_scr[...].astype(jnp.bfloat16)
    modes = lax.dot_general(
        tt_ref[...], gradient, (((1,), (1,)), ((), ())), preferred_element_type=jnp.float32
    )
    bands = send_ref.shape[0]
    split = modes.reshape(bands, 2, 8, rows)
    send_ref[...] = jnp.concatenate([split[:, 0], split[:, 1]], axis=2).astype(jnp.bfloat16)


def spectral_kernel(
    meta_ref, sel_ref, modes_ref, noise_ref, spec_ref, part_ref, tt_ref, ht_ref, send_ref, pack_scr,
):
    bands = modes_ref.shape[0]
    half = LANES // 2
    modes_here, n_modes = spec_ref.shape
    rows = tt_ref.shape[1]
    norm_factor = 4.0 / (rows * rows)
    position = source_slot(sel_ref, meta_ref) & (GROUP - 1)
    lane = lane_iota()
    low = lane < half
    tops, bottoms = [], []
    for pair in range(bands // 2):
        even = modes_ref[2 * pair].astype(jnp.float32)
        odd = modes_ref[2 * pair + 1].astype(jnp.float32)
        tops.append(jnp.where(low, even, pltpu.roll(odd, half, axis=1)))
        bottoms.append(jnp.where(low, pltpu.roll(even, half, axis=1), odd))
    columns = jnp.concatenate(
        [jnp.concatenate(tops, axis=1), jnp.concatenate(bottoms, axis=1)], axis=0
    ).astype(jnp.bfloat16)
    coefficients = lax.dot_general(
        columns, tt_ref[...], (((1,), (1,)), ((), ())), preferred_element_type=jnp.float32
    )
    scaled = norm_factor * spec_ref[...]
    weighted = coefficients * scaled
    energy = summed(coefficients * weighted)
    noise = noise_ref[position][0 : noise_ref.shape[1] - 32, :]
    noise = jnp.concatenate(
        [noise[at : at + modes_here] for at in range(0, noise.shape[0], modes_here)], axis=1
    )
    shaped = (jnp.sqrt(scaled) * noise.astype(jnp.float32)).astype(jnp.bfloat16)
    weighted = weighted.astype(jnp.bfloat16)
    stacked = jnp.concatenate([weighted, shaped], axis=0)
    inverted = jnp.dot(stacked, tt_ref[...], preferred_element_type=jnp.float32)
    block = modes_here + 2
    low16 = lax.broadcasted_iota(jnp.int32, (modes_here, LANES), 1) < half
    for pair in range(bands // 2):
        first = inverted[0:modes_here, pair * LANES : (pair + 1) * LANES]
        second = inverted[modes_here:, pair * LANES : (pair + 1) * LANES]
        at = 2 * pair * block
        pack_scr[at : at + modes_here, :] = jnp.where(
            low16, first, pltpu.roll(second, half, axis=1)
        )
        at += block
        pack_scr[at : at + modes_here, :] = jnp.where(
            low16, pltpu.roll(first, half, axis=1), second
        )
    halo = lax.dot_general(
        ht_ref[...], stacked, (((1,), (1,)), ((), ())), preferred_element_type=jnp.float32
    )
    halo = jnp.concatenate(
        [halo, jnp.zeros((4 * bands, LANES - 2 * modes_here), jnp.float32)], axis=1
    )
    window = lax.broadcasted_iota(jnp.int32, (bands, LANES), 1) // modes_here
    edges = jnp.zeros((bands, LANES), jnp.float32)
    for at in range(8):
        field, row = at // 4, at % 4
        shift = (at - field) * modes_here % LANES
        value = halo[row * bands : (row + 1) * bands]
        edges = jnp.where(window == at, pltpu.roll(value, shift, axis=1) if shift else value, edges)
    lane1 = lax.broadcasted_iota(jnp.int32, (1, LANES), 1)
    pieces = jnp.zeros((1, LANES), jnp.float32)
    for at, piece in enumerate(split3(part_ref[0:1, 0:1]) + split3(energy)):
        pieces = jnp.where(lane1 == at, piece, pieces)
    for band in range(bands):
        at = band * block + modes_here
        pack_scr[at : at + 1, :] = edges[band : band + 1]
        pack_scr[at + 1 : at + 2, :] = pieces
    send_ref[...] = pack_scr[...].astype(jnp.bfloat16)


def relax_kernel(
    target_ref, col_scr, wgt_scr, miss_ref, depth_hbm, above_ref, below_ref, modes_ref, tt_ref,
    field_ref, part_ref, unpack_scr, seen_scr, inc_scr, one_scr, rate_ref, depth_ref,
    sem,
):
    depth = pltpu.make_async_copy(depth_hbm, depth_ref, sem)
    depth.start()
    rows = depth_ref.shape[0]

    def rate(depth):
        return RELAX_RATE * depth / (4.0 * depth + STRETCH)

    n_modes, columns = tt_ref.shape
    bands = part_ref.shape[0]
    modes_here = n_modes // bands
    lane = lane_iota()
    block = modes_here + 2
    unpack_scr[...] = modes_ref[...].astype(jnp.float32)
    edges = unpack_scr[pl.ds(modes_here, bands, stride=block), :]
    scalars = unpack_scr[pl.ds(modes_here + 1, bands, stride=block), :]
    row = lax.broadcasted_iota(jnp.int32, (8, LANES), 0)
    window = lane // modes_here
    quads = []
    for quad in range(0, bands, 8):
        tile = edges[quad : quad + 8]
        for bit in (1, 2, 4):
            up = pltpu.roll(pltpu.roll(tile, 8 - bit, axis=0), bit * modes_here, axis=1)
            down = pltpu.roll(pltpu.roll(tile, bit, axis=0), LANES - bit * modes_here, axis=1)
            upper, later = (row & bit) == 0, (window & bit) == 0
            tile = jnp.where(upper == later, tile, jnp.where(upper, up, down))
        quads.append(tile)
    halo = jnp.concatenate(quads, axis=1)
    lanes = lax.broadcasted_iota(jnp.int32, scalars.shape, 1)
    misfit = summed(jnp.where(lanes < 3, scalars, 0.0))
    energy = summed(jnp.where((lanes >= 3) & (lanes < 6), scalars, 0.0))
    weight = miss_ref[rows : rows + 1, 0:1]
    step = (misfit + weight - target_ref[0]) / (energy + 1.0)
    main = jnp.concatenate(
        [unpack_scr[at * block : at * block + modes_here, :] for at in range(bands)], axis=0
    ).astype(jnp.bfloat16)
    pulled = lax.dot_general(main, tt_ref[...], (((0,), (0,)), ((), ())), preferred_element_type=jnp.float32)
    pulled_h = jnp.dot(halo.astype(jnp.bfloat16), tt_ref[...], preferred_element_type=jnp.float32)
    for at in range(0, rows, 8):
        inc_scr[at : at + 8, :] = step * pulled[at : at + 8] + NOISE_AMP * pulled[rows + at : rows + at + 8]
    edge = pulled_h
    edge = step * edge + NOISE_AMP * pltpu.roll(edge, 4, axis=0)
    row8 = lax.broadcasted_iota(jnp.int32, (8, columns), 0)
    inc_scr[rows:, :] = jnp.where(row8 < 2, edge, jnp.where(row8 < 6, 0.0, pltpu.roll(edge, 4, axis=0)))
    depth.wait()

    def rate(depth):
        return RELAX_RATE * depth / (4.0 * depth + STRETCH)

    rate_ref[rows:, :] = jnp.where(
        row8 == 0, rate(below_ref[...]), jnp.where(row8 == 7, rate(above_ref[...]), 0.0)
    )
    for at in range(0, rows, 8):
        rate_ref[at : at + 8, :] = rate(depth_ref[at : at + 8, :])
    length = rows + 8

    def relaxed(source_ref, at):
        here = source_ref[at : at + 8, :]
        before = source_ref[(at - 8) % length : (at - 8) % length + 8, :]
        after = source_ref[(at + 8) % length : (at + 8) % length + 8, :]
        around = (
            pltpu.roll(jnp.where(row8 == 7, before, here), 1, axis=0)
            + pltpu.roll(jnp.where(row8 == 0, after, here), 7, axis=0)
            + pltpu.roll(here, 1, axis=1)
            + pltpu.roll(here, columns - 1, axis=1)
        )
        return (1.0 - RELAX_RATE) * here + rate_ref[at : at + 8, :] * (
            around - inc_scr[at : at + 8, :]
        )

    for at in range(0, length, 8):
        one_scr[at : at + 8, :] = relaxed(inc_scr, at)
    for at in range(0, rows, 8):
        field_ref[at : at + 8, :] = relaxed(one_scr, at)
    gather_rows(field_ref, col_scr, seen_scr)
    left_over = miss_ref[0:rows, :] - seen_scr[...]
    part = 0.5 * summed(wgt_scr[...] * left_over * left_over)
    part_ref[...] = jnp.broadcast_to(part[None], part_ref.shape)


SMEM = pl.BlockSpec(memory_space=pltpu.SMEM)
VMEM = pl.BlockSpec(memory_space=pltpu.VMEM)
HBM = pl.BlockSpec(memory_space=pltpu.HBM)


COST = {"observe": 40, "gradient": 40, "spectral": 1, "relax": 1}


def call(kernel, in_specs, out_shape, scratch, name, out_specs=None):
    return pl.pallas_call(
        kernel,
        in_specs=in_specs,
        out_specs=out_specs or jax.tree.map(lambda _: VMEM, out_shape),
        out_shape=out_shape,
        scratch_shapes=scratch,
        name=name,
        cost_estimate=pl.CostEstimate(
            flops=COST[name] * 10**9, transcendentals=0, bytes_accessed=4 * 10**6
        ),
        compiler_params=pltpu.CompilerParams(vmem_limit_bytes=VMEM_LIMIT),
    )


def in_hbm(value):
    return pltpu.with_memory_space_constraint(value, pltpu.HBM)


def swapped(value, axis, bit):
    mask = 2**bit
    pairs = [(source, source ^ mask) for source in range(lax.axis_size(axis))]
    return lax.ppermute(value, axis, pairs)


def per_device(
    stream, depth_field, obs_col, obs_val, obs_weight, log_weight, target, spectrum, noise_coef,
    selection,
):
    _, rows, columns = stream.shape
    per_row = obs_col.shape[1]
    modes_here, n_modes = spectrum.shape
    bands = lax.axis_size("space")
    particles = lax.axis_size("particle")
    y_table = table(rows * bands, n_modes // 2)
    tt_all = jnp.asarray(np.ascontiguousarray(y_table.T))
    ht_all = jnp.asarray(halo_table(y_table, bands))
    f32, bf16 = jnp.float32, jnp.bfloat16
    shape = jax.ShapeDtypeStruct
    groups = [[g * GROUP + i for i in range(GROUP)] for g in range(particles // GROUP)]
    slot = lax.axis_index("particle")
    meta = jnp.stack([slot, lax.axis_index("space")]).astype(jnp.int32)
    own = stream[0]
    col_t, val_t, wgt_t = obs_col.T, obs_val.T, obs_weight.T
    vmem = pltpu.VMEM
    tile = vmem((rows, LANES), f32)
    whole = vmem((rows, columns), f32)
    padded = vmem((rows + 8, columns), f32)
    small = (per_row, rows)
    dma = pltpu.SemaphoreType.DMA

    sent, col_tile, wgt_tile, tt, first, last = call(
        observe_kernel,
        [SMEM] + [HBM] * 7,
        (
            shape((GROUP, modes_here * n_modes // LANES + 32, LANES), bf16),
            shape((rows, LANES), jnp.int32),
            shape((rows, LANES), f32),
            shape((n_modes, columns), bf16),
            shape((1, columns), f32),
            shape((1, columns), f32),
        ),
        [vmem(small, jnp.int32), vmem(small, f32), vmem(small, f32),
         vmem((modes_here, n_modes), bf16), whole, vmem((16, columns), f32), tile, tile, dma((8,))],
        "observe",
    )(log_weight, *map(in_hbm, (col_t, val_t, wgt_t, noise_coef[0], own, depth_field, tt_all)))
    sent, held = lax.optimization_barrier((sent, own))
    sent = lax.all_to_all(sent, "particle", 0, 0, axis_index_groups=groups, tiled=True)
    swap = swapped(held, "particle", 0)

    send, miss, part = call(
        gradient_kernel,
        [SMEM, SMEM, VMEM, VMEM, VMEM, VMEM],
        (shape((bands, 8, LANES), bf16), shape((rows + 8, LANES), f32), shape((8, LANES), f32)),
        [whole],
        "gradient",
    )(meta, selection, col_tile, wgt_tile, sent, tt)
    col_modes = lax.all_to_all(send, "space", 0, 0, tiled=True)

    near = jnp.where(selection[0, slot] < 1, own, swap)
    far = swapped(near, "particle", 1)
    col_modes, near = lax.optimization_barrier((col_modes, near))

    send = call(
        spectral_kernel,
        [SMEM, SMEM, VMEM, VMEM, VMEM, VMEM, VMEM, VMEM],
        shape((bands * (modes_here + 2), LANES), bf16),
        [vmem((bands * (modes_here + 2), LANES), f32)],
        "spectral",
    )(meta, selection, col_modes, sent, spectrum, part, tt, ht_all)
    send, first, last = lax.optimization_barrier((send, first, last))
    send = send.reshape(bands, modes_here // 2 + 1, 2, LANES)
    band_modes = lax.all_to_all(send, "space", 0, 0, tiled=True)
    band_modes = band_modes.reshape(bands * (modes_here + 2), LANES)
    above = lax.ppermute(last, "space", [(i, i + 1) for i in range(bands - 1)])
    below = lax.ppermute(first, "space", [(i + 1, i) for i in range(bands - 1)])

    field, part = call(
        relax_kernel,
        [SMEM, VMEM, VMEM, VMEM, HBM, VMEM, VMEM, VMEM, VMEM],
        (shape((rows, columns), f32), shape((bands, 1, LANES), f32)),
        [vmem((bands * (modes_here + 2), LANES), f32), tile, padded, padded, padded, whole, dma(())],
        "relax",
    )(target, col_tile, wgt_tile, miss, in_hbm(depth_field), above, below, band_modes, tt)
    parts = lax.all_to_all(part, "space", 0, 0, tiled=True)
    analysis = field + jnp.where(selection[1, slot] < 1, near, far)
    parts, analysis = lax.optimization_barrier((parts, analysis))
    misfit_out = jnp.sum(parts[:, 0, 0:1], axis=0)
    return analysis[None], misfit_out


def solution(mesh):
    return jax.shard_map(
        per_device,
        mesh=mesh,
        in_specs=(
            P("particle", "space", None),
            P("space", None),
            P("space", None),
            P("space", None),
            P("space", None),
            P("particle"),
            P(),
            P("space", None),
            P("particle", "space", None),
            P(),
        ),
        out_specs=(P("particle", "space", None), P("particle")),
        check_vma=False,
    )
```

```python
import math

import jax
import jax.numpy as jnp
import ml_dtypes
import numpy as np
from jax import lax
from jax.experimental import pallas as pl
from jax.experimental.pallas import tpu as pltpu
from jax.sharding import PartitionSpec as P

STRETCH = 0.05
RELAX_RATE = 0.8
NOISE_AMP = 0.3
LANES = 128
GROUP = 4
VMEM_LIMIT = 48 * 1024 * 1024


def table(extent, half_modes):
    cell = np.arange(extent, dtype=np.int64)[:, None]
    freq = np.arange(half_modes + 1, dtype=np.int64)[None, :]
    angles = (cell * freq % extent).astype(np.float64) * (2.0 * math.pi / extent)
    return np.concatenate([np.cos(angles), np.sin(angles[:, 1:half_modes])], axis=1).astype(
        ml_dtypes.bfloat16
    )


def halo_table(y_table, bands):
    rows = y_table.shape[0]
    width = rows // bands
    out = np.zeros((4, bands, y_table.shape[1]), dtype=y_table.dtype)
    for band in range(bands):
        for at, row in enumerate((width, width + 1, -2, -1)):
            source = band * width + row
            if 0 <= source < rows:
                out[at, band] = y_table[source]
    return out.reshape(bands * 4, y_table.shape[1])


def lane_iota():
    return lax.broadcasted_iota(jnp.int32, (8, LANES), 1)


def summed(values):
    return jnp.sum(jnp.sum(values, axis=0, keepdims=True), axis=1, keepdims=True)


def split3(value):
    high = value.astype(jnp.bfloat16).astype(jnp.float32)
    rest = value - high
    mid = rest.astype(jnp.bfloat16).astype(jnp.float32)
    return high, mid, rest - mid


def source_slot(sel_ref, meta_ref):
    slot = meta_ref[0]
    one = jnp.where(sel_ref[1, slot] < 1, slot, slot ^ 2)
    return jnp.where(sel_ref[0, one] < 1, one, one ^ 1)


def fill_tile(source_ref, scr):
    per_row = source_ref.shape[0]
    scr[...] = jnp.zeros(scr.shape, scr.dtype)
    scr[:, 0:per_row] = source_ref[...].T


def gather_rows(field_ref, col_scr, seen_scr):
    rows, columns = field_ref.shape
    for at in range(0, rows, 8):
        cols = col_scr[at : at + 8, :]
        high, low = cols >> 7, cols & 127
        seen = jnp.zeros((8, LANES), jnp.float32)
        for chunk in range(columns // LANES):
            here = field_ref[at : at + 8, chunk * LANES : (chunk + 1) * LANES]
            got = jnp.take_along_axis(here, low, axis=1, mode="promise_in_bounds")
            seen = jnp.where(high == chunk, got, seen)
        seen_scr[at : at + 8, :] = seen


def packed(tile, per_row):
    lane = lane_iota()
    out = tile[0:8, :]
    for group in range(1, tile.shape[0] // 8):
        rolled = pltpu.roll(tile[group * 8 : group * 8 + 8, :], group * per_row, axis=1)
        out = jnp.where(lane // per_row == group, rolled, out)
    return out


def observe_kernel(
    lw_ref, col_hbm, val_hbm, wgt_hbm, noise_hbm, stream_hbm, depth_hbm, tt_hbm,
    out_ref, col_scr, wgt_scr, tt_ref, first_ref, last_ref,
    col_ref, val_ref, wgt_ref, noise_ref, stream_ref, depth_ref, val_scr, seen_scr, sems,
):
    rows = depth_hbm.shape[0]
    pairs = (
        (col_hbm, col_ref),
        (val_hbm, val_ref),
        (stream_hbm, stream_ref),
        (noise_hbm, noise_ref),
        (wgt_hbm, wgt_ref),
        (depth_hbm.at[0:8, :], depth_ref.at[0:8, :]),
        (depth_hbm.at[rows - 8 : rows, :], depth_ref.at[8:16, :]),
        (tt_hbm, tt_ref),
    )
    loads = [pltpu.make_async_copy(a, b, sems.at[at]) for at, (a, b) in enumerate(pairs)]
    for load in loads:
        load.start()
    per_row = col_ref.shape[0]
    modes_here, n_modes = noise_ref.shape
    loads[0].wait()
    loads[1].wait()
    fill_tile(col_ref, col_scr)
    fill_tile(val_ref, val_scr)
    loads[2].wait()
    gather_rows(stream_ref, col_scr, seen_scr)
    mismatch = packed(val_scr[...] - seen_scr[...], per_row)
    weight = jnp.full((8, LANES), lw_ref[0], jnp.float32)
    row = lax.broadcasted_iota(jnp.int32, (8, LANES), 0)
    high, mid, low = split3(weight)
    weight = jnp.where(row == 0, high, jnp.where(row == 1, mid, jnp.where(row == 2, low, 0.0)))
    values = jnp.concatenate(list(split3(mismatch)) + [weight], axis=0).astype(jnp.bfloat16)
    loads[4].wait()
    fill_tile(wgt_ref, wgt_scr)
    loads[3].wait()
    noise = noise_ref[...]
    chunks = n_modes // LANES
    for peer in range(GROUP):
        for chunk in range(chunks):
            out_ref[peer, chunk * modes_here : (chunk + 1) * modes_here, :] = noise[
                :, chunk * LANES : (chunk + 1) * LANES
            ]
        out_ref[peer, chunks * modes_here :, :] = values
    loads[5].wait()
    loads[6].wait()
    first_ref[...] = depth_ref[0:1, :]
    last_ref[...] = depth_ref[15:16, :]
    loads[7].wait()


def gradient_kernel(
    meta_ref, sel_ref, target_ref, col_scr, wgt_scr, seen_ref, tt_ref, top_ref, bottom_ref,
    send_ref, miss_ref, part_ref, first_ref, second_ref, grad_scr, pack_scr,
):
    rows = grad_scr.shape[0]
    per_row = LANES * 8 // rows
    columns = tt_ref.shape[1]
    position = source_slot(sel_ref, meta_ref) & (GROUP - 1)
    first = seen_ref.shape[1] - 32
    sent = seen_ref[position][first:, :].astype(jnp.float32)
    mismatch = sent[0:8] + sent[8:16] + sent[16:24]
    weight = sent[24:25] + sent[25:26] + sent[26:27] - target_ref[0]
    slot = meta_ref[0]
    for section, stay_ref in enumerate((first_ref, second_ref)):
        stay = jnp.where(sel_ref[section, slot] < 1, 1.0, 0.0)
        stay_ref[...] = jnp.full(stay_ref.shape, stay, jnp.float32)
    miss_ref[rows:, :] = jnp.broadcast_to(weight, (8, LANES))
    tiles = [mismatch] + [
        pltpu.roll(mismatch, LANES - group * per_row, axis=1) for group in range(1, rows // 8)
    ]
    mismatch = jnp.concatenate(tiles, axis=0)
    miss_ref[0:rows, :] = mismatch
    weighted = wgt_scr[...] * mismatch
    part_ref[...] = jnp.broadcast_to(0.5 * summed(weighted * mismatch), (8, LANES))

    def repeated(tile):
        step = per_row
        while step < LANES:
            tile = tile + pltpu.roll(tile, step, axis=1)
            step *= 2
        return tile

    diagonal = lane_iota() // per_row == lax.broadcasted_iota(jnp.int32, (8, LANES), 0)
    row_f = lax.broadcasted_iota(jnp.int32, (LANES, LANES), 0).astype(jnp.float32)
    for group in range(rows // 8):
        at = group * 8
        cols = repeated(col_scr[at : at + 8, :])
        high = jnp.where(diagonal, cols >> 7, -1)
        low = jnp.sum(
            jnp.where(diagonal, (cols & 127).astype(jnp.float32), 0.0), axis=0, keepdims=True
        )
        one_hot = jnp.where(row_f == low, 1.0, 0.0).astype(jnp.bfloat16)
        left = []
        for piece in split3(repeated(weighted[at : at + 8, :])):
            left.append(
                jnp.concatenate(
                    [jnp.where(high == chunk, piece, 0.0) for chunk in range(columns // LANES)], axis=0
                ).astype(jnp.bfloat16)
            )
        spread = lax.dot_general(
            jnp.concatenate(left, axis=1),
            jnp.concatenate([one_hot] * 3, axis=1),
            (((1,), (1,)), ((), ())),
            preferred_element_type=jnp.float32,
        )
        for chunk in range(columns // LANES):
            grad_scr[at : at + 8, chunk * LANES : (chunk + 1) * LANES] = spread[
                chunk * 8 : chunk * 8 + 8, :
            ]
    gradient = grad_scr[...].astype(jnp.bfloat16)
    modes = lax.dot_general(
        tt_ref[...], gradient, (((1,), (1,)), ((), ())), preferred_element_type=jnp.float32
    )
    bands = modes.shape[0] // 16
    block = send_ref.shape[0] // bands
    split = modes.reshape(bands, 2, 8, rows)
    values = jnp.concatenate([split[:, 0], split[:, 1]], axis=2)
    pairs = columns // LANES
    top, bottom = (
        jnp.concatenate(
            [ref[:, pair * LANES : (pair + 1) * LANES] for pair in range(pairs)], axis=0
        )
        for ref in (top_ref, bottom_ref)
    )
    half = LANES // 2
    low = lax.broadcasted_iota(jnp.int32, (pairs, LANES), 1) < half
    even = split3(jnp.where(low, top, pltpu.roll(bottom, half, axis=1)))
    odd = split3(jnp.where(low, pltpu.roll(top, half, axis=1), bottom))
    for band in range(bands):
        at = band * block
        pack_scr[at : at + 8, :] = values[band]
        for piece in range(3):
            row = (odd if band % 2 else even)[piece][band // 2 : band // 2 + 1]
            pack_scr[at + 8 + piece : at + 9 + piece, :] = row
        pack_scr[at + 11 : at + 12, :] = jnp.zeros((1, LANES), jnp.float32)
    send_ref[...] = pack_scr[...].astype(jnp.bfloat16)


def spectral_kernel(
    meta_ref, sel_ref, modes_ref, noise_ref, spec_ref, part_ref, tt_ref, ht_ref, send_ref, pack_scr,
    unpack_scr,
):
    half = LANES // 2
    modes_here, n_modes = spec_ref.shape
    bands = n_modes // modes_here
    unpack_scr[...] = modes_ref[...].astype(jnp.float32)
    rows = tt_ref.shape[1]
    norm_factor = 4.0 / (rows * rows)
    position = source_slot(sel_ref, meta_ref) & (GROUP - 1)
    lane = lane_iota()
    low = lane < half
    tops, bottoms = [], []
    for pair in range(bands // 2):
        even = unpack_scr[24 * pair : 24 * pair + 8, :]
        odd = unpack_scr[24 * pair + 12 : 24 * pair + 20, :]
        tops.append(jnp.where(low, even, pltpu.roll(odd, half, axis=1)))
        bottoms.append(jnp.where(low, pltpu.roll(even, half, axis=1), odd))
    columns = jnp.concatenate(
        [jnp.concatenate(tops, axis=1), jnp.concatenate(bottoms, axis=1)], axis=0
    ).astype(jnp.bfloat16)
    coefficients = lax.dot_general(
        columns, tt_ref[...], (((1,), (1,)), ((), ())), preferred_element_type=jnp.float32
    )
    scaled = norm_factor * spec_ref[...]
    weighted = coefficients * scaled
    energy = summed(coefficients * weighted)
    noise = noise_ref[position][0 : noise_ref.shape[1] - 32, :]
    noise = jnp.concatenate(
        [noise[at : at + modes_here] for at in range(0, noise.shape[0], modes_here)], axis=1
    )
    shaped = (jnp.sqrt(scaled) * noise.astype(jnp.float32)).astype(jnp.bfloat16)
    weighted = weighted.astype(jnp.bfloat16)
    stacked = jnp.concatenate([weighted, shaped], axis=0)
    inverted = jnp.dot(stacked, tt_ref[...], preferred_element_type=jnp.float32)
    depth = sum(unpack_scr[pl.ds(8 + piece, bands, stride=12), :] for piece in range(3))
    band_row = lax.broadcasted_iota(jnp.int32, (bands, LANES), 0)
    band_low = lax.broadcasted_iota(jnp.int32, (bands, LANES), 1) < half
    above = jnp.where(band_row > 0, pltpu.roll(depth, 1, axis=0), 0.0)
    below = jnp.where(band_row < bands - 1, pltpu.roll(depth, bands - 1, axis=0), 0.0)
    beside = split3(pltpu.roll(jnp.where(band_low, below, above), half, axis=1))
    block = modes_here + 6
    low16 = lax.broadcasted_iota(jnp.int32, (modes_here, LANES), 1) < half
    for pair in range(bands // 2):
        first = inverted[0:modes_here, pair * LANES : (pair + 1) * LANES]
        second = inverted[modes_here:, pair * LANES : (pair + 1) * LANES]
        at = 2 * pair * block
        pack_scr[at : at + modes_here, :] = jnp.where(
            low16, first, pltpu.roll(second, half, axis=1)
        )
        at += block
        pack_scr[at : at + modes_here, :] = jnp.where(
            low16, pltpu.roll(first, half, axis=1), second
        )
    halo = lax.dot_general(
        ht_ref[...], stacked, (((1,), (1,)), ((), ())), preferred_element_type=jnp.float32
    )
    halo = jnp.concatenate(
        [halo, jnp.zeros((4 * bands, LANES - 2 * modes_here), jnp.float32)], axis=1
    )
    window = lax.broadcasted_iota(jnp.int32, (bands, LANES), 1) // modes_here
    edges = jnp.zeros((bands, LANES), jnp.float32)
    for at in range(8):
        field, row = at // 4, at % 4
        shift = (at - field) * modes_here % LANES
        value = halo[row * bands : (row + 1) * bands]
        edges = jnp.where(window == at, pltpu.roll(value, shift, axis=1) if shift else value, edges)
    lane1 = lax.broadcasted_iota(jnp.int32, (1, LANES), 1)
    pieces = jnp.zeros((1, LANES), jnp.float32)
    for at, piece in enumerate(split3(part_ref[0:1, 0:1]) + split3(energy)):
        pieces = jnp.where(lane1 == at, piece, pieces)
    for band in range(bands):
        at = band * block + modes_here
        pack_scr[at : at + 1, :] = edges[band : band + 1]
        pack_scr[at + 1 : at + 2, :] = pieces
        for piece in range(3):
            pack_scr[at + 2 + piece : at + 3 + piece, :] = beside[piece][band : band + 1]
        pack_scr[at + 5 : at + 6, :] = jnp.zeros((1, LANES), jnp.float32)
    send_ref[...] = pack_scr[...].astype(jnp.bfloat16)


def relax_kernel(
    col_scr, wgt_scr, miss_ref, depth_hbm, modes_ref, tt_ref,
    field_ref, part_ref, unpack_scr, seen_scr, inc_scr, one_scr, rate_ref, depth_ref,
    sem,
):
    depth = pltpu.make_async_copy(depth_hbm, depth_ref, sem)
    depth.start()
    rows = depth_ref.shape[0]

    def rate(depth):
        return RELAX_RATE * depth / (4.0 * depth + STRETCH)

    n_modes, columns = tt_ref.shape
    bands = part_ref.shape[0]
    modes_here = n_modes // bands
    lane = lane_iota()
    block = modes_here + 6
    unpack_scr[...] = modes_ref[...].astype(jnp.float32)
    edges = unpack_scr[pl.ds(modes_here, bands, stride=block), :]
    scalars = unpack_scr[pl.ds(modes_here + 1, bands, stride=block), :]
    row = lax.broadcasted_iota(jnp.int32, (8, LANES), 0)
    window = lane // modes_here
    quads = []
    for quad in range(0, bands, 8):
        tile = edges[quad : quad + 8]
        for bit in (1, 2, 4):
            up = pltpu.roll(pltpu.roll(tile, 8 - bit, axis=0), bit * modes_here, axis=1)
            down = pltpu.roll(pltpu.roll(tile, bit, axis=0), LANES - bit * modes_here, axis=1)
            upper, later = (row & bit) == 0, (window & bit) == 0
            tile = jnp.where(upper == later, tile, jnp.where(upper, up, down))
        quads.append(tile)
    halo = jnp.concatenate(quads, axis=1)
    lanes = lax.broadcasted_iota(jnp.int32, scalars.shape, 1)
    misfit = summed(jnp.where(lanes < 3, scalars, 0.0))
    energy = summed(jnp.where((lanes >= 3) & (lanes < 6), scalars, 0.0))
    weight = miss_ref[rows : rows + 1, 0:1]
    step = (misfit + weight) / (energy + 1.0)
    main = jnp.concatenate(
        [unpack_scr[at * block : at * block + modes_here, :] for at in range(bands)], axis=0
    ).astype(jnp.bfloat16)
    pulled = lax.dot_general(main, tt_ref[...], (((0,), (0,)), ((), ())), preferred_element_type=jnp.float32)
    pulled_h = jnp.dot(halo.astype(jnp.bfloat16), tt_ref[...], preferred_element_type=jnp.float32)
    for at in range(0, rows, 8):
        inc_scr[at : at + 8, :] = step * pulled[at : at + 8] + NOISE_AMP * pulled[rows + at : rows + at + 8]
    edge = pulled_h
    edge = step * edge + NOISE_AMP * pltpu.roll(edge, 4, axis=0)
    row8 = lax.broadcasted_iota(jnp.int32, (8, columns), 0)
    inc_scr[rows:, :] = jnp.where(row8 < 2, edge, jnp.where(row8 < 6, 0.0, pltpu.roll(edge, 4, axis=0)))
    depth.wait()

    def rate(depth):
        return RELAX_RATE * depth / (4.0 * depth + STRETCH)

    even, odd = (
        sum(
            unpack_scr[pl.ds(start + piece, bands // 2, stride=2 * block), :] for piece in range(3)
        )
        for start in (modes_here + 2, modes_here + 2 + block)
    )
    half = LANES // 2
    low = lax.broadcasted_iota(jnp.int32, (bands // 2, LANES), 1) < half
    above = rate(jnp.where(low, even, pltpu.roll(odd, half, axis=1)))
    below = rate(jnp.where(low, pltpu.roll(even, half, axis=1), odd))
    for pair in range(bands // 2):
        rate_ref[rows:, pair * LANES : (pair + 1) * LANES] = jnp.where(
            row == 0,
            below[pair : pair + 1],
            jnp.where(row == 7, above[pair : pair + 1], 0.0),
        )
    for at in range(0, rows, 8):
        rate_ref[at : at + 8, :] = rate(depth_ref[at : at + 8, :])
    length = rows + 8

    def relaxed(source_ref, at):
        here = source_ref[at : at + 8, :]
        before = source_ref[(at - 8) % length : (at - 8) % length + 8, :]
        after = source_ref[(at + 8) % length : (at + 8) % length + 8, :]
        around = (
            pltpu.roll(jnp.where(row8 == 7, before, here), 1, axis=0)
            + pltpu.roll(jnp.where(row8 == 0, after, here), 7, axis=0)
            + pltpu.roll(here, 1, axis=1)
            + pltpu.roll(here, columns - 1, axis=1)
        )
        return (1.0 - RELAX_RATE) * here + rate_ref[at : at + 8, :] * (
            around - inc_scr[at : at + 8, :]
        )

    for at in range(0, length, 8):
        one_scr[at : at + 8, :] = relaxed(inc_scr, at)
    for at in range(0, rows, 8):
        field_ref[at : at + 8, :] = relaxed(one_scr, at)
    gather_rows(field_ref, col_scr, seen_scr)
    left_over = miss_ref[0:rows, :] - seen_scr[...]
    part = 0.5 * summed(wgt_scr[...] * left_over * left_over)
    part_ref[...] = jnp.broadcast_to(part[None], part_ref.shape)


SMEM = pl.BlockSpec(memory_space=pltpu.SMEM)
VMEM = pl.BlockSpec(memory_space=pltpu.VMEM)
HBM = pl.BlockSpec(memory_space=pltpu.HBM)


COST = {"observe": 40, "gradient": 40, "spectral": 1, "relax": 1}


def call(kernel, in_specs, out_shape, scratch, name, out_specs=None):
    return pl.pallas_call(
        kernel,
        in_specs=in_specs,
        out_specs=out_specs or jax.tree.map(lambda _: VMEM, out_shape),
        out_shape=out_shape,
        scratch_shapes=scratch,
        name=name,
        cost_estimate=pl.CostEstimate(
            flops=COST[name] * 10**9, transcendentals=0, bytes_accessed=4 * 10**6
        ),
        compiler_params=pltpu.CompilerParams(vmem_limit_bytes=VMEM_LIMIT),
    )


def in_hbm(value):
    return pltpu.with_memory_space_constraint(value, pltpu.HBM)


def swapped(value, axis, bit):
    mask = 2**bit
    pairs = [(source, source ^ mask) for source in range(lax.axis_size(axis))]
    return lax.ppermute(value, axis, pairs)


def per_device(
    stream, depth_field, obs_col, obs_val, obs_weight, log_weight, target, spectrum, noise_coef,
    selection,
):
    _, rows, columns = stream.shape
    per_row = obs_col.shape[1]
    modes_here, n_modes = spectrum.shape
    bands = lax.axis_size("space")
    particles = lax.axis_size("particle")
    y_table = table(rows * bands, n_modes // 2)
    tt_all = jnp.asarray(np.ascontiguousarray(y_table.T))
    ht_all = jnp.asarray(halo_table(y_table, bands))
    f32, bf16 = jnp.float32, jnp.bfloat16
    shape = jax.ShapeDtypeStruct
    groups = [[g * GROUP + i for i in range(GROUP)] for g in range(particles // GROUP)]
    slot = lax.axis_index("particle")
    meta = jnp.stack([slot, lax.axis_index("space")]).astype(jnp.int32)
    own = stream[0]
    col_t, val_t, wgt_t = obs_col.T, obs_val.T, obs_weight.T
    vmem = pltpu.VMEM
    tile = vmem((rows, LANES), f32)
    whole = vmem((rows, columns), f32)
    padded = vmem((rows + 8, columns), f32)
    small = (per_row, rows)
    dma = pltpu.SemaphoreType.DMA

    sent, col_tile, wgt_tile, tt, first, last = call(
        observe_kernel,
        [SMEM] + [HBM] * 7,
        (
            shape((GROUP, modes_here * n_modes // LANES + 32, LANES), bf16),
            shape((rows, LANES), jnp.int32),
            shape((rows, LANES), f32),
            shape((n_modes, columns), bf16),
            shape((1, columns), f32),
            shape((1, columns), f32),
        ),
        [vmem(small, jnp.int32), vmem(small, f32), vmem(small, f32),
         vmem((modes_here, n_modes), bf16), whole, vmem((16, columns), f32), tile, tile, dma((8,))],
        "observe",
    )(log_weight, *map(in_hbm, (col_t, val_t, wgt_t, noise_coef[0], own, depth_field, tt_all)))
    sent, held = lax.optimization_barrier((sent, own))
    sent = lax.all_to_all(sent, "particle", 0, 0, axis_index_groups=groups, tiled=True)
    swap = swapped(held, "particle", 0)

    send, miss, part, stay_first, stay_second = call(
        gradient_kernel,
        [SMEM, SMEM, SMEM] + [VMEM] * 6,
        (
            shape((bands * 12, LANES), bf16),
            shape((rows + 8, LANES), f32),
            shape((8, LANES), f32),
            shape((1, columns), f32),
            shape((1, columns), f32),
        ),
        [whole, vmem((bands * 12, LANES), f32)],
        "gradient",
    )(meta, selection, target, col_tile, wgt_tile, sent, tt, first, last)
    send = send.reshape(bands, 6, 2, LANES)
    col_modes = lax.all_to_all(send, "space", 0, 0, tiled=True).reshape(bands * 12, LANES)

    near = jnp.where(stay_first > 0.0, own, swap)
    far = swapped(near, "particle", 1)
    col_modes, near = lax.optimization_barrier((col_modes, near))

    send = call(
        spectral_kernel,
        [SMEM, SMEM, VMEM, VMEM, VMEM, VMEM, VMEM, VMEM],
        shape((bands * (modes_here + 6), LANES), bf16),
        [vmem((bands * (modes_here + 6), LANES), f32), vmem((bands * 12, LANES), f32)],
        "spectral",
    )(meta, selection, col_modes, sent, spectrum, part, tt, ht_all)
    send = send.reshape(bands, modes_here // 2 + 3, 2, LANES)
    band_modes = lax.all_to_all(send, "space", 0, 0, tiled=True)
    band_modes = band_modes.reshape(bands * (modes_here + 6), LANES)

    field, part = call(
        relax_kernel,
        [VMEM, VMEM, VMEM, HBM, VMEM, VMEM],
        (shape((rows, columns), f32), shape((bands, 1, LANES), f32)),
        [vmem((bands * (modes_here + 6), LANES), f32), tile, padded, padded, padded, whole, dma(())],
        "relax",
    )(col_tile, wgt_tile, miss, in_hbm(depth_field), band_modes, tt)
    parts = lax.all_to_all(part, "space", 0, 0, tiled=True)
    analysis = field + jnp.where(stay_second > 0.0, near, far)
    parts, analysis = lax.optimization_barrier((parts, analysis))
    misfit_out = jnp.sum(parts[:, 0, 0:1], axis=0)
    return analysis[None], misfit_out


def solution(mesh):
    return jax.shard_map(
        per_device,
        mesh=mesh,
        in_specs=(
            P("particle", "space", None),
            P("space", None),
            P("space", None),
            P("space", None),
            P("space", None),
            P("particle"),
            P(),
            P("space", None),
            P("particle", "space", None),
            P(),
        ),
        out_specs=(P("particle", "space", None), P("particle")),
        check_vma=False,
    )
```

```python
import math

import jax
import jax.numpy as jnp
import ml_dtypes
import numpy as np
from jax import lax
from jax.experimental import pallas as pl
from jax.experimental.pallas import tpu as pltpu
from jax.sharding import PartitionSpec as P

STRETCH = 0.05
RELAX_RATE = 0.8
NOISE_AMP = 0.3
LANES = 128
GROUP = 4
VMEM_LIMIT = 48 * 1024 * 1024


def table(extent, half_modes):
    cell = np.arange(extent, dtype=np.int64)[:, None]
    freq = np.arange(half_modes + 1, dtype=np.int64)[None, :]
    angles = (cell * freq % extent).astype(np.float64) * (2.0 * math.pi / extent)
    return np.concatenate([np.cos(angles), np.sin(angles[:, 1:half_modes])], axis=1).astype(
        ml_dtypes.bfloat16
    )


def halo_table(y_table, bands):
    rows = y_table.shape[0]
    width = rows // bands
    out = np.zeros((4, bands, y_table.shape[1]), dtype=y_table.dtype)
    for band in range(bands):
        for at, row in enumerate((width, width + 1, -2, -1)):
            source = band * width + row
            if 0 <= source < rows:
                out[at, band] = y_table[source]
    return out.reshape(bands * 4, y_table.shape[1])


def lane_iota():
    return lax.broadcasted_iota(jnp.int32, (8, LANES), 1)


def summed(values):
    return jnp.sum(jnp.sum(values, axis=0, keepdims=True), axis=1, keepdims=True)


def split2(value):
    high = value.astype(jnp.bfloat16).astype(jnp.float32)
    return high, value - high


def split3(value):
    high = value.astype(jnp.bfloat16).astype(jnp.float32)
    rest = value - high
    mid = rest.astype(jnp.bfloat16).astype(jnp.float32)
    return high, mid, rest - mid


def source_slot(sel_ref, meta_ref):
    slot = meta_ref[0]
    one = jnp.where(sel_ref[1, slot] < 1, slot, slot ^ 2)
    return jnp.where(sel_ref[0, one] < 1, one, one ^ 1)


def fill_tile(source_ref, scr):
    per_row = source_ref.shape[0]
    scr[...] = jnp.zeros(scr.shape, scr.dtype)
    scr[:, 0:per_row] = source_ref[...].T


def gather_rows(field_ref, col_scr, seen_scr):
    rows, columns = field_ref.shape
    for at in range(0, rows, 8):
        cols = col_scr[at : at + 8, :]
        high, low = cols >> 7, cols & 127
        seen = jnp.zeros((8, LANES), jnp.float32)
        for chunk in range(columns // LANES):
            here = field_ref[at : at + 8, chunk * LANES : (chunk + 1) * LANES]
            got = jnp.take_along_axis(here, low, axis=1, mode="promise_in_bounds")
            seen = jnp.where(high == chunk, got, seen)
        seen_scr[at : at + 8, :] = seen


def packed(tile, per_row):
    lane = lane_iota()
    out = tile[0:8, :]
    for group in range(1, tile.shape[0] // 8):
        rolled = pltpu.roll(tile[group * 8 : group * 8 + 8, :], group * per_row, axis=1)
        out = jnp.where(lane // per_row == group, rolled, out)
    return out


def observe_kernel(
    lw_ref, col_hbm, val_hbm, wgt_hbm, noise_hbm, stream_hbm, depth_hbm, tt_hbm,
    out_ref, col_scr, wgt_scr, tt_ref, first_ref, last_ref,
    col_ref, val_ref, wgt_ref, noise_ref, stream_ref, depth_ref, val_scr, seen_scr, sems,
):
    rows = depth_hbm.shape[0]
    pairs = (
        (col_hbm, col_ref),
        (val_hbm, val_ref),
        (stream_hbm, stream_ref),
        (noise_hbm, noise_ref),
        (wgt_hbm, wgt_ref),
        (depth_hbm.at[0:8, :], depth_ref.at[0:8, :]),
        (depth_hbm.at[rows - 8 : rows, :], depth_ref.at[8:16, :]),
        (tt_hbm, tt_ref),
    )
    loads = [pltpu.make_async_copy(a, b, sems.at[at]) for at, (a, b) in enumerate(pairs)]
    for load in loads:
        load.start()
    per_row = col_ref.shape[0]
    modes_here, n_modes = noise_ref.shape
    loads[0].wait()
    loads[1].wait()
    fill_tile(col_ref, col_scr)
    fill_tile(val_ref, val_scr)
    loads[2].wait()
    gather_rows(stream_ref, col_scr, seen_scr)
    mismatch = packed(val_scr[...] - seen_scr[...], per_row)
    weight = jnp.full((8, LANES), lw_ref[0], jnp.float32)
    row = lax.broadcasted_iota(jnp.int32, (8, LANES), 0)
    high, mid, low = split3(weight)
    weight = jnp.where(row == 0, high, jnp.where(row == 1, mid, jnp.where(row == 2, low, 0.0)))
    values = jnp.concatenate(list(split3(mismatch)) + [weight], axis=0).astype(jnp.bfloat16)
    loads[4].wait()
    fill_tile(wgt_ref, wgt_scr)
    loads[3].wait()
    noise = noise_ref[...]
    chunks = n_modes // LANES
    for peer in range(GROUP):
        for chunk in range(chunks):
            out_ref[peer, chunk * modes_here : (chunk + 1) * modes_here, :] = noise[
                :, chunk * LANES : (chunk + 1) * LANES
            ]
        out_ref[peer, chunks * modes_here :, :] = values
    loads[5].wait()
    loads[6].wait()
    first_ref[...] = depth_ref[0:1, :]
    last_ref[...] = depth_ref[15:16, :]
    loads[7].wait()


def gradient_kernel(
    meta_ref, sel_ref, target_ref, col_scr, wgt_scr, seen_ref, tt_ref, top_ref, bottom_ref,
    send_ref, miss_ref, part_ref, first_ref, second_ref, grad_scr, pack_scr,
):
    rows = grad_scr.shape[0]
    per_row = LANES * 8 // rows
    columns = tt_ref.shape[1]
    position = source_slot(sel_ref, meta_ref) & (GROUP - 1)
    first = seen_ref.shape[1] - 32
    sent = seen_ref[position][first:, :].astype(jnp.float32)
    mismatch = sent[0:8] + sent[8:16] + sent[16:24]
    weight = sent[24:25] + sent[25:26] + sent[26:27] - target_ref[0]
    slot = meta_ref[0]
    for section, stay_ref in enumerate((first_ref, second_ref)):
        stay = jnp.where(sel_ref[section, slot] < 1, 1.0, 0.0)
        stay_ref[...] = jnp.full(stay_ref.shape, stay, jnp.float32)
    miss_ref[rows:, :] = jnp.broadcast_to(weight, (8, LANES))
    tiles = [mismatch] + [
        pltpu.roll(mismatch, LANES - group * per_row, axis=1) for group in range(1, rows // 8)
    ]
    mismatch = jnp.concatenate(tiles, axis=0)
    miss_ref[0:rows, :] = mismatch
    weighted = wgt_scr[...] * mismatch
    part_ref[...] = jnp.broadcast_to(0.5 * summed(weighted * mismatch), (8, LANES))

    def repeated(tile):
        step = per_row
        while step < LANES:
            tile = tile + pltpu.roll(tile, step, axis=1)
            step *= 2
        return tile

    diagonal = lane_iota() // per_row == lax.broadcasted_iota(jnp.int32, (8, LANES), 0)
    row_f = lax.broadcasted_iota(jnp.int32, (LANES, LANES), 0).astype(jnp.float32)
    for group in range(rows // 8):
        at = group * 8
        cols = repeated(col_scr[at : at + 8, :])
        high = jnp.where(diagonal, cols >> 7, -1)
        low = jnp.sum(
            jnp.where(diagonal, (cols & 127).astype(jnp.float32), 0.0), axis=0, keepdims=True
        )
        one_hot = jnp.where(row_f == low, 1.0, 0.0).astype(jnp.bfloat16)
        left = []
        for piece in split3(repeated(weighted[at : at + 8, :])):
            left.append(
                jnp.concatenate(
                    [jnp.where(high == chunk, piece, 0.0) for chunk in range(columns // LANES)], axis=0
                ).astype(jnp.bfloat16)
            )
        spread = lax.dot_general(
            jnp.concatenate(left, axis=1),
            jnp.concatenate([one_hot] * 3, axis=1),
            (((1,), (1,)), ((), ())),
            preferred_element_type=jnp.float32,
        )
        for chunk in range(columns // LANES):
            grad_scr[at : at + 8, chunk * LANES : (chunk + 1) * LANES] = spread[
                chunk * 8 : chunk * 8 + 8, :
            ]
    gradient = grad_scr[...].astype(jnp.bfloat16)
    modes = lax.dot_general(
        tt_ref[...], gradient, (((1,), (1,)), ((), ())), preferred_element_type=jnp.float32
    )
    bands = modes.shape[0] // 16
    block = send_ref.shape[0] // bands
    split = modes.reshape(bands, 2, 8, rows)
    values = jnp.concatenate([split[:, 0], split[:, 1]], axis=2)
    pairs = columns // LANES
    top, bottom = (
        jnp.concatenate(
            [ref[:, pair * LANES : (pair + 1) * LANES] for pair in range(pairs)], axis=0
        )
        for ref in (top_ref, bottom_ref)
    )
    half = LANES // 2
    low = lax.broadcasted_iota(jnp.int32, (pairs, LANES), 1) < half
    even = split2(jnp.where(low, top, pltpu.roll(bottom, half, axis=1)))
    odd = split2(jnp.where(low, pltpu.roll(top, half, axis=1), bottom))
    for band in range(bands):
        at = band * block
        pack_scr[at : at + 8, :] = values[band]
        for piece in range(2):
            row = (odd if band % 2 else even)[piece][band // 2 : band // 2 + 1]
            pack_scr[at + 8 + piece : at + 9 + piece, :] = row
    send_ref[...] = pack_scr[...].astype(jnp.bfloat16)


def spectral_kernel(
    meta_ref, sel_ref, modes_ref, noise_ref, spec_ref, part_ref, tt_ref, ht_ref, send_ref, pack_scr,
    unpack_scr,
):
    half = LANES // 2
    modes_here, n_modes = spec_ref.shape
    bands = n_modes // modes_here
    unpack_scr[...] = modes_ref[...].astype(jnp.float32)
    rows = tt_ref.shape[1]
    norm_factor = 4.0 / (rows * rows)
    position = source_slot(sel_ref, meta_ref) & (GROUP - 1)
    lane = lane_iota()
    low = lane < half
    tops, bottoms = [], []
    for pair in range(bands // 2):
        even = unpack_scr[20 * pair : 20 * pair + 8, :]
        odd = unpack_scr[20 * pair + 10 : 20 * pair + 18, :]
        tops.append(jnp.where(low, even, pltpu.roll(odd, half, axis=1)))
        bottoms.append(jnp.where(low, pltpu.roll(even, half, axis=1), odd))
    columns = jnp.concatenate(
        [jnp.concatenate(tops, axis=1), jnp.concatenate(bottoms, axis=1)], axis=0
    ).astype(jnp.bfloat16)
    coefficients = lax.dot_general(
        columns, tt_ref[...], (((1,), (1,)), ((), ())), preferred_element_type=jnp.float32
    )
    scaled = norm_factor * spec_ref[...]
    weighted = coefficients * scaled
    energy = summed(coefficients * weighted)
    noise = noise_ref[position][0 : noise_ref.shape[1] - 32, :]
    noise = jnp.concatenate(
        [noise[at : at + modes_here] for at in range(0, noise.shape[0], modes_here)], axis=1
    )
    shaped = (jnp.sqrt(scaled) * noise.astype(jnp.float32)).astype(jnp.bfloat16)
    weighted = weighted.astype(jnp.bfloat16)
    stacked = jnp.concatenate([weighted, shaped], axis=0)
    inverted = jnp.dot(stacked, tt_ref[...], preferred_element_type=jnp.float32)
    depth = sum(unpack_scr[pl.ds(8 + piece, bands, stride=10), :] for piece in range(2))
    band_row = lax.broadcasted_iota(jnp.int32, (bands, LANES), 0)
    band_low = lax.broadcasted_iota(jnp.int32, (bands, LANES), 1) < half
    above = jnp.where(band_row > 0, pltpu.roll(depth, 1, axis=0), 0.0)
    below = jnp.where(band_row < bands - 1, pltpu.roll(depth, bands - 1, axis=0), 0.0)
    beside = split2(pltpu.roll(jnp.where(band_low, below, above), half, axis=1))
    block = modes_here + 4
    low16 = lax.broadcasted_iota(jnp.int32, (modes_here, LANES), 1) < half
    for pair in range(bands // 2):
        first = inverted[0:modes_here, pair * LANES : (pair + 1) * LANES]
        second = inverted[modes_here:, pair * LANES : (pair + 1) * LANES]
        at = 2 * pair * block
        pack_scr[at : at + modes_here, :] = jnp.where(
            low16, first, pltpu.roll(second, half, axis=1)
        )
        at += block
        pack_scr[at : at + modes_here, :] = jnp.where(
            low16, pltpu.roll(first, half, axis=1), second
        )
    halo = lax.dot_general(
        ht_ref[...], stacked, (((1,), (1,)), ((), ())), preferred_element_type=jnp.float32
    )
    halo = jnp.concatenate(
        [halo, jnp.zeros((4 * bands, LANES - 2 * modes_here), jnp.float32)], axis=1
    )
    window = lax.broadcasted_iota(jnp.int32, (bands, LANES), 1) // modes_here
    edges = jnp.zeros((bands, LANES), jnp.float32)
    for at in range(8):
        field, row = at // 4, at % 4
        shift = (at - field) * modes_here % LANES
        value = halo[row * bands : (row + 1) * bands]
        edges = jnp.where(window == at, pltpu.roll(value, shift, axis=1) if shift else value, edges)
    lane1 = lax.broadcasted_iota(jnp.int32, (1, LANES), 1)
    pieces = jnp.zeros((1, LANES), jnp.float32)
    for at, piece in enumerate(split3(part_ref[0:1, 0:1]) + split3(energy)):
        pieces = jnp.where(lane1 == at, piece, pieces)
    for band in range(bands):
        at = band * block + modes_here
        pack_scr[at : at + 1, :] = edges[band : band + 1]
        pack_scr[at + 1 : at + 2, :] = pieces
        for piece in range(2):
            pack_scr[at + 2 + piece : at + 3 + piece, :] = beside[piece][band : band + 1]
    send_ref[...] = pack_scr[...].astype(jnp.bfloat16)


def relax_kernel(
    col_scr, wgt_scr, miss_ref, depth_hbm, modes_ref, tt_ref,
    field_ref, part_ref, unpack_scr, seen_scr, inc_scr, one_scr, rate_ref, depth_ref,
    sem,
):
    depth = pltpu.make_async_copy(depth_hbm, depth_ref, sem)
    depth.start()
    rows = depth_ref.shape[0]

    def rate(depth):
        return RELAX_RATE * depth / (4.0 * depth + STRETCH)

    n_modes, columns = tt_ref.shape
    bands = part_ref.shape[0]
    modes_here = n_modes // bands
    lane = lane_iota()
    block = modes_here + 4
    unpack_scr[...] = modes_ref[...].astype(jnp.float32)
    edges = unpack_scr[pl.ds(modes_here, bands, stride=block), :]
    scalars = unpack_scr[pl.ds(modes_here + 1, bands, stride=block), :]
    row = lax.broadcasted_iota(jnp.int32, (8, LANES), 0)
    window = lane // modes_here
    quads = []
    for quad in range(0, bands, 8):
        tile = edges[quad : quad + 8]
        for bit in (1, 2, 4):
            up = pltpu.roll(pltpu.roll(tile, 8 - bit, axis=0), bit * modes_here, axis=1)
            down = pltpu.roll(pltpu.roll(tile, bit, axis=0), LANES - bit * modes_here, axis=1)
            upper, later = (row & bit) == 0, (window & bit) == 0
            tile = jnp.where(upper == later, tile, jnp.where(upper, up, down))
        quads.append(tile)
    halo = jnp.concatenate(quads, axis=1)
    lanes = lax.broadcasted_iota(jnp.int32, scalars.shape, 1)
    misfit = summed(jnp.where(lanes < 3, scalars, 0.0))
    energy = summed(jnp.where((lanes >= 3) & (lanes < 6), scalars, 0.0))
    weight = miss_ref[rows : rows + 1, 0:1]
    step = (misfit + weight) / (energy + 1.0)
    main = jnp.concatenate(
        [unpack_scr[at * block : at * block + modes_here, :] for at in range(bands)], axis=0
    ).astype(jnp.bfloat16)
    pulled = lax.dot_general(main, tt_ref[...], (((0,), (0,)), ((), ())), preferred_element_type=jnp.float32)
    pulled_h = jnp.dot(halo.astype(jnp.bfloat16), tt_ref[...], preferred_element_type=jnp.float32)
    for at in range(0, rows, 8):
        inc_scr[at : at + 8, :] = step * pulled[at : at + 8] + NOISE_AMP * pulled[rows + at : rows + at + 8]
    edge = pulled_h
    edge = step * edge + NOISE_AMP * pltpu.roll(edge, 4, axis=0)
    row8 = lax.broadcasted_iota(jnp.int32, (8, columns), 0)
    inc_scr[rows:, :] = jnp.where(row8 < 2, edge, jnp.where(row8 < 6, 0.0, pltpu.roll(edge, 4, axis=0)))
    depth.wait()

    def rate(depth):
        return RELAX_RATE * depth / (4.0 * depth + STRETCH)

    even, odd = (
        sum(
            unpack_scr[pl.ds(start + piece, bands // 2, stride=2 * block), :] for piece in range(2)
        )
        for start in (modes_here + 2, modes_here + 2 + block)
    )
    half = LANES // 2
    low = lax.broadcasted_iota(jnp.int32, (bands // 2, LANES), 1) < half
    above = rate(jnp.where(low, even, pltpu.roll(odd, half, axis=1)))
    below = rate(jnp.where(low, pltpu.roll(even, half, axis=1), odd))
    for pair in range(bands // 2):
        rate_ref[rows:, pair * LANES : (pair + 1) * LANES] = jnp.where(
            row == 0,
            below[pair : pair + 1],
            jnp.where(row == 7, above[pair : pair + 1], 0.0),
        )
    for at in range(0, rows, 8):
        rate_ref[at : at + 8, :] = rate(depth_ref[at : at + 8, :])
    length = rows + 8

    def relaxed(source_ref, at):
        here = source_ref[at : at + 8, :]
        before = source_ref[(at - 8) % length : (at - 8) % length + 8, :]
        after = source_ref[(at + 8) % length : (at + 8) % length + 8, :]
        around = (
            pltpu.roll(jnp.where(row8 == 7, before, here), 1, axis=0)
            + pltpu.roll(jnp.where(row8 == 0, after, here), 7, axis=0)
            + pltpu.roll(here, 1, axis=1)
            + pltpu.roll(here, columns - 1, axis=1)
        )
        return (1.0 - RELAX_RATE) * here + rate_ref[at : at + 8, :] * (
            around - inc_scr[at : at + 8, :]
        )

    for at in range(0, length, 8):
        one_scr[at : at + 8, :] = relaxed(inc_scr, at)
    for at in range(0, rows, 8):
        field_ref[at : at + 8, :] = relaxed(one_scr, at)
    gather_rows(field_ref, col_scr, seen_scr)
    left_over = miss_ref[0:rows, :] - seen_scr[...]
    part = 0.5 * summed(wgt_scr[...] * left_over * left_over)
    part_ref[...] = jnp.broadcast_to(part[None], part_ref.shape)


SMEM = pl.BlockSpec(memory_space=pltpu.SMEM)
VMEM = pl.BlockSpec(memory_space=pltpu.VMEM)
HBM = pl.BlockSpec(memory_space=pltpu.HBM)


COST = {"observe": 40, "gradient": 40, "spectral": 1, "relax": 1}


def call(kernel, in_specs, out_shape, scratch, name, out_specs=None):
    return pl.pallas_call(
        kernel,
        in_specs=in_specs,
        out_specs=out_specs or jax.tree.map(lambda _: VMEM, out_shape),
        out_shape=out_shape,
        scratch_shapes=scratch,
        name=name,
        cost_estimate=pl.CostEstimate(
            flops=COST[name] * 10**9, transcendentals=0, bytes_accessed=4 * 10**6
        ),
        compiler_params=pltpu.CompilerParams(vmem_limit_bytes=VMEM_LIMIT),
    )


def in_hbm(value):
    return pltpu.with_memory_space_constraint(value, pltpu.HBM)


def swapped(value, axis, bit):
    mask = 2**bit
    pairs = [(source, source ^ mask) for source in range(lax.axis_size(axis))]
    return lax.ppermute(value, axis, pairs)


def per_device(
    stream, depth_field, obs_col, obs_val, obs_weight, log_weight, target, spectrum, noise_coef,
    selection,
):
    _, rows, columns = stream.shape
    per_row = obs_col.shape[1]
    modes_here, n_modes = spectrum.shape
    bands = lax.axis_size("space")
    particles = lax.axis_size("particle")
    y_table = table(rows * bands, n_modes // 2)
    tt_all = jnp.asarray(np.ascontiguousarray(y_table.T))
    ht_all = jnp.asarray(halo_table(y_table, bands))
    f32, bf16 = jnp.float32, jnp.bfloat16
    shape = jax.ShapeDtypeStruct
    groups = [[g * GROUP + i for i in range(GROUP)] for g in range(particles // GROUP)]
    slot = lax.axis_index("particle")
    meta = jnp.stack([slot, lax.axis_index("space")]).astype(jnp.int32)
    own = stream[0]
    col_t, val_t, wgt_t = obs_col.T, obs_val.T, obs_weight.T
    vmem = pltpu.VMEM
    tile = vmem((rows, LANES), f32)
    whole = vmem((rows, columns), f32)
    padded = vmem((rows + 8, columns), f32)
    small = (per_row, rows)
    dma = pltpu.SemaphoreType.DMA

    sent, col_tile, wgt_tile, tt, first, last = call(
        observe_kernel,
        [SMEM] + [HBM] * 7,
        (
            shape((GROUP, modes_here * n_modes // LANES + 32, LANES), bf16),
            shape((rows, LANES), jnp.int32),
            shape((rows, LANES), f32),
            shape((n_modes, columns), bf16),
            shape((1, columns), f32),
            shape((1, columns), f32),
        ),
        [vmem(small, jnp.int32), vmem(small, f32), vmem(small, f32),
         vmem((modes_here, n_modes), bf16), whole, vmem((16, columns), f32), tile, tile, dma((8,))],
        "observe",
    )(log_weight, *map(in_hbm, (col_t, val_t, wgt_t, noise_coef[0], own, depth_field, tt_all)))
    sent, held = lax.optimization_barrier((sent, own))
    sent = lax.all_to_all(sent, "particle", 0, 0, axis_index_groups=groups, tiled=True)
    swap = swapped(held, "particle", 0)

    send, miss, part, stay_first, stay_second = call(
        gradient_kernel,
        [SMEM, SMEM, SMEM] + [VMEM] * 6,
        (
            shape((bands * 10, LANES), bf16),
            shape((rows + 8, LANES), f32),
            shape((8, LANES), f32),
            shape((1, columns), f32),
            shape((1, columns), f32),
        ),
        [whole, vmem((bands * 10, LANES), f32)],
        "gradient",
    )(meta, selection, target, col_tile, wgt_tile, sent, tt, first, last)
    send = send.reshape(bands, 5, 2, LANES)
    col_modes = lax.all_to_all(send, "space", 0, 0, tiled=True).reshape(bands * 10, LANES)

    near = jnp.where(stay_first > 0.0, own, swap)
    far = swapped(near, "particle", 1)
    col_modes, near = lax.optimization_barrier((col_modes, near))

    send = call(
        spectral_kernel,
        [SMEM, SMEM, VMEM, VMEM, VMEM, VMEM, VMEM, VMEM],
        shape((bands * (modes_here + 4), LANES), bf16),
        [vmem((bands * (modes_here + 4), LANES), f32), vmem((bands * 10, LANES), f32)],
        "spectral",
    )(meta, selection, col_modes, sent, spectrum, part, tt, ht_all)
    send = send.reshape(bands, modes_here // 2 + 2, 2, LANES)
    band_modes = lax.all_to_all(send, "space", 0, 0, tiled=True)
    band_modes = band_modes.reshape(bands * (modes_here + 4), LANES)

    field, part = call(
        relax_kernel,
        [VMEM, VMEM, VMEM, HBM, VMEM, VMEM],
        (shape((rows, columns), f32), shape((bands, 1, LANES), f32)),
        [vmem((bands * (modes_here + 4), LANES), f32), tile, padded, padded, padded, whole, dma(())],
        "relax",
    )(col_tile, wgt_tile, miss, in_hbm(depth_field), band_modes, tt)
    parts = lax.all_to_all(part, "space", 0, 0, tiled=True)
    analysis = field + jnp.where(stay_second > 0.0, near, far)
    parts, analysis = lax.optimization_barrier((parts, analysis))
    misfit_out = jnp.sum(parts[:, 0, 0:1], axis=0)
    return analysis[None], misfit_out


def solution(mesh):
    return jax.shard_map(
        per_device,
        mesh=mesh,
        in_specs=(
            P("particle", "space", None),
            P("space", None),
            P("space", None),
            P("space", None),
            P("space", None),
            P("particle"),
            P(),
            P("space", None),
            P("particle", "space", None),
            P(),
        ),
        out_specs=(P("particle", "space", None), P("particle")),
        check_vma=False,
    )
```

```python
import math

import jax
import jax.numpy as jnp
import ml_dtypes
import numpy as np
from jax import lax
from jax.experimental import pallas as pl
from jax.experimental.pallas import tpu as pltpu
from jax.sharding import PartitionSpec as P

STRETCH = 0.05
RELAX_RATE = 0.8
NOISE_AMP = 0.3
LANES = 128
GROUP = 4
VMEM_LIMIT = 48 * 1024 * 1024


def table(extent, half_modes):
    cell = np.arange(extent, dtype=np.int64)[:, None]
    freq = np.arange(half_modes + 1, dtype=np.int64)[None, :]
    angles = (cell * freq % extent).astype(np.float64) * (2.0 * math.pi / extent)
    return np.concatenate([np.cos(angles), np.sin(angles[:, 1:half_modes])], axis=1).astype(
        ml_dtypes.bfloat16
    )


def halo_table(y_table, bands):
    rows = y_table.shape[0]
    width = rows // bands
    out = np.zeros((4, bands, y_table.shape[1]), dtype=y_table.dtype)
    for band in range(bands):
        for at, row in enumerate((width, width + 1, -2, -1)):
            source = band * width + row
            if 0 <= source < rows:
                out[at, band] = y_table[source]
    return out.reshape(bands * 4, y_table.shape[1])


def lane_iota():
    return lax.broadcasted_iota(jnp.int32, (8, LANES), 1)


def parity_sign(shape, axis):
    place = lax.broadcasted_iota(jnp.int32, shape, axis)
    return (1 - 2 * (place & 1)).astype(jnp.float32)


def summed(values):
    return jnp.sum(jnp.sum(values, axis=0, keepdims=True), axis=1, keepdims=True)


def split2(value):
    high = value.astype(jnp.bfloat16).astype(jnp.float32)
    return high, value - high


def split3(value):
    high = value.astype(jnp.bfloat16).astype(jnp.float32)
    rest = value - high
    mid = rest.astype(jnp.bfloat16).astype(jnp.float32)
    return high, mid, rest - mid


def source_slot(sel_ref, meta_ref):
    slot = meta_ref[0]
    one = jnp.where(sel_ref[1, slot] < 1, slot, slot ^ 2)
    return jnp.where(sel_ref[0, one] < 1, one, one ^ 1)


def fill_tile(source_ref, scr):
    per_row = source_ref.shape[0]
    scr[...] = jnp.zeros(scr.shape, scr.dtype)
    scr[:, 0:per_row] = source_ref[...].T


def gather_rows(field_ref, col_scr, seen_scr):
    rows, columns = field_ref.shape
    for at in range(0, rows, 8):
        cols = col_scr[at : at + 8, :]
        high, low = cols >> 7, cols & 127
        seen = jnp.zeros((8, LANES), jnp.float32)
        for chunk in range(columns // LANES):
            here = field_ref[at : at + 8, chunk * LANES : (chunk + 1) * LANES]
            got = jnp.take_along_axis(here, low, axis=1, mode="promise_in_bounds")
            seen = jnp.where(high == chunk, got, seen)
        seen_scr[at : at + 8, :] = seen


def packed(tile, per_row):
    lane = lane_iota()
    out = tile[0:8, :]
    for group in range(1, tile.shape[0] // 8):
        rolled = pltpu.roll(tile[group * 8 : group * 8 + 8, :], group * per_row, axis=1)
        out = jnp.where(lane // per_row == group, rolled, out)
    return out


def observe_kernel(
    lw_ref, col_hbm, val_hbm, wgt_hbm, noise_hbm, stream_hbm, depth_hbm, tt_hbm,
    out_ref, col_scr, wgt_scr, tt_ref, first_ref, last_ref,
    col_ref, val_ref, wgt_ref, noise_ref, stream_ref, depth_ref, val_scr, seen_scr, sems,
):
    rows = depth_hbm.shape[0]
    pairs = (
        (col_hbm, col_ref),
        (val_hbm, val_ref),
        (stream_hbm, stream_ref),
        (noise_hbm, noise_ref),
        (wgt_hbm, wgt_ref),
        (depth_hbm.at[0:8, :], depth_ref.at[0:8, :]),
        (depth_hbm.at[rows - 8 : rows, :], depth_ref.at[8:16, :]),
        (tt_hbm, tt_ref),
    )
    loads = [pltpu.make_async_copy(a, b, sems.at[at]) for at, (a, b) in enumerate(pairs)]
    for load in loads:
        load.start()
    per_row = col_ref.shape[0]
    modes_here, n_modes = noise_ref.shape
    loads[0].wait()
    loads[1].wait()
    fill_tile(col_ref, col_scr)
    fill_tile(val_ref, val_scr)
    loads[2].wait()
    gather_rows(stream_ref, col_scr, seen_scr)
    mismatch = packed(val_scr[...] - seen_scr[...], per_row)
    weight = jnp.full((8, LANES), lw_ref[0], jnp.float32)
    row = lax.broadcasted_iota(jnp.int32, (8, LANES), 0)
    high, mid, low = split3(weight)
    weight = jnp.where(row == 0, high, jnp.where(row == 1, mid, jnp.where(row == 2, low, 0.0)))
    values = jnp.concatenate(list(split3(mismatch)) + [weight], axis=0).astype(jnp.bfloat16)
    loads[4].wait()
    fill_tile(wgt_ref, wgt_scr)
    loads[3].wait()
    noise = noise_ref[...]
    chunks = n_modes // LANES
    for peer in range(GROUP):
        for chunk in range(chunks):
            out_ref[peer, chunk * modes_here : (chunk + 1) * modes_here, :] = noise[
                :, chunk * LANES : (chunk + 1) * LANES
            ]
        out_ref[peer, chunks * modes_here :, :] = values
    loads[5].wait()
    loads[6].wait()
    first_ref[...] = depth_ref[0:1, :]
    last_ref[...] = depth_ref[15:16, :]
    loads[7].wait()


def gradient_kernel(
    meta_ref, sel_ref, target_ref, col_scr, wgt_scr, seen_ref, tt_ref, top_ref, bottom_ref,
    send_ref, miss_ref, part_ref, first_ref, second_ref, grad_scr, pack_scr,
):
    rows = grad_scr.shape[0]
    per_row = LANES * 8 // rows
    columns = 2 * tt_ref.shape[1]
    position = source_slot(sel_ref, meta_ref) & (GROUP - 1)
    first = seen_ref.shape[1] - 32
    sent = seen_ref[position][first:, :].astype(jnp.float32)
    mismatch = sent[0:8] + sent[8:16] + sent[16:24]
    weight = sent[24:25] + sent[25:26] + sent[26:27] - target_ref[0]
    slot = meta_ref[0]
    for section, stay_ref in enumerate((first_ref, second_ref)):
        stay = jnp.where(sel_ref[section, slot] < 1, 1.0, 0.0)
        stay_ref[...] = jnp.full(stay_ref.shape, stay, jnp.float32)
    miss_ref[rows:, :] = jnp.broadcast_to(weight, (8, LANES))
    tiles = [mismatch] + [
        pltpu.roll(mismatch, LANES - group * per_row, axis=1) for group in range(1, rows // 8)
    ]
    mismatch = jnp.concatenate(tiles, axis=0)
    miss_ref[0:rows, :] = mismatch
    weighted = wgt_scr[...] * mismatch
    part_ref[...] = jnp.broadcast_to(0.5 * summed(weighted * mismatch), (8, LANES))

    def repeated(tile):
        step = per_row
        while step < LANES:
            tile = tile + pltpu.roll(tile, step, axis=1)
            step *= 2
        return tile

    diagonal = lane_iota() // per_row == lax.broadcasted_iota(jnp.int32, (8, LANES), 0)
    row_f = lax.broadcasted_iota(jnp.int32, (LANES, LANES), 0).astype(jnp.float32)
    for group in range(rows // 8):
        at = group * 8
        cols = repeated(col_scr[at : at + 8, :])
        high = jnp.where(diagonal, cols >> 7, -1)
        low = jnp.sum(
            jnp.where(diagonal, (cols & 127).astype(jnp.float32), 0.0), axis=0, keepdims=True
        )
        one_hot = jnp.where(row_f == low, 1.0, 0.0).astype(jnp.bfloat16)
        left = []
        for piece in split3(repeated(weighted[at : at + 8, :])):
            left.append(
                jnp.concatenate(
                    [jnp.where(high == chunk, piece, 0.0) for chunk in range(columns // LANES)], axis=0
                ).astype(jnp.bfloat16)
            )
        spread = lax.dot_general(
            jnp.concatenate(left, axis=1),
            jnp.concatenate([one_hot] * 3, axis=1),
            (((1,), (1,)), ((), ())),
            preferred_element_type=jnp.float32,
        )
        for chunk in range(columns // LANES):
            grad_scr[at : at + 8, chunk * LANES : (chunk + 1) * LANES] = spread[
                chunk * 8 : chunk * 8 + 8, :
            ]
    gradient = grad_scr[...].astype(jnp.bfloat16)
    gradient = jnp.concatenate([gradient[:, : columns // 2], gradient[:, columns // 2 :]], axis=0)
    modes = lax.dot_general(
        tt_ref[...], gradient, (((1,), (1,)), ((), ())), preferred_element_type=jnp.float32
    )
    half = LANES // 2
    bands = modes.shape[0] // 16
    block = send_ref.shape[0] // bands
    modes = modes + parity_sign(modes.shape, 0) * pltpu.roll(modes, half, axis=1)
    split = modes.reshape(bands, 2, 8, LANES)
    small = (bands, 8, LANES)
    values = jnp.where(
        lax.broadcasted_iota(jnp.int32, small, 2) < half,
        split[:, 0],
        parity_sign(small, 1) * split[:, 1],
    )
    pairs = columns // LANES
    top, bottom = (
        jnp.concatenate(
            [ref[:, pair * LANES : (pair + 1) * LANES] for pair in range(pairs)], axis=0
        )
        for ref in (top_ref, bottom_ref)
    )
    low = lax.broadcasted_iota(jnp.int32, (pairs, LANES), 1) < half
    even = split2(jnp.where(low, top, pltpu.roll(bottom, half, axis=1)))
    odd = split2(jnp.where(low, pltpu.roll(top, half, axis=1), bottom))
    for band in range(bands):
        at = band * block
        pack_scr[at : at + 8, :] = values[band]
        for piece in range(2):
            row = (odd if band % 2 else even)[piece][band // 2 : band // 2 + 1]
            pack_scr[at + 8 + piece : at + 9 + piece, :] = row
    send_ref[...] = pack_scr[...].astype(jnp.bfloat16)


def spectral_kernel(
    meta_ref, sel_ref, modes_ref, noise_ref, spec_ref, part_ref, tt_ref, ht_ref, send_ref, pack_scr,
    unpack_scr,
):
    half = LANES // 2
    modes_here, n_modes = spec_ref.shape
    bands = n_modes // modes_here
    unpack_scr[...] = modes_ref[...].astype(jnp.float32)
    rows = 2 * tt_ref.shape[1]
    norm_factor = 4.0 / (rows * rows)
    position = source_slot(sel_ref, meta_ref) & (GROUP - 1)
    lane = lane_iota()
    low = lane < half
    tops, bottoms = [], []
    for pair in range(bands // 2):
        even = unpack_scr[20 * pair : 20 * pair + 8, :]
        odd = unpack_scr[20 * pair + 10 : 20 * pair + 18, :]
        tops.append(jnp.where(low, even, pltpu.roll(odd, half, axis=1)))
        bottoms.append(jnp.where(low, pltpu.roll(even, half, axis=1), odd))
    folded = bands // 4
    columns = jnp.concatenate(
        [
            jnp.concatenate(part, axis=1)
            for part in (tops[:folded], bottoms[:folded], tops[folded:], bottoms[folded:])
        ],
        axis=0,
    ).astype(jnp.bfloat16)
    sums = lax.dot_general(
        columns, tt_ref[...], (((1,), (1,)), ((), ())), preferred_element_type=jnp.float32
    )
    coefficients = sums[:modes_here] + parity_sign(spec_ref.shape, 1) * sums[modes_here:]
    scaled = norm_factor * spec_ref[...]
    weighted = coefficients * scaled
    energy = summed(coefficients * weighted)
    noise = noise_ref[position][0 : noise_ref.shape[1] - 32, :]
    noise = jnp.concatenate(
        [noise[at : at + modes_here] for at in range(0, noise.shape[0], modes_here)], axis=1
    )
    shaped = (jnp.sqrt(scaled) * noise.astype(jnp.float32)).astype(jnp.bfloat16)
    weighted = weighted.astype(jnp.bfloat16)
    stacked = jnp.concatenate([weighted, shaped], axis=0)
    flipped = stacked.astype(jnp.float32) * parity_sign(stacked.shape, 1)
    both = jnp.concatenate([stacked, flipped.astype(jnp.bfloat16)], axis=0)
    inverted = jnp.dot(both, tt_ref[...], preferred_element_type=jnp.float32)
    inverted = jnp.concatenate(
        [inverted[: 2 * modes_here], inverted[2 * modes_here :]], axis=1
    )
    depth = sum(unpack_scr[pl.ds(8 + piece, bands, stride=10), :] for piece in range(2))
    band_row = lax.broadcasted_iota(jnp.int32, (bands, LANES), 0)
    band_low = lax.broadcasted_iota(jnp.int32, (bands, LANES), 1) < half
    above = jnp.where(band_row > 0, pltpu.roll(depth, 1, axis=0), 0.0)
    below = jnp.where(band_row < bands - 1, pltpu.roll(depth, bands - 1, axis=0), 0.0)
    beside = split2(pltpu.roll(jnp.where(band_low, below, above), half, axis=1))
    block = modes_here + 4
    low16 = lax.broadcasted_iota(jnp.int32, (modes_here, LANES), 1) < half
    for pair in range(bands // 2):
        first = inverted[0:modes_here, pair * LANES : (pair + 1) * LANES]
        second = inverted[modes_here:, pair * LANES : (pair + 1) * LANES]
        at = 2 * pair * block
        pack_scr[at : at + modes_here, :] = jnp.where(
            low16, first, pltpu.roll(second, half, axis=1)
        )
        at += block
        pack_scr[at : at + modes_here, :] = jnp.where(
            low16, pltpu.roll(first, half, axis=1), second
        )
    halo = lax.dot_general(
        ht_ref[...], stacked, (((1,), (1,)), ((), ())), preferred_element_type=jnp.float32
    )
    halo = jnp.concatenate(
        [halo, jnp.zeros((4 * bands, LANES - 2 * modes_here), jnp.float32)], axis=1
    )
    window = lax.broadcasted_iota(jnp.int32, (bands, LANES), 1) // modes_here
    edges = jnp.zeros((bands, LANES), jnp.float32)
    for at in range(8):
        field, row = at // 4, at % 4
        shift = (at - field) * modes_here % LANES
        value = halo[row * bands : (row + 1) * bands]
        edges = jnp.where(window == at, pltpu.roll(value, shift, axis=1) if shift else value, edges)
    lane1 = lax.broadcasted_iota(jnp.int32, (1, LANES), 1)
    pieces = jnp.zeros((1, LANES), jnp.float32)
    for at, piece in enumerate(split3(part_ref[0:1, 0:1]) + split3(energy)):
        pieces = jnp.where(lane1 == at, piece, pieces)
    for band in range(bands):
        at = band * block + modes_here
        pack_scr[at : at + 1, :] = edges[band : band + 1]
        pack_scr[at + 1 : at + 2, :] = pieces
        for piece in range(2):
            pack_scr[at + 2 + piece : at + 3 + piece, :] = beside[piece][band : band + 1]
    send_ref[...] = pack_scr[...].astype(jnp.bfloat16)


def relax_kernel(
    col_scr, wgt_scr, miss_ref, depth_hbm, modes_ref, tt_ref,
    field_ref, part_ref, unpack_scr, seen_scr, inc_scr, one_scr, rate_ref, depth_ref,
    sem,
):
    depth = pltpu.make_async_copy(depth_hbm, depth_ref, sem)
    depth.start()
    rows = depth_ref.shape[0]

    def rate(depth):
        return RELAX_RATE * depth / (4.0 * depth + STRETCH)

    n_modes, columns = tt_ref.shape[0], 2 * tt_ref.shape[1]
    bands = part_ref.shape[0]
    modes_here = n_modes // bands
    lane = lane_iota()
    block = modes_here + 4
    unpack_scr[...] = modes_ref[...].astype(jnp.float32)
    edges = unpack_scr[pl.ds(modes_here, bands, stride=block), :]
    scalars = unpack_scr[pl.ds(modes_here + 1, bands, stride=block), :]
    row = lax.broadcasted_iota(jnp.int32, (8, LANES), 0)
    window = lane // modes_here
    quads = []
    for quad in range(0, bands, 8):
        tile = edges[quad : quad + 8]
        for bit in (1, 2, 4):
            up = pltpu.roll(pltpu.roll(tile, 8 - bit, axis=0), bit * modes_here, axis=1)
            down = pltpu.roll(pltpu.roll(tile, bit, axis=0), LANES - bit * modes_here, axis=1)
            upper, later = (row & bit) == 0, (window & bit) == 0
            tile = jnp.where(upper == later, tile, jnp.where(upper, up, down))
        quads.append(tile)
    halo = jnp.concatenate(quads, axis=1)
    lanes = lax.broadcasted_iota(jnp.int32, scalars.shape, 1)
    misfit = summed(jnp.where(lanes < 3, scalars, 0.0))
    energy = summed(jnp.where((lanes >= 3) & (lanes < 6), scalars, 0.0))
    weight = miss_ref[rows : rows + 1, 0:1]
    step = (misfit + weight) / (energy + 1.0)
    main = jnp.concatenate(
        [unpack_scr[at * block : at * block + modes_here, :] for at in range(bands)], axis=0
    )
    both = jnp.concatenate([main, main * parity_sign(main.shape, 0)], axis=1)
    pulled = lax.dot_general(
        both.astype(jnp.bfloat16),
        tt_ref[...],
        (((0,), (0,)), ((), ())),
        preferred_element_type=jnp.float32,
    )
    pulled = jnp.concatenate([pulled[:LANES], pulled[LANES:]], axis=1)
    both = jnp.concatenate([halo, halo * parity_sign(halo.shape, 1)], axis=0)
    pulled_h = jnp.dot(
        both.astype(jnp.bfloat16), tt_ref[...], preferred_element_type=jnp.float32
    )
    pulled_h = jnp.concatenate([pulled_h[:8], pulled_h[8:]], axis=1)
    for at in range(0, rows, 8):
        inc_scr[at : at + 8, :] = step * pulled[at : at + 8] + NOISE_AMP * pulled[rows + at : rows + at + 8]
    edge = pulled_h
    edge = step * edge + NOISE_AMP * pltpu.roll(edge, 4, axis=0)
    row8 = lax.broadcasted_iota(jnp.int32, (8, columns), 0)
    inc_scr[rows:, :] = jnp.where(row8 < 2, edge, jnp.where(row8 < 6, 0.0, pltpu.roll(edge, 4, axis=0)))
    depth.wait()

    def rate(depth):
        return RELAX_RATE * depth / (4.0 * depth + STRETCH)

    even, odd = (
        sum(
            unpack_scr[pl.ds(start + piece, bands // 2, stride=2 * block), :] for piece in range(2)
        )
        for start in (modes_here + 2, modes_here + 2 + block)
    )
    half = LANES // 2
    low = lax.broadcasted_iota(jnp.int32, (bands // 2, LANES), 1) < half
    above = rate(jnp.where(low, even, pltpu.roll(odd, half, axis=1)))
    below = rate(jnp.where(low, pltpu.roll(even, half, axis=1), odd))
    for pair in range(bands // 2):
        rate_ref[rows:, pair * LANES : (pair + 1) * LANES] = jnp.where(
            row == 0,
            below[pair : pair + 1],
            jnp.where(row == 7, above[pair : pair + 1], 0.0),
        )
    for at in range(0, rows, 8):
        rate_ref[at : at + 8, :] = rate(depth_ref[at : at + 8, :])
    length = rows + 8

    def relaxed(source_ref, at):
        here = source_ref[at : at + 8, :]
        before = source_ref[(at - 8) % length : (at - 8) % length + 8, :]
        after = source_ref[(at + 8) % length : (at + 8) % length + 8, :]
        around = (
            pltpu.roll(jnp.where(row8 == 7, before, here), 1, axis=0)
            + pltpu.roll(jnp.where(row8 == 0, after, here), 7, axis=0)
            + pltpu.roll(here, 1, axis=1)
            + pltpu.roll(here, columns - 1, axis=1)
        )
        return (1.0 - RELAX_RATE) * here + rate_ref[at : at + 8, :] * (
            around - inc_scr[at : at + 8, :]
        )

    for at in range(0, length, 8):
        one_scr[at : at + 8, :] = relaxed(inc_scr, at)
    for at in range(0, rows, 8):
        field_ref[at : at + 8, :] = relaxed(one_scr, at)
    gather_rows(field_ref, col_scr, seen_scr)
    left_over = miss_ref[0:rows, :] - seen_scr[...]
    part = 0.5 * summed(wgt_scr[...] * left_over * left_over)
    part_ref[...] = jnp.broadcast_to(part[None], part_ref.shape)


SMEM = pl.BlockSpec(memory_space=pltpu.SMEM)
VMEM = pl.BlockSpec(memory_space=pltpu.VMEM)
HBM = pl.BlockSpec(memory_space=pltpu.HBM)


COST = {"observe": 40, "gradient": 40, "spectral": 1, "relax": 1}


def call(kernel, in_specs, out_shape, scratch, name, out_specs=None):
    return pl.pallas_call(
        kernel,
        in_specs=in_specs,
        out_specs=out_specs or jax.tree.map(lambda _: VMEM, out_shape),
        out_shape=out_shape,
        scratch_shapes=scratch,
        name=name,
        cost_estimate=pl.CostEstimate(
            flops=COST[name] * 10**9, transcendentals=0, bytes_accessed=4 * 10**6
        ),
        compiler_params=pltpu.CompilerParams(vmem_limit_bytes=VMEM_LIMIT),
    )


def in_hbm(value):
    return pltpu.with_memory_space_constraint(value, pltpu.HBM)


def swapped(value, axis, bit):
    mask = 2**bit
    pairs = [(source, source ^ mask) for source in range(lax.axis_size(axis))]
    return lax.ppermute(value, axis, pairs)


def per_device(
    stream, depth_field, obs_col, obs_val, obs_weight, log_weight, target, spectrum, noise_coef,
    selection,
):
    _, rows, columns = stream.shape
    per_row = obs_col.shape[1]
    modes_here, n_modes = spectrum.shape
    bands = lax.axis_size("space")
    particles = lax.axis_size("particle")
    y_table = table(rows * bands, n_modes // 2)
    tt_all = jnp.asarray(np.ascontiguousarray(y_table[: columns // 2].T))
    ht_all = jnp.asarray(halo_table(y_table, bands))
    f32, bf16 = jnp.float32, jnp.bfloat16
    shape = jax.ShapeDtypeStruct
    groups = [[g * GROUP + i for i in range(GROUP)] for g in range(particles // GROUP)]
    slot = lax.axis_index("particle")
    meta = jnp.stack([slot, lax.axis_index("space")]).astype(jnp.int32)
    own = stream[0]
    col_t, val_t, wgt_t = obs_col.T, obs_val.T, obs_weight.T
    vmem = pltpu.VMEM
    tile = vmem((rows, LANES), f32)
    whole = vmem((rows, columns), f32)
    padded = vmem((rows + 8, columns), f32)
    small = (per_row, rows)
    dma = pltpu.SemaphoreType.DMA

    sent, col_tile, wgt_tile, tt, first, last = call(
        observe_kernel,
        [SMEM] + [HBM] * 7,
        (
            shape((GROUP, modes_here * n_modes // LANES + 32, LANES), bf16),
            shape((rows, LANES), jnp.int32),
            shape((rows, LANES), f32),
            shape((n_modes, columns // 2), bf16),
            shape((1, columns), f32),
            shape((1, columns), f32),
        ),
        [vmem(small, jnp.int32), vmem(small, f32), vmem(small, f32),
         vmem((modes_here, n_modes), bf16), whole, vmem((16, columns), f32), tile, tile, dma((8,))],
        "observe",
    )(log_weight, *map(in_hbm, (col_t, val_t, wgt_t, noise_coef[0], own, depth_field, tt_all)))
    sent, held = lax.optimization_barrier((sent, own))
    sent = lax.all_to_all(sent, "particle", 0, 0, axis_index_groups=groups, tiled=True)
    swap = swapped(held, "particle", 0)

    send, miss, part, stay_first, stay_second = call(
        gradient_kernel,
        [SMEM, SMEM, SMEM] + [VMEM] * 6,
        (
            shape((bands * 10, LANES), bf16),
            shape((rows + 8, LANES), f32),
            shape((8, LANES), f32),
            shape((1, columns), f32),
            shape((1, columns), f32),
        ),
        [whole, vmem((bands * 10, LANES), f32)],
        "gradient",
    )(meta, selection, target, col_tile, wgt_tile, sent, tt, first, last)
    send = send.reshape(bands, 5, 2, LANES)
    col_modes = lax.all_to_all(send, "space", 0, 0, tiled=True).reshape(bands * 10, LANES)

    near = jnp.where(stay_first > 0.0, own, swap)
    far = swapped(near, "particle", 1)
    col_modes, near = lax.optimization_barrier((col_modes, near))

    send = call(
        spectral_kernel,
        [SMEM, SMEM, VMEM, VMEM, VMEM, VMEM, VMEM, VMEM],
        shape((bands * (modes_here + 4), LANES), bf16),
        [vmem((bands * (modes_here + 4), LANES), f32), vmem((bands * 10, LANES), f32)],
        "spectral",
    )(meta, selection, col_modes, sent, spectrum, part, tt, ht_all)
    send = send.reshape(bands, modes_here // 2 + 2, 2, LANES)
    band_modes = lax.all_to_all(send, "space", 0, 0, tiled=True)
    band_modes = band_modes.reshape(bands * (modes_here + 4), LANES)

    field, part = call(
        relax_kernel,
        [VMEM, VMEM, VMEM, HBM, VMEM, VMEM],
        (shape((rows, columns), f32), shape((bands, 1, LANES), f32)),
        [vmem((bands * (modes_here + 4), LANES), f32), tile, padded, padded, padded, whole, dma(())],
        "relax",
    )(col_tile, wgt_tile, miss, in_hbm(depth_field), band_modes, tt)
    parts = lax.all_to_all(part, "space", 0, 0, tiled=True)
    analysis = field + jnp.where(stay_second > 0.0, near, far)
    parts, analysis = lax.optimization_barrier((parts, analysis))
    misfit_out = jnp.sum(parts[:, 0, 0:1], axis=0)
    return analysis[None], misfit_out


def solution(mesh):
    return jax.shard_map(
        per_device,
        mesh=mesh,
        in_specs=(
            P("particle", "space", None),
            P("space", None),
            P("space", None),
            P("space", None),
            P("space", None),
            P("particle"),
            P(),
            P("space", None),
            P("particle", "space", None),
            P(),
        ),
        out_specs=(P("particle", "space", None), P("particle")),
        check_vma=False,
    )
```

```python
import math

import jax
import jax.numpy as jnp
import ml_dtypes
import numpy as np
from jax import lax
from jax.experimental import pallas as pl
from jax.experimental.pallas import tpu as pltpu
from jax.sharding import PartitionSpec as P

STRETCH = 0.05
RELAX_RATE = 0.8
NOISE_AMP = 0.3
LANES = 128
GROUP = 4
VMEM_LIMIT = 48 * 1024 * 1024


def table(extent, half_modes):
    cell = np.arange(extent, dtype=np.int64)[:, None]
    freq = np.arange(half_modes + 1, dtype=np.int64)[None, :]
    angles = (cell * freq % extent).astype(np.float64) * (2.0 * math.pi / extent)
    return np.concatenate([np.cos(angles), np.sin(angles[:, 1:half_modes])], axis=1).astype(
        ml_dtypes.bfloat16
    )


def halo_table(y_table, bands):
    rows = y_table.shape[0]
    width = rows // bands
    out = np.zeros((4, bands, y_table.shape[1]), dtype=y_table.dtype)
    for band in range(bands):
        for at, row in enumerate((width, width + 1, -2, -1)):
            source = band * width + row
            if 0 <= source < rows:
                out[at, band] = y_table[source]
    return out.reshape(bands * 4, y_table.shape[1])


def lane_iota():
    return lax.broadcasted_iota(jnp.int32, (8, LANES), 1)


def parity_sign(shape, axis):
    place = lax.broadcasted_iota(jnp.int32, shape, axis)
    return (1 - 2 * (place & 1)).astype(jnp.float32)


def summed(values):
    return jnp.sum(jnp.sum(values, axis=0, keepdims=True), axis=1, keepdims=True)


def split2(value):
    high = value.astype(jnp.bfloat16).astype(jnp.float32)
    return high, value - high


def split3(value):
    high = value.astype(jnp.bfloat16).astype(jnp.float32)
    rest = value - high
    mid = rest.astype(jnp.bfloat16).astype(jnp.float32)
    return high, mid, rest - mid


def chosen(info_ref, section, slot):
    per_section = (info_ref.shape[0] - 2) // 2
    return info_ref[2 + section * per_section + slot]


def source_slot(info_ref):
    slot = info_ref[0]
    one = jnp.where(chosen(info_ref, 1, slot) < 1, slot, slot ^ 2)
    return jnp.where(chosen(info_ref, 0, one) < 1, one, one ^ 1)


def fill_tile(source_ref, scr):
    per_row = source_ref.shape[0]
    scr[...] = jnp.zeros(scr.shape, scr.dtype)
    scr[:, 0:per_row] = source_ref[...].T


def gather_rows(field_ref, col_scr, seen_scr):
    rows, columns = field_ref.shape
    for at in range(0, rows, 8):
        cols = col_scr[at : at + 8, :]
        high, low = cols >> 7, cols & 127
        seen = jnp.zeros((8, LANES), jnp.float32)
        for chunk in range(columns // LANES):
            here = field_ref[at : at + 8, chunk * LANES : (chunk + 1) * LANES]
            got = jnp.take_along_axis(here, low, axis=1, mode="promise_in_bounds")
            seen = jnp.where(high == chunk, got, seen)
        seen_scr[at : at + 8, :] = seen


def packed(tile, per_row):
    lane = lane_iota()
    out = tile[0:8, :]
    for group in range(1, tile.shape[0] // 8):
        rolled = pltpu.roll(tile[group * 8 : group * 8 + 8, :], group * per_row, axis=1)
        out = jnp.where(lane // per_row == group, rolled, out)
    return out


def observe_kernel(
    lw_ref, col_hbm, val_hbm, wgt_hbm, noise_hbm, stream_hbm, depth_hbm, tt_hbm,
    out_ref, col_scr, wgt_scr, tt_ref, first_ref, last_ref,
    col_ref, val_ref, wgt_ref, noise_ref, stream_ref, depth_ref, val_scr, seen_scr, sems,
):
    rows = depth_hbm.shape[0]
    pairs = (
        (col_hbm, col_ref),
        (val_hbm, val_ref),
        (stream_hbm, stream_ref),
        (noise_hbm, noise_ref),
        (wgt_hbm, wgt_ref),
        (depth_hbm.at[0:8, :], depth_ref.at[0:8, :]),
        (depth_hbm.at[rows - 8 : rows, :], depth_ref.at[8:16, :]),
        (tt_hbm, tt_ref),
    )
    loads = [pltpu.make_async_copy(a, b, sems.at[at]) for at, (a, b) in enumerate(pairs)]
    for load in loads:
        load.start()
    per_row = col_ref.shape[0]
    modes_here, n_modes = noise_ref.shape
    loads[0].wait()
    loads[1].wait()
    fill_tile(col_ref, col_scr)
    fill_tile(val_ref, val_scr)
    loads[2].wait()
    gather_rows(stream_ref, col_scr, seen_scr)
    mismatch = packed(val_scr[...] - seen_scr[...], per_row)
    weight = jnp.full((8, LANES), lw_ref[0], jnp.float32)
    row = lax.broadcasted_iota(jnp.int32, (8, LANES), 0)
    high, mid, low = split3(weight)
    weight = jnp.where(row == 0, high, jnp.where(row == 1, mid, jnp.where(row == 2, low, 0.0)))
    values = jnp.concatenate(list(split3(mismatch)) + [weight], axis=0).astype(jnp.bfloat16)
    loads[4].wait()
    fill_tile(wgt_ref, wgt_scr)
    loads[3].wait()
    noise = noise_ref[...]
    chunks = n_modes // LANES
    for peer in range(GROUP):
        for chunk in range(chunks):
            out_ref[peer, chunk * modes_here : (chunk + 1) * modes_here, :] = noise[
                :, chunk * LANES : (chunk + 1) * LANES
            ]
        out_ref[peer, chunks * modes_here :, :] = values
    loads[5].wait()
    loads[6].wait()
    first_ref[...] = depth_ref[0:1, :]
    last_ref[...] = depth_ref[15:16, :]
    loads[7].wait()


def gradient_kernel(
    info_ref, target_ref, col_scr, wgt_scr, seen_ref, tt_ref, top_ref, bottom_ref,
    send_ref, miss_ref, part_ref, first_ref, second_ref, grad_scr, pack_scr,
):
    rows = grad_scr.shape[0]
    per_row = LANES * 8 // rows
    columns = 2 * tt_ref.shape[1]
    position = source_slot(info_ref) & (GROUP - 1)
    first = seen_ref.shape[1] - 32
    sent = seen_ref[position][first:, :].astype(jnp.float32)
    mismatch = sent[0:8] + sent[8:16] + sent[16:24]
    weight = sent[24:25] + sent[25:26] + sent[26:27] - target_ref[0]
    slot = info_ref[0]
    for section, stay_ref in enumerate((first_ref, second_ref)):
        stay = jnp.where(chosen(info_ref, section, slot) < 1, 1.0, 0.0)
        stay_ref[...] = jnp.full(stay_ref.shape, stay, jnp.float32)
    miss_ref[rows:, :] = jnp.broadcast_to(weight, (8, LANES))
    tiles = [mismatch] + [
        pltpu.roll(mismatch, LANES - group * per_row, axis=1) for group in range(1, rows // 8)
    ]
    mismatch = jnp.concatenate(tiles, axis=0)
    miss_ref[0:rows, :] = mismatch
    weighted = wgt_scr[...] * mismatch
    part_ref[...] = jnp.broadcast_to(0.5 * summed(weighted * mismatch), (8, LANES))

    def repeated(tile):
        step = per_row
        while step < LANES:
            tile = tile + pltpu.roll(tile, step, axis=1)
            step *= 2
        return tile

    diagonal = lane_iota() // per_row == lax.broadcasted_iota(jnp.int32, (8, LANES), 0)
    row_f = lax.broadcasted_iota(jnp.int32, (LANES, LANES), 0).astype(jnp.float32)
    for group in range(rows // 8):
        at = group * 8
        cols = repeated(col_scr[at : at + 8, :])
        high = jnp.where(diagonal, cols >> 7, -1)
        low = jnp.sum(
            jnp.where(diagonal, (cols & 127).astype(jnp.float32), 0.0), axis=0, keepdims=True
        )
        one_hot = jnp.where(row_f == low, 1.0, 0.0).astype(jnp.bfloat16)
        left = []
        for piece in split3(repeated(weighted[at : at + 8, :])):
            left.append(
                jnp.concatenate(
                    [jnp.where(high == chunk, piece, 0.0) for chunk in range(columns // LANES)], axis=0
                ).astype(jnp.bfloat16)
            )
        spread = lax.dot_general(
            jnp.concatenate(left, axis=1),
            jnp.concatenate([one_hot] * 3, axis=1),
            (((1,), (1,)), ((), ())),
            preferred_element_type=jnp.float32,
        )
        for chunk in range(columns // LANES):
            grad_scr[at : at + 8, chunk * LANES : (chunk + 1) * LANES] = spread[
                chunk * 8 : chunk * 8 + 8, :
            ]
    gradient = grad_scr[...].astype(jnp.bfloat16)
    gradient = jnp.concatenate([gradient[:, : columns // 2], gradient[:, columns // 2 :]], axis=0)
    modes = lax.dot_general(
        tt_ref[...], gradient, (((1,), (1,)), ((), ())), preferred_element_type=jnp.float32
    )
    half = LANES // 2
    bands = modes.shape[0] // 16
    block = send_ref.shape[0] // bands
    modes = modes + parity_sign(modes.shape, 0) * pltpu.roll(modes, half, axis=1)
    split = modes.reshape(bands, 2, 8, LANES)
    small = (bands, 8, LANES)
    values = jnp.where(
        lax.broadcasted_iota(jnp.int32, small, 2) < half,
        split[:, 0],
        parity_sign(small, 1) * split[:, 1],
    )
    pairs = columns // LANES
    top, bottom = (
        jnp.concatenate(
            [ref[:, pair * LANES : (pair + 1) * LANES] for pair in range(pairs)], axis=0
        )
        for ref in (top_ref, bottom_ref)
    )
    low = lax.broadcasted_iota(jnp.int32, (pairs, LANES), 1) < half
    even = split2(jnp.where(low, top, pltpu.roll(bottom, half, axis=1)))
    odd = split2(jnp.where(low, pltpu.roll(top, half, axis=1), bottom))
    for band in range(bands):
        at = band * block
        pack_scr[at : at + 8, :] = values[band]
        for piece in range(2):
            row = (odd if band % 2 else even)[piece][band // 2 : band // 2 + 1]
            pack_scr[at + 8 + piece : at + 9 + piece, :] = row
    send_ref[...] = pack_scr[...].astype(jnp.bfloat16)


def spectral_kernel(
    info_ref, modes_ref, noise_ref, spec_ref, part_ref, tt_ref, ht_ref, send_ref, pack_scr,
    unpack_scr,
):
    half = LANES // 2
    modes_here, n_modes = spec_ref.shape
    bands = n_modes // modes_here
    unpack_scr[...] = modes_ref[...].astype(jnp.float32)
    rows = 2 * tt_ref.shape[1]
    norm_factor = 4.0 / (rows * rows)
    position = source_slot(info_ref) & (GROUP - 1)
    lane = lane_iota()
    low = lane < half
    tops, bottoms = [], []
    for pair in range(bands // 2):
        even = unpack_scr[20 * pair : 20 * pair + 8, :]
        odd = unpack_scr[20 * pair + 10 : 20 * pair + 18, :]
        tops.append(jnp.where(low, even, pltpu.roll(odd, half, axis=1)))
        bottoms.append(jnp.where(low, pltpu.roll(even, half, axis=1), odd))
    folded = bands // 4
    columns = jnp.concatenate(
        [
            jnp.concatenate(part, axis=1)
            for part in (tops[:folded], bottoms[:folded], tops[folded:], bottoms[folded:])
        ],
        axis=0,
    ).astype(jnp.bfloat16)
    sums = lax.dot_general(
        columns, tt_ref[...], (((1,), (1,)), ((), ())), preferred_element_type=jnp.float32
    )
    coefficients = sums[:modes_here] + parity_sign(spec_ref.shape, 1) * sums[modes_here:]
    scaled = norm_factor * spec_ref[...]
    weighted = coefficients * scaled
    energy = summed(coefficients * weighted)
    noise = noise_ref[position][0 : noise_ref.shape[1] - 32, :]
    noise = jnp.concatenate(
        [noise[at : at + modes_here] for at in range(0, noise.shape[0], modes_here)], axis=1
    )
    shaped = (jnp.sqrt(scaled) * noise.astype(jnp.float32)).astype(jnp.bfloat16)
    weighted = weighted.astype(jnp.bfloat16)
    stacked = jnp.concatenate([weighted, shaped], axis=0)
    flipped = stacked.astype(jnp.float32) * parity_sign(stacked.shape, 1)
    both = jnp.concatenate([stacked, flipped.astype(jnp.bfloat16)], axis=0)
    inverted = jnp.dot(both, tt_ref[...], preferred_element_type=jnp.float32)
    inverted = jnp.concatenate(
        [inverted[: 2 * modes_here], inverted[2 * modes_here :]], axis=1
    )
    depth = sum(unpack_scr[pl.ds(8 + piece, bands, stride=10), :] for piece in range(2))
    band_row = lax.broadcasted_iota(jnp.int32, (bands, LANES), 0)
    band_low = lax.broadcasted_iota(jnp.int32, (bands, LANES), 1) < half
    above = jnp.where(band_row > 0, pltpu.roll(depth, 1, axis=0), 0.0)
    below = jnp.where(band_row < bands - 1, pltpu.roll(depth, bands - 1, axis=0), 0.0)
    beside = split2(pltpu.roll(jnp.where(band_low, below, above), half, axis=1))
    block = modes_here + 4
    low16 = lax.broadcasted_iota(jnp.int32, (modes_here, LANES), 1) < half
    for pair in range(bands // 2):
        first = inverted[0:modes_here, pair * LANES : (pair + 1) * LANES]
        second = inverted[modes_here:, pair * LANES : (pair + 1) * LANES]
        at = 2 * pair * block
        pack_scr[at : at + modes_here, :] = jnp.where(
            low16, first, pltpu.roll(second, half, axis=1)
        )
        at += block
        pack_scr[at : at + modes_here, :] = jnp.where(
            low16, pltpu.roll(first, half, axis=1), second
        )
    halo = lax.dot_general(
        ht_ref[...], stacked, (((1,), (1,)), ((), ())), preferred_element_type=jnp.float32
    )
    halo = jnp.concatenate(
        [halo, jnp.zeros((4 * bands, LANES - 2 * modes_here), jnp.float32)], axis=1
    )
    window = lax.broadcasted_iota(jnp.int32, (bands, LANES), 1) // modes_here
    edges = jnp.zeros((bands, LANES), jnp.float32)
    for at in range(8):
        field, row = at // 4, at % 4
        shift = (at - field) * modes_here % LANES
        value = halo[row * bands : (row + 1) * bands]
        edges = jnp.where(window == at, pltpu.roll(value, shift, axis=1) if shift else value, edges)
    lane1 = lax.broadcasted_iota(jnp.int32, (1, LANES), 1)
    pieces = jnp.zeros((1, LANES), jnp.float32)
    for at, piece in enumerate(split3(part_ref[0:1, 0:1]) + split3(energy)):
        pieces = jnp.where(lane1 == at, piece, pieces)
    for band in range(bands):
        at = band * block + modes_here
        pack_scr[at : at + 1, :] = edges[band : band + 1]
        pack_scr[at + 1 : at + 2, :] = pieces
        for piece in range(2):
            pack_scr[at + 2 + piece : at + 3 + piece, :] = beside[piece][band : band + 1]
    send_ref[...] = pack_scr[...].astype(jnp.bfloat16)


def relax_kernel(
    col_scr, wgt_scr, miss_ref, depth_hbm, modes_ref, tt_ref,
    field_ref, part_ref, unpack_scr, seen_scr, inc_scr, one_scr, rate_ref, depth_ref,
    sem,
):
    depth = pltpu.make_async_copy(depth_hbm, depth_ref, sem)
    depth.start()
    rows = depth_ref.shape[0]

    def rate(depth):
        return RELAX_RATE * depth / (4.0 * depth + STRETCH)

    n_modes, columns = tt_ref.shape[0], 2 * tt_ref.shape[1]
    bands = part_ref.shape[0]
    modes_here = n_modes // bands
    lane = lane_iota()
    block = modes_here + 4
    unpack_scr[...] = modes_ref[...].astype(jnp.float32)
    edges = unpack_scr[pl.ds(modes_here, bands, stride=block), :]
    scalars = unpack_scr[pl.ds(modes_here + 1, bands, stride=block), :]
    row = lax.broadcasted_iota(jnp.int32, (8, LANES), 0)
    window = lane // modes_here
    quads = []
    for quad in range(0, bands, 8):
        tile = edges[quad : quad + 8]
        for bit in (1, 2, 4):
            up = pltpu.roll(pltpu.roll(tile, 8 - bit, axis=0), bit * modes_here, axis=1)
            down = pltpu.roll(pltpu.roll(tile, bit, axis=0), LANES - bit * modes_here, axis=1)
            upper, later = (row & bit) == 0, (window & bit) == 0
            tile = jnp.where(upper == later, tile, jnp.where(upper, up, down))
        quads.append(tile)
    halo = jnp.concatenate(quads, axis=1)
    lanes = lax.broadcasted_iota(jnp.int32, scalars.shape, 1)
    misfit = summed(jnp.where(lanes < 3, scalars, 0.0))
    energy = summed(jnp.where((lanes >= 3) & (lanes < 6), scalars, 0.0))
    weight = miss_ref[rows : rows + 1, 0:1]
    step = (misfit + weight) / (energy + 1.0)
    main = jnp.concatenate(
        [unpack_scr[at * block : at * block + modes_here, :] for at in range(bands)], axis=0
    )
    both = jnp.concatenate([main, main * parity_sign(main.shape, 0)], axis=1)
    pulled = lax.dot_general(
        both.astype(jnp.bfloat16),
        tt_ref[...],
        (((0,), (0,)), ((), ())),
        preferred_element_type=jnp.float32,
    )
    pulled = jnp.concatenate([pulled[:LANES], pulled[LANES:]], axis=1)
    both = jnp.concatenate([halo, halo * parity_sign(halo.shape, 1)], axis=0)
    pulled_h = jnp.dot(
        both.astype(jnp.bfloat16), tt_ref[...], preferred_element_type=jnp.float32
    )
    pulled_h = jnp.concatenate([pulled_h[:8], pulled_h[8:]], axis=1)
    for at in range(0, rows, 8):
        inc_scr[at : at + 8, :] = step * pulled[at : at + 8] + NOISE_AMP * pulled[rows + at : rows + at + 8]
    edge = pulled_h
    edge = step * edge + NOISE_AMP * pltpu.roll(edge, 4, axis=0)
    row8 = lax.broadcasted_iota(jnp.int32, (8, columns), 0)
    inc_scr[rows:, :] = jnp.where(row8 < 2, edge, jnp.where(row8 < 6, 0.0, pltpu.roll(edge, 4, axis=0)))
    depth.wait()

    def rate(depth):
        return RELAX_RATE * depth / (4.0 * depth + STRETCH)

    even, odd = (
        sum(
            unpack_scr[pl.ds(start + piece, bands // 2, stride=2 * block), :] for piece in range(2)
        )
        for start in (modes_here + 2, modes_here + 2 + block)
    )
    half = LANES // 2
    low = lax.broadcasted_iota(jnp.int32, (bands // 2, LANES), 1) < half
    above = rate(jnp.where(low, even, pltpu.roll(odd, half, axis=1)))
    below = rate(jnp.where(low, pltpu.roll(even, half, axis=1), odd))
    for pair in range(bands // 2):
        rate_ref[rows:, pair * LANES : (pair + 1) * LANES] = jnp.where(
            row == 0,
            below[pair : pair + 1],
            jnp.where(row == 7, above[pair : pair + 1], 0.0),
        )
    for at in range(0, rows, 8):
        rate_ref[at : at + 8, :] = rate(depth_ref[at : at + 8, :])
    length = rows + 8

    def relaxed(source_ref, at):
        here = source_ref[at : at + 8, :]
        before = source_ref[(at - 8) % length : (at - 8) % length + 8, :]
        after = source_ref[(at + 8) % length : (at + 8) % length + 8, :]
        around = (
            pltpu.roll(jnp.where(row8 == 7, before, here), 1, axis=0)
            + pltpu.roll(jnp.where(row8 == 0, after, here), 7, axis=0)
            + pltpu.roll(here, 1, axis=1)
            + pltpu.roll(here, columns - 1, axis=1)
        )
        return (1.0 - RELAX_RATE) * here + rate_ref[at : at + 8, :] * (
            around - inc_scr[at : at + 8, :]
        )

    for at in range(0, length, 8):
        one_scr[at : at + 8, :] = relaxed(inc_scr, at)
    for at in range(0, rows, 8):
        field_ref[at : at + 8, :] = relaxed(one_scr, at)
    gather_rows(field_ref, col_scr, seen_scr)
    left_over = miss_ref[0:rows, :] - seen_scr[...]
    part = 0.5 * summed(wgt_scr[...] * left_over * left_over)
    part_ref[...] = jnp.broadcast_to(part[None], part_ref.shape)


SMEM = pl.BlockSpec(memory_space=pltpu.SMEM)
VMEM = pl.BlockSpec(memory_space=pltpu.VMEM)
HBM = pl.BlockSpec(memory_space=pltpu.HBM)


COST = {"observe": 40, "gradient": 40, "spectral": 1, "relax": 1}


def call(kernel, in_specs, out_shape, scratch, name, out_specs=None):
    return pl.pallas_call(
        kernel,
        in_specs=in_specs,
        out_specs=out_specs or jax.tree.map(lambda _: VMEM, out_shape),
        out_shape=out_shape,
        scratch_shapes=scratch,
        name=name,
        cost_estimate=pl.CostEstimate(
            flops=COST[name] * 10**9, transcendentals=0, bytes_accessed=4 * 10**6
        ),
        compiler_params=pltpu.CompilerParams(vmem_limit_bytes=VMEM_LIMIT),
    )


def in_hbm(value):
    return pltpu.with_memory_space_constraint(value, pltpu.HBM)


def swapped(value, axis, bit):
    mask = 2**bit
    pairs = [(source, source ^ mask) for source in range(lax.axis_size(axis))]
    return lax.ppermute(value, axis, pairs)


def per_device(
    stream, depth_field, obs_col, obs_val, obs_weight, log_weight, target, spectrum, noise_coef,
    selection,
):
    _, rows, columns = stream.shape
    per_row = obs_col.shape[1]
    modes_here, n_modes = spectrum.shape
    bands = lax.axis_size("space")
    particles = lax.axis_size("particle")
    y_table = table(rows * bands, n_modes // 2)
    tt_all = jnp.asarray(np.ascontiguousarray(y_table[: columns // 2].T))
    ht_all = jnp.asarray(halo_table(y_table, bands))
    f32, bf16 = jnp.float32, jnp.bfloat16
    shape = jax.ShapeDtypeStruct
    groups = [[g * GROUP + i for i in range(GROUP)] for g in range(particles // GROUP)]
    slot = lax.axis_index("particle")
    place = jnp.stack([slot, lax.axis_index("space")]).astype(jnp.int32)
    info = jnp.concatenate([place, selection.reshape(-1)])
    own = stream[0]
    col_t, val_t, wgt_t = obs_col.T, obs_val.T, obs_weight.T
    vmem = pltpu.VMEM
    tile = vmem((rows, LANES), f32)
    whole = vmem((rows, columns), f32)
    padded = vmem((rows + 8, columns), f32)
    small = (per_row, rows)
    dma = pltpu.SemaphoreType.DMA

    sent, col_tile, wgt_tile, tt, first, last = call(
        observe_kernel,
        [SMEM] + [HBM] * 7,
        (
            shape((GROUP, modes_here * n_modes // LANES + 32, LANES), bf16),
            shape((rows, LANES), jnp.int32),
            shape((rows, LANES), f32),
            shape((n_modes, columns // 2), bf16),
            shape((1, columns), f32),
            shape((1, columns), f32),
        ),
        [vmem(small, jnp.int32), vmem(small, f32), vmem(small, f32),
         vmem((modes_here, n_modes), bf16), whole, vmem((16, columns), f32), tile, tile, dma((8,))],
        "observe",
    )(log_weight, *map(in_hbm, (col_t, val_t, wgt_t, noise_coef[0], own, depth_field, tt_all)))
    sent, held = lax.optimization_barrier((sent, own))
    sent = lax.all_to_all(sent, "particle", 0, 0, axis_index_groups=groups, tiled=True)
    swap = swapped(held, "particle", 0)

    send, miss, part, stay_first, stay_second = call(
        gradient_kernel,
        [SMEM, SMEM] + [VMEM] * 6,
        (
            shape((bands * 10, LANES), bf16),
            shape((rows + 8, LANES), f32),
            shape((8, LANES), f32),
            shape((1, columns), f32),
            shape((1, columns), f32),
        ),
        [whole, vmem((bands * 10, LANES), f32)],
        "gradient",
    )(info, target, col_tile, wgt_tile, sent, tt, first, last)
    send = send.reshape(bands, 5, 2, LANES)
    col_modes = lax.all_to_all(send, "space", 0, 0, tiled=True).reshape(bands * 10, LANES)

    near = jnp.where(stay_first > 0.0, own, swap)
    far = swapped(near, "particle", 1)
    col_modes, near = lax.optimization_barrier((col_modes, near))

    send = call(
        spectral_kernel,
        [SMEM] + [VMEM] * 6,
        shape((bands * (modes_here + 4), LANES), bf16),
        [vmem((bands * (modes_here + 4), LANES), f32), vmem((bands * 10, LANES), f32)],
        "spectral",
    )(info, col_modes, sent, spectrum, part, tt, ht_all)
    send = send.reshape(bands, modes_here // 2 + 2, 2, LANES)
    band_modes = lax.all_to_all(send, "space", 0, 0, tiled=True)
    band_modes = band_modes.reshape(bands * (modes_here + 4), LANES)

    field, part = call(
        relax_kernel,
        [VMEM, VMEM, VMEM, HBM, VMEM, VMEM],
        (shape((rows, columns), f32), shape((bands, 1, LANES), f32)),
        [vmem((bands * (modes_here + 4), LANES), f32), tile, padded, padded, padded, whole, dma(())],
        "relax",
    )(col_tile, wgt_tile, miss, in_hbm(depth_field), band_modes, tt)
    parts = lax.all_to_all(part, "space", 0, 0, tiled=True)
    analysis = field + jnp.where(stay_second > 0.0, near, far)
    parts, analysis = lax.optimization_barrier((parts, analysis))
    misfit_out = jnp.sum(parts[:, 0, 0:1], axis=0)
    return analysis[None], misfit_out


def solution(mesh):
    return jax.shard_map(
        per_device,
        mesh=mesh,
        in_specs=(
            P("particle", "space", None),
            P("space", None),
            P("space", None),
            P("space", None),
            P("space", None),
            P("particle"),
            P(),
            P("space", None),
            P("particle", "space", None),
            P(),
        ),
        out_specs=(P("particle", "space", None), P("particle")),
        check_vma=False,
    )
```

```python
import math

import jax
import jax.numpy as jnp
import ml_dtypes
import numpy as np
from jax import lax
from jax.experimental import pallas as pl
from jax.experimental.pallas import tpu as pltpu
from jax.sharding import PartitionSpec as P

STRETCH = 0.05
RELAX_RATE = 0.8
NOISE_AMP = 0.3
LANES = 128
GROUP = 4
VMEM_LIMIT = 48 * 1024 * 1024


def table(extent, half_modes):
    cell = np.arange(extent, dtype=np.int64)[:, None]
    freq = np.arange(half_modes + 1, dtype=np.int64)[None, :]
    angles = (cell * freq % extent).astype(np.float64) * (2.0 * math.pi / extent)
    return np.concatenate([np.cos(angles), np.sin(angles[:, 1:half_modes])], axis=1).astype(
        ml_dtypes.bfloat16
    )


def halo_table(y_table, bands):
    rows = y_table.shape[0]
    width = rows // bands
    out = np.zeros((4, bands, y_table.shape[1]), dtype=y_table.dtype)
    for band in range(bands):
        for at, row in enumerate((width, width + 1, -2, -1)):
            source = band * width + row
            if 0 <= source < rows:
                out[at, band] = y_table[source]
    return out.reshape(bands * 4, y_table.shape[1])


def lane_iota():
    return lax.broadcasted_iota(jnp.int32, (8, LANES), 1)


def parity_sign(shape, axis):
    place = lax.broadcasted_iota(jnp.int32, shape, axis)
    return (1 - 2 * (place & 1)).astype(jnp.float32)


def summed(values):
    return jnp.sum(jnp.sum(values, axis=0, keepdims=True), axis=1, keepdims=True)


def split2(value):
    high = value.astype(jnp.bfloat16).astype(jnp.float32)
    return high, value - high


def split3(value):
    high = value.astype(jnp.bfloat16).astype(jnp.float32)
    rest = value - high
    mid = rest.astype(jnp.bfloat16).astype(jnp.float32)
    return high, mid, rest - mid


def chosen(info_ref, section, slot):
    per_section = (info_ref.shape[0] - 2) // 2
    return info_ref[2 + section * per_section + slot]


def source_slot(info_ref):
    slot = info_ref[0]
    one = jnp.where(chosen(info_ref, 1, slot) < 1, slot, slot ^ 2)
    return jnp.where(chosen(info_ref, 0, one) < 1, one, one ^ 1)


def fill_tile(source_ref, scr):
    per_row = source_ref.shape[0]
    scr[...] = jnp.zeros(scr.shape, scr.dtype)
    scr[:, 0:per_row] = source_ref[...].T


def gather_rows(field_ref, col_scr, seen_scr):
    rows, columns = field_ref.shape
    for at in range(0, rows, 8):
        cols = col_scr[at : at + 8, :]
        high, low = cols >> 7, cols & 127
        seen = jnp.zeros((8, LANES), jnp.float32)
        for chunk in range(columns // LANES):
            here = field_ref[at : at + 8, chunk * LANES : (chunk + 1) * LANES]
            got = jnp.take_along_axis(here, low, axis=1, mode="promise_in_bounds")
            seen = jnp.where(high == chunk, got, seen)
        seen_scr[at : at + 8, :] = seen


def packed(tile, per_row):
    lane = lane_iota()
    out = tile[0:8, :]
    for group in range(1, tile.shape[0] // 8):
        rolled = pltpu.roll(tile[group * 8 : group * 8 + 8, :], group * per_row, axis=1)
        out = jnp.where(lane // per_row == group, rolled, out)
    return out


def observe_kernel(
    lw_ref, col_hbm, val_hbm, wgt_hbm, noise_hbm, stream_hbm, depth_hbm, tt_hbm,
    out_ref, col_scr, wgt_scr, tt_ref, first_ref, last_ref,
    col_ref, val_ref, wgt_ref, noise_ref, stream_ref, depth_ref, val_scr, seen_scr, sems,
):
    rows = depth_hbm.shape[0]
    pairs = (
        (col_hbm, col_ref),
        (val_hbm, val_ref),
        (wgt_hbm, wgt_ref),
        (noise_hbm, noise_ref),
        (depth_hbm.at[0:8, :], depth_ref.at[0:8, :]),
        (depth_hbm.at[rows - 8 : rows, :], depth_ref.at[8:16, :]),
        (stream_hbm, stream_ref),
        (tt_hbm, tt_ref),
    )
    loads = [pltpu.make_async_copy(a, b, sems.at[at]) for at, (a, b) in enumerate(pairs)]
    for load in loads:
        load.start()
    per_row = col_ref.shape[0]
    modes_here, n_modes = noise_ref.shape
    for at, (source, tile) in enumerate(((col_ref, col_scr), (val_ref, val_scr), (wgt_ref, wgt_scr))):
        loads[at].wait()
        fill_tile(source, tile)
    loads[3].wait()
    noise = noise_ref[...]
    chunks = n_modes // LANES
    for peer in range(GROUP):
        for chunk in range(chunks):
            out_ref[peer, chunk * modes_here : (chunk + 1) * modes_here, :] = noise[
                :, chunk * LANES : (chunk + 1) * LANES
            ]
    loads[4].wait()
    loads[5].wait()
    first_ref[...] = depth_ref[0:1, :]
    last_ref[...] = depth_ref[15:16, :]
    weight = jnp.full((8, LANES), lw_ref[0], jnp.float32)
    row = lax.broadcasted_iota(jnp.int32, (8, LANES), 0)
    high, mid, low = split3(weight)
    weight = jnp.where(row == 0, high, jnp.where(row == 1, mid, jnp.where(row == 2, low, 0.0)))
    loads[6].wait()
    gather_rows(stream_ref, col_scr, seen_scr)
    mismatch = packed(val_scr[...] - seen_scr[...], per_row)
    values = jnp.concatenate(list(split3(mismatch)) + [weight], axis=0).astype(jnp.bfloat16)
    for peer in range(GROUP):
        out_ref[peer, chunks * modes_here :, :] = values
    loads[7].wait()


def gradient_kernel(
    info_ref, target_ref, col_scr, wgt_scr, seen_ref, tt_ref, top_ref, bottom_ref,
    send_ref, miss_ref, part_ref, first_ref, second_ref, grad_scr, pack_scr,
):
    rows = grad_scr.shape[0]
    per_row = LANES * 8 // rows
    columns = 2 * tt_ref.shape[1]
    position = source_slot(info_ref) & (GROUP - 1)
    first = seen_ref.shape[1] - 32
    sent = seen_ref[position][first:, :].astype(jnp.float32)
    mismatch = sent[0:8] + sent[8:16] + sent[16:24]
    weight = sent[24:25] + sent[25:26] + sent[26:27] - target_ref[0]
    slot = info_ref[0]
    for section, stay_ref in enumerate((first_ref, second_ref)):
        stay = jnp.where(chosen(info_ref, section, slot) < 1, 1.0, 0.0)
        stay_ref[...] = jnp.full(stay_ref.shape, stay, jnp.float32)
    miss_ref[rows:, :] = jnp.broadcast_to(weight, (8, LANES))
    tiles = [mismatch] + [
        pltpu.roll(mismatch, LANES - group * per_row, axis=1) for group in range(1, rows // 8)
    ]
    mismatch = jnp.concatenate(tiles, axis=0)
    miss_ref[0:rows, :] = mismatch
    weighted = wgt_scr[...] * mismatch
    part_ref[...] = jnp.broadcast_to(0.5 * summed(weighted * mismatch), (8, LANES))

    def repeated(tile):
        step = per_row
        while step < LANES:
            tile = tile + pltpu.roll(tile, step, axis=1)
            step *= 2
        return tile

    diagonal = lane_iota() // per_row == lax.broadcasted_iota(jnp.int32, (8, LANES), 0)
    row_f = lax.broadcasted_iota(jnp.int32, (LANES, LANES), 0).astype(jnp.float32)
    for group in range(rows // 8):
        at = group * 8
        cols = repeated(col_scr[at : at + 8, :])
        high = jnp.where(diagonal, cols >> 7, -1)
        low = jnp.sum(
            jnp.where(diagonal, (cols & 127).astype(jnp.float32), 0.0), axis=0, keepdims=True
        )
        one_hot = jnp.where(row_f == low, 1.0, 0.0).astype(jnp.bfloat16)
        left = []
        for piece in split3(repeated(weighted[at : at + 8, :])):
            left.append(
                jnp.concatenate(
                    [jnp.where(high == chunk, piece, 0.0) for chunk in range(columns // LANES)], axis=0
                ).astype(jnp.bfloat16)
            )
        spread = lax.dot_general(
            jnp.concatenate(left, axis=1),
            jnp.concatenate([one_hot] * 3, axis=1),
            (((1,), (1,)), ((), ())),
            preferred_element_type=jnp.float32,
        )
        for chunk in range(columns // LANES):
            grad_scr[at : at + 8, chunk * LANES : (chunk + 1) * LANES] = spread[
                chunk * 8 : chunk * 8 + 8, :
            ]
    gradient = grad_scr[...].astype(jnp.bfloat16)
    gradient = jnp.concatenate([gradient[:, : columns // 2], gradient[:, columns // 2 :]], axis=0)
    modes = lax.dot_general(
        tt_ref[...], gradient, (((1,), (1,)), ((), ())), preferred_element_type=jnp.float32
    )
    half = LANES // 2
    bands = modes.shape[0] // 16
    block = send_ref.shape[0] // bands
    modes = modes + parity_sign(modes.shape, 0) * pltpu.roll(modes, half, axis=1)
    split = modes.reshape(bands, 2, 8, LANES)
    small = (bands, 8, LANES)
    values = jnp.where(
        lax.broadcasted_iota(jnp.int32, small, 2) < half,
        split[:, 0],
        parity_sign(small, 1) * split[:, 1],
    )
    pairs = columns // LANES
    top, bottom = (
        jnp.concatenate(
            [ref[:, pair * LANES : (pair + 1) * LANES] for pair in range(pairs)], axis=0
        )
        for ref in (top_ref, bottom_ref)
    )
    low = lax.broadcasted_iota(jnp.int32, (pairs, LANES), 1) < half
    even = split2(jnp.where(low, top, pltpu.roll(bottom, half, axis=1)))
    odd = split2(jnp.where(low, pltpu.roll(top, half, axis=1), bottom))
    for band in range(bands):
        at = band * block
        pack_scr[at : at + 8, :] = values[band]
        for piece in range(2):
            row = (odd if band % 2 else even)[piece][band // 2 : band // 2 + 1]
            pack_scr[at + 8 + piece : at + 9 + piece, :] = row
    send_ref[...] = pack_scr[...].astype(jnp.bfloat16)


def spectral_kernel(
    info_ref, modes_ref, noise_ref, spec_ref, part_ref, tt_ref, ht_ref, send_ref, pack_scr,
    unpack_scr,
):
    half = LANES // 2
    modes_here, n_modes = spec_ref.shape
    bands = n_modes // modes_here
    unpack_scr[...] = modes_ref[...].astype(jnp.float32)
    rows = 2 * tt_ref.shape[1]
    norm_factor = 4.0 / (rows * rows)
    position = source_slot(info_ref) & (GROUP - 1)
    lane = lane_iota()
    low = lane < half
    tops, bottoms = [], []
    for pair in range(bands // 2):
        even = unpack_scr[20 * pair : 20 * pair + 8, :]
        odd = unpack_scr[20 * pair + 10 : 20 * pair + 18, :]
        tops.append(jnp.where(low, even, pltpu.roll(odd, half, axis=1)))
        bottoms.append(jnp.where(low, pltpu.roll(even, half, axis=1), odd))
    folded = bands // 4
    columns = jnp.concatenate(
        [
            jnp.concatenate(part, axis=1)
            for part in (tops[:folded], bottoms[:folded], tops[folded:], bottoms[folded:])
        ],
        axis=0,
    ).astype(jnp.bfloat16)
    sums = lax.dot_general(
        columns, tt_ref[...], (((1,), (1,)), ((), ())), preferred_element_type=jnp.float32
    )
    coefficients = sums[:modes_here] + parity_sign(spec_ref.shape, 1) * sums[modes_here:]
    scaled = norm_factor * spec_ref[...]
    weighted = coefficients * scaled
    energy = summed(coefficients * weighted)
    noise = noise_ref[position][0 : noise_ref.shape[1] - 32, :]
    noise = jnp.concatenate(
        [noise[at : at + modes_here] for at in range(0, noise.shape[0], modes_here)], axis=1
    )
    shaped = (jnp.sqrt(scaled) * noise.astype(jnp.float32)).astype(jnp.bfloat16)
    weighted = weighted.astype(jnp.bfloat16)
    stacked = jnp.concatenate([weighted, shaped], axis=0)
    flipped = stacked.astype(jnp.float32) * parity_sign(stacked.shape, 1)
    both = jnp.concatenate([stacked, flipped.astype(jnp.bfloat16)], axis=0)
    inverted = jnp.dot(both, tt_ref[...], preferred_element_type=jnp.float32)
    inverted = jnp.concatenate(
        [inverted[: 2 * modes_here], inverted[2 * modes_here :]], axis=1
    )
    depth = sum(unpack_scr[pl.ds(8 + piece, bands, stride=10), :] for piece in range(2))
    band_row = lax.broadcasted_iota(jnp.int32, (bands, LANES), 0)
    band_low = lax.broadcasted_iota(jnp.int32, (bands, LANES), 1) < half
    above = jnp.where(band_row > 0, pltpu.roll(depth, 1, axis=0), 0.0)
    below = jnp.where(band_row < bands - 1, pltpu.roll(depth, bands - 1, axis=0), 0.0)
    beside = split2(pltpu.roll(jnp.where(band_low, below, above), half, axis=1))
    block = modes_here + 4
    low16 = lax.broadcasted_iota(jnp.int32, (modes_here, LANES), 1) < half
    for pair in range(bands // 2):
        first = inverted[0:modes_here, pair * LANES : (pair + 1) * LANES]
        second = inverted[modes_here:, pair * LANES : (pair + 1) * LANES]
        at = 2 * pair * block
        pack_scr[at : at + modes_here, :] = jnp.where(
            low16, first, pltpu.roll(second, half, axis=1)
        )
        at += block
        pack_scr[at : at + modes_here, :] = jnp.where(
            low16, pltpu.roll(first, half, axis=1), second
        )
    halo = lax.dot_general(
        ht_ref[...], stacked, (((1,), (1,)), ((), ())), preferred_element_type=jnp.float32
    )
    halo = jnp.concatenate(
        [halo, jnp.zeros((4 * bands, LANES - 2 * modes_here), jnp.float32)], axis=1
    )
    window = lax.broadcasted_iota(jnp.int32, (bands, LANES), 1) // modes_here
    edges = jnp.zeros((bands, LANES), jnp.float32)
    for at in range(8):
        field, row = at // 4, at % 4
        shift = (at - field) * modes_here % LANES
        value = halo[row * bands : (row + 1) * bands]
        edges = jnp.where(window == at, pltpu.roll(value, shift, axis=1) if shift else value, edges)
    lane1 = lax.broadcasted_iota(jnp.int32, (1, LANES), 1)
    pieces = jnp.zeros((1, LANES), jnp.float32)
    for at, piece in enumerate(split3(part_ref[0:1, 0:1]) + split3(energy)):
        pieces = jnp.where(lane1 == at, piece, pieces)
    for band in range(bands):
        at = band * block + modes_here
        pack_scr[at : at + 1, :] = edges[band : band + 1]
        pack_scr[at + 1 : at + 2, :] = pieces
        for piece in range(2):
            pack_scr[at + 2 + piece : at + 3 + piece, :] = beside[piece][band : band + 1]
    send_ref[...] = pack_scr[...].astype(jnp.bfloat16)


def relax_kernel(
    col_scr, wgt_scr, miss_ref, depth_hbm, modes_ref, tt_ref,
    field_ref, part_ref, unpack_scr, seen_scr, inc_scr, one_scr, rate_ref, depth_ref,
    sem,
):
    depth = pltpu.make_async_copy(depth_hbm, depth_ref, sem)
    depth.start()
    rows = depth_ref.shape[0]

    def rate(depth):
        return RELAX_RATE * depth / (4.0 * depth + STRETCH)

    n_modes, columns = tt_ref.shape[0], 2 * tt_ref.shape[1]
    bands = part_ref.shape[0]
    modes_here = n_modes // bands
    lane = lane_iota()
    block = modes_here + 4
    unpack_scr[...] = modes_ref[...].astype(jnp.float32)
    edges = unpack_scr[pl.ds(modes_here, bands, stride=block), :]
    scalars = unpack_scr[pl.ds(modes_here + 1, bands, stride=block), :]
    row = lax.broadcasted_iota(jnp.int32, (8, LANES), 0)
    window = lane // modes_here
    quads = []
    for quad in range(0, bands, 8):
        tile = edges[quad : quad + 8]
        for bit in (1, 2, 4):
            up = pltpu.roll(pltpu.roll(tile, 8 - bit, axis=0), bit * modes_here, axis=1)
            down = pltpu.roll(pltpu.roll(tile, bit, axis=0), LANES - bit * modes_here, axis=1)
            upper, later = (row & bit) == 0, (window & bit) == 0
            tile = jnp.where(upper == later, tile, jnp.where(upper, up, down))
        quads.append(tile)
    halo = jnp.concatenate(quads, axis=1)
    lanes = lax.broadcasted_iota(jnp.int32, scalars.shape, 1)
    misfit = summed(jnp.where(lanes < 3, scalars, 0.0))
    energy = summed(jnp.where((lanes >= 3) & (lanes < 6), scalars, 0.0))
    weight = miss_ref[rows : rows + 1, 0:1]
    step = (misfit + weight) / (energy + 1.0)
    main = jnp.concatenate(
        [unpack_scr[at * block : at * block + modes_here, :] for at in range(bands)], axis=0
    )
    both = jnp.concatenate([main, main * parity_sign(main.shape, 0)], axis=1)
    pulled = lax.dot_general(
        both.astype(jnp.bfloat16),
        tt_ref[...],
        (((0,), (0,)), ((), ())),
        preferred_element_type=jnp.float32,
    )
    pulled = jnp.concatenate([pulled[:LANES], pulled[LANES:]], axis=1)
    both = jnp.concatenate([halo, halo * parity_sign(halo.shape, 1)], axis=0)
    pulled_h = jnp.dot(
        both.astype(jnp.bfloat16), tt_ref[...], preferred_element_type=jnp.float32
    )
    pulled_h = jnp.concatenate([pulled_h[:8], pulled_h[8:]], axis=1)
    for at in range(0, rows, 8):
        inc_scr[at : at + 8, :] = step * pulled[at : at + 8] + NOISE_AMP * pulled[rows + at : rows + at + 8]
    edge = pulled_h
    edge = step * edge + NOISE_AMP * pltpu.roll(edge, 4, axis=0)
    row8 = lax.broadcasted_iota(jnp.int32, (8, columns), 0)
    inc_scr[rows:, :] = jnp.where(row8 < 2, edge, jnp.where(row8 < 6, 0.0, pltpu.roll(edge, 4, axis=0)))
    depth.wait()

    def rate(depth):
        return RELAX_RATE * depth / (4.0 * depth + STRETCH)

    even, odd = (
        sum(
            unpack_scr[pl.ds(start + piece, bands // 2, stride=2 * block), :] for piece in range(2)
        )
        for start in (modes_here + 2, modes_here + 2 + block)
    )
    half = LANES // 2
    low = lax.broadcasted_iota(jnp.int32, (bands // 2, LANES), 1) < half
    above = rate(jnp.where(low, even, pltpu.roll(odd, half, axis=1)))
    below = rate(jnp.where(low, pltpu.roll(even, half, axis=1), odd))
    for pair in range(bands // 2):
        rate_ref[rows:, pair * LANES : (pair + 1) * LANES] = jnp.where(
            row == 0,
            below[pair : pair + 1],
            jnp.where(row == 7, above[pair : pair + 1], 0.0),
        )
    for at in range(0, rows, 8):
        rate_ref[at : at + 8, :] = rate(depth_ref[at : at + 8, :])
    length = rows + 8

    def relaxed(source_ref, at):
        here = source_ref[at : at + 8, :]
        before = source_ref[(at - 8) % length : (at - 8) % length + 8, :]
        after = source_ref[(at + 8) % length : (at + 8) % length + 8, :]
        around = (
            pltpu.roll(jnp.where(row8 == 7, before, here), 1, axis=0)
            + pltpu.roll(jnp.where(row8 == 0, after, here), 7, axis=0)
            + pltpu.roll(here, 1, axis=1)
            + pltpu.roll(here, columns - 1, axis=1)
        )
        return (1.0 - RELAX_RATE) * here + rate_ref[at : at + 8, :] * (
            around - inc_scr[at : at + 8, :]
        )

    for at in range(0, length, 8):
        one_scr[at : at + 8, :] = relaxed(inc_scr, at)
    for at in range(0, rows, 8):
        field_ref[at : at + 8, :] = relaxed(one_scr, at)
    gather_rows(field_ref, col_scr, seen_scr)
    left_over = miss_ref[0:rows, :] - seen_scr[...]
    part = 0.5 * summed(wgt_scr[...] * left_over * left_over)
    part_ref[...] = jnp.broadcast_to(part[None], part_ref.shape)


SMEM = pl.BlockSpec(memory_space=pltpu.SMEM)
VMEM = pl.BlockSpec(memory_space=pltpu.VMEM)
HBM = pl.BlockSpec(memory_space=pltpu.HBM)


COST = {"observe": 40, "gradient": 40, "spectral": 1, "relax": 1}


def call(kernel, in_specs, out_shape, scratch, name, out_specs=None):
    return pl.pallas_call(
        kernel,
        in_specs=in_specs,
        out_specs=out_specs or jax.tree.map(lambda _: VMEM, out_shape),
        out_shape=out_shape,
        scratch_shapes=scratch,
        name=name,
        cost_estimate=pl.CostEstimate(
            flops=COST[name] * 10**9, transcendentals=0, bytes_accessed=4 * 10**6
        ),
        compiler_params=pltpu.CompilerParams(vmem_limit_bytes=VMEM_LIMIT),
    )


def in_hbm(value):
    return pltpu.with_memory_space_constraint(value, pltpu.HBM)


def swapped(value, axis, bit):
    mask = 2**bit
    pairs = [(source, source ^ mask) for source in range(lax.axis_size(axis))]
    return lax.ppermute(value, axis, pairs)


def per_device(
    stream, depth_field, obs_col, obs_val, obs_weight, log_weight, target, spectrum, noise_coef,
    selection,
):
    _, rows, columns = stream.shape
    per_row = obs_col.shape[1]
    modes_here, n_modes = spectrum.shape
    bands = lax.axis_size("space")
    particles = lax.axis_size("particle")
    y_table = table(rows * bands, n_modes // 2)
    tt_all = jnp.asarray(np.ascontiguousarray(y_table[: columns // 2].T))
    ht_all = jnp.asarray(halo_table(y_table, bands))
    f32, bf16 = jnp.float32, jnp.bfloat16
    shape = jax.ShapeDtypeStruct
    groups = [[g * GROUP + i for i in range(GROUP)] for g in range(particles // GROUP)]
    slot = lax.axis_index("particle")
    place = jnp.stack([slot, lax.axis_index("space")]).astype(jnp.int32)
    info = jnp.concatenate([place, selection.reshape(-1)])
    own = stream[0]
    col_t, val_t, wgt_t = obs_col.T, obs_val.T, obs_weight.T
    vmem = pltpu.VMEM
    tile = vmem((rows, LANES), f32)
    whole = vmem((rows, columns), f32)
    padded = vmem((rows + 8, columns), f32)
    small = (per_row, rows)
    dma = pltpu.SemaphoreType.DMA

    sent, col_tile, wgt_tile, tt, first, last = call(
        observe_kernel,
        [SMEM] + [HBM] * 7,
        (
            shape((GROUP, modes_here * n_modes // LANES + 32, LANES), bf16),
            shape((rows, LANES), jnp.int32),
            shape((rows, LANES), f32),
            shape((n_modes, columns // 2), bf16),
            shape((1, columns), f32),
            shape((1, columns), f32),
        ),
        [vmem(small, jnp.int32), vmem(small, f32), vmem(small, f32),
         vmem((modes_here, n_modes), bf16), whole, vmem((16, columns), f32), tile, tile, dma((8,))],
        "observe",
    )(log_weight, *map(in_hbm, (col_t, val_t, wgt_t, noise_coef[0], own, depth_field, tt_all)))
    sent, held = lax.optimization_barrier((sent, own))
    sent = lax.all_to_all(sent, "particle", 0, 0, axis_index_groups=groups, tiled=True)
    swap = swapped(held, "particle", 0)

    send, miss, part, stay_first, stay_second = call(
        gradient_kernel,
        [SMEM, SMEM] + [VMEM] * 6,
        (
            shape((bands * 10, LANES), bf16),
            shape((rows + 8, LANES), f32),
            shape((8, LANES), f32),
            shape((1, columns), f32),
            shape((1, columns), f32),
        ),
        [whole, vmem((bands * 10, LANES), f32)],
        "gradient",
    )(info, target, col_tile, wgt_tile, sent, tt, first, last)
    send = send.reshape(bands, 5, 2, LANES)
    col_modes = lax.all_to_all(send, "space", 0, 0, tiled=True).reshape(bands * 10, LANES)

    near = jnp.where(stay_first > 0.0, own, swap)
    far = swapped(near, "particle", 1)
    col_modes, near = lax.optimization_barrier((col_modes, near))

    send = call(
        spectral_kernel,
        [SMEM] + [VMEM] * 6,
        shape((bands * (modes_here + 4), LANES), bf16),
        [vmem((bands * (modes_here + 4), LANES), f32), vmem((bands * 10, LANES), f32)],
        "spectral",
    )(info, col_modes, sent, spectrum, part, tt, ht_all)
    send = send.reshape(bands, modes_here // 2 + 2, 2, LANES)
    band_modes = lax.all_to_all(send, "space", 0, 0, tiled=True)
    band_modes = band_modes.reshape(bands * (modes_here + 4), LANES)

    field, part = call(
        relax_kernel,
        [VMEM, VMEM, VMEM, HBM, VMEM, VMEM],
        (shape((rows, columns), f32), shape((bands, 1, LANES), f32)),
        [vmem((bands * (modes_here + 4), LANES), f32), tile, padded, padded, padded, whole, dma(())],
        "relax",
    )(col_tile, wgt_tile, miss, in_hbm(depth_field), band_modes, tt)
    parts = lax.all_to_all(part, "space", 0, 0, tiled=True)
    analysis = field + jnp.where(stay_second > 0.0, near, far)
    parts, analysis = lax.optimization_barrier((parts, analysis))
    misfit_out = jnp.sum(parts[:, 0, 0:1], axis=0)
    return analysis[None], misfit_out


def solution(mesh):
    return jax.shard_map(
        per_device,
        mesh=mesh,
        in_specs=(
            P("particle", "space", None),
            P("space", None),
            P("space", None),
            P("space", None),
            P("space", None),
            P("particle"),
            P(),
            P("space", None),
            P("particle", "space", None),
            P(),
        ),
        out_specs=(P("particle", "space", None), P("particle")),
        check_vma=False,
    )
```
